32 devices in a mesh: fn: 2 (over y), pts: 16 (over z, x, core).
Axes of the slice: x: 2, y: 2, z: 4, core: 2. Of those that a mesh axis runs over, the one named last changes fastest.
Arguments:
- points_in: bfloat16 [16, 4096, 128], P('pts', 'fn'), may hold values from -6 to 6
- geometry: bfloat16 [16, 4096, 128], P('pts', 'fn'), may hold values from -6 to 6
- functions: bfloat16 [2, 16, 2048, 128], P('fn', 'pts'), may hold values from -6 to 6
- presence: int32 [2, 16], P('fn', 'pts'), may hold values from 0 to 1, as said below
- fn_counts: int32 [2, 16], P('fn', 'pts'), may hold values from 512 to 2048
- item_counts: int32 [16], P('pts'), may hold values from 2048 to 4096, as said below
- cotangent: bfloat16 [16, 4096, 128], P('pts', 'fn'), may hold values from -6 to 6
- shared_weights: float32 [361728], replicated, may hold values from -4.4748737 to 4.4748737
- shared_momentum: float32 [361728], replicated, may hold values from -12288 to 12288
- shared_average: float32 [361728], replicated, may hold values from -4.4748737 to 4.4748737
- branch_weights: float32 [2, 33024], P('fn'), may hold values from -2 to 2
- branch_momentum: float32 [2, 33024], P('fn'), may hold values from -4344.464 to 4344.464
- branch_average: float32 [2, 33024], P('fn'), may hold values from -2 to 2
Outputs:
- output: bfloat16 [16, 4096, 128], P('pts', 'fn')
- input_grad: bfloat16 [16, 4096, 128], P('pts', 'fn')
- shared_weights_new: float32 [361728], replicated
- shared_momentum_new: float32 [361728], replicated
- shared_average_new: float32 [361728], replicated
- shared_copy: bfloat16 [361728], replicated
- branch_weights_new: float32 [2, 33024], P('fn')
- branch_momentum_new: float32 [2, 33024], P('fn')
- branch_average_new: float32 [2, 33024], P('fn')
- branch_copy: bfloat16 [2, 33024], P('fn')
- norm_grads: float32 [6, 128], replicated
The draws below stay inside these ranges and needn't reach their ends.
Inputs may be any that keep to these rules, and one draw needn't show every extreme that they name: `presence`: each item has at least one present function, and one present function of each item uses all 2048 slots. `item_counts`: some item uses all 4096 slots.
All inputs are finite; a program needn't handle non-finite values.
Results may differ from the reference program's by a relative error of at most 0.012.
Values may be sent and summed in bfloat16 or wider, within the bound.
A program may use at most 128 MiB of HBM per device.

```python
import math
import jax
import jax.numpy as jnp
from jax import lax

D = 128
HEADS = 8
FF = 256
EXPERTS = 4
QP_DEV = 2048
IN_PTS = 2048
HEAD_DIM = 16
F = 2
PTS = 4096
ITEMS = 16
N_FN = 2


def drawn_segments(key, leading, segments):
    columns = []
    for number, segment in enumerate(segments):
        samples = jax.random.normal(jax.random.fold_in(key, number), leading + (segment[0],), jnp.float32)
        columns.append(segment[1] + segment[2] * jnp.clip(samples, -4.0, 4.0))
    return jnp.concatenate(columns, axis=-1)


def shared_weight_segments():
    matrix_scale = 1.2 / math.sqrt(D)
    branch_out = 7.0 / math.sqrt(D)
    return [(D, 1.0, 0.1), (D, 0.0, 0.1), (D * D, 0.0, matrix_scale), (D * D, 0.0, branch_out), (D, 1.0, 0.1), (D, 0.0, 0.1), (3 * D * D, 0.0, matrix_scale), (D * D, 0.0, branch_out), (D, 1.0, 0.1), (D, 0.0, 0.1), (D * EXPERTS, 0.0, 0.5 / math.sqrt(D)), (EXPERTS * D * FF, 0.0, 1.0 / math.sqrt(D)), (EXPERTS * FF * D, 0.0, 4.2 / math.sqrt(FF))]


def shared_momentum_segments():
    factor = math.sqrt(ITEMS * PTS)
    return [(D, 0.0, 0.3 * factor), (D, 0.0, 0.3 * factor), (D * D, 0.0, 0.2 * factor), (D * D, 0.0, 0.4 * factor), (D, 0.0, 2.0 * factor), (D, 0.0, 8.0 * factor), (3 * D * D, 0.0, 0.5 * factor), (D * D, 0.0, 0.4 * factor), (D, 0.0, 2.5 * factor), (D, 0.0, 2.5 * factor), (D * EXPERTS, 0.0, 12.0 * factor), (EXPERTS * D * FF, 0.0, 0.9 * factor), (EXPERTS * FF * D, 0.0, 0.3 * factor)]


def branch_weight_segments():
    return [(D, 1.0, 0.1), (D, 0.0, 0.1), (2 * D * D, 0.0, 1.2 / math.sqrt(D))]


def branch_momentum_segments():
    factor = math.sqrt(ITEMS * IN_PTS)
    return [(D, 0.0, factor), (D, 0.0, 6.0 * factor), (2 * D * D, 0.0, 0.6 * factor)]


def draw_shared_weights(key, part):
    return drawn_segments(jax.random.fold_in(key, 1), (), shared_weight_segments())


def draw_shared_average(key, part):
    return drawn_segments(jax.random.fold_in(key, 2), (), shared_weight_segments())


def draw_shared_momentum(key, part):
    return drawn_segments(jax.random.fold_in(key, 3), (), shared_momentum_segments())


def draw_branch_weights(key, part):
    return drawn_segments(jax.random.fold_in(key, 4), (F,), branch_weight_segments())


def draw_branch_average(key, part):
    return drawn_segments(jax.random.fold_in(key, 5), (F,), branch_weight_segments())


def draw_branch_momentum(key, part):
    return drawn_segments(jax.random.fold_in(key, 6), (F,), branch_momentum_segments())


def function_table(key):
    full_fn = jax.random.randint(jax.random.fold_in(key, 11), (ITEMS,), 0, F)
    chosen = jnp.arange(F)[:, None] == full_fn[None, :]
    counts = jax.random.randint(jax.random.fold_in(key, 12), (F, ITEMS), IN_PTS // 4, IN_PTS + 1)
    counts = jnp.where(chosen, IN_PTS, counts)
    present = jax.random.randint(jax.random.fold_in(key, 13), (F, ITEMS), 0, 2)
    present = jnp.where(chosen, 1, present)
    return (counts.astype(jnp.int32), present.astype(jnp.int32))


def draw_fn_counts(key, part):
    return function_table(key)[0]


def draw_presence(key, part):
    return function_table(key)[1]


def draw_item_counts(key, part):
    counts = jax.random.randint(jax.random.fold_in(key, 21), (ITEMS,), PTS // 2, PTS + 1)
    full_item = jax.random.randint(jax.random.fold_in(key, 22), (), 0, ITEMS)
    counts = jnp.where(jnp.arange(ITEMS) == full_item, PTS, counts)
    return counts.astype(jnp.int32)


def levels(rng, extent, shards, least, largest):
    factor_of, own = 1.0, jax.random.fold_in(rng, 6)
    for axis_at, shards_of in shards:
        steps = jnp.exp(jax.random.uniform(jax.random.fold_in(own, axis_at), (shards_of,), jnp.float32, least / len(shards), largest / len(shards)))
        factor_of = factor_of * jnp.repeat(steps, extent[axis_at] // shards_of).reshape([-1 if axis == axis_at else 1 for axis in range(len(extent))])
    return factor_of


def scatter_about(stream_key, shape, scale, most, split=(), kind=jnp.bfloat16):
    result = scale * jax.random.normal(stream_key, shape, jnp.float32)
    if split:
        result = result * levels(stream_key, shape, split, -0.22, 0.18)
    return jnp.clip(result, -most, most).astype(kind)


def setup_inputs(seed: int = 0) -> dict:
    streams_of = jax.random.split(jax.random.key(seed), 14)
    return {
        "points_in": scatter_about(streams_of[0], (ITEMS, PTS, D), 1.0, 6.0, ((0, 16), (1, 2))),
        "geometry": scatter_about(streams_of[1], (ITEMS, PTS, D), 1.0, 6.0, ((0, 16), (1, 2))),
        "functions": scatter_about(streams_of[2], (F, ITEMS, IN_PTS, D), 1.0, 6.0, ((0, 2), (1, 16))),
        "presence": draw_presence(jax.random.fold_in(streams_of[13], 71), 0),
        "fn_counts": draw_fn_counts(jax.random.fold_in(streams_of[13], 71), 0),
        "item_counts": draw_item_counts(jax.random.fold_in(streams_of[13], 71), 0),
        "cotangent": scatter_about(streams_of[6], (ITEMS, PTS, D), 1.0, 6.0, ((0, 16), (1, 2))),
        "shared_weights": draw_shared_weights(jax.random.fold_in(streams_of[13], 71), 0),
        "shared_momentum": draw_shared_momentum(jax.random.fold_in(streams_of[13], 71), 0),
        "shared_average": draw_shared_average(jax.random.fold_in(streams_of[13], 71), 0),
        "branch_weights": draw_branch_weights(jax.random.fold_in(streams_of[13], 71), 0),
        "branch_momentum": draw_branch_momentum(jax.random.fold_in(streams_of[13], 71), 0),
        "branch_average": draw_branch_average(jax.random.fold_in(streams_of[13], 71), 0),
    }


@jax.custom_vjp
def low(v):
    return lax.optimization_barrier(v.astype(jnp.bfloat16)).astype(jnp.float32)

@jax.custom_vjp
def low_back(v):
    return v

def low_keep(v):
    return (low(v), None)

def low_pass(kept, grad):
    return (grad,)

def back_keep(v):
    return (v, None)

def back_low(kept, grad):
    return (low(grad),)
low.defvjp(low_keep, low_pass)
low_back.defvjp(back_keep, back_low)
epsilon = 1e-05
highest = lax.Precision.HIGHEST
far_below = -1e+30
momentum_decay = 0.9
average_decay = 0.95

def split_shared(flat):
    shapes = [(D,), (D,), (D, D), (D, D), (D,), (D,), (D, 3 * D), (D, D), (D,), (D,), (D, EXPERTS), (EXPERTS, D, FF), (EXPERTS, FF, D)]
    pieces = []
    offset = 0
    for segment_shape in shapes:
        segment_size = math.prod(segment_shape)
        pieces.append(flat[offset:offset + segment_size].reshape(segment_shape))
        offset = offset + segment_size
    return tuple(pieces)

def layer_norm(values, norm_gain, norm_bias):
    centred = values - lax.optimization_barrier(jnp.mean(values, axis=-1, keepdims=True))
    spread = lax.optimization_barrier(jnp.mean(centred * centred, axis=-1, keepdims=True))
    return centred * lax.rsqrt(spread + epsilon) * norm_gain + norm_bias

def heads_view(values):
    return values.reshape(values.shape[:-1] + (HEADS, HEAD_DIM))

def feature_softmax(values):
    shaped = heads_view(values)
    powers = jnp.exp(shaped - lax.optimization_barrier(jnp.max(shaped, axis=-1, keepdims=True)))
    return (powers / lax.optimization_barrier(jnp.sum(powers, axis=-1, keepdims=True))).reshape(values.shape)

def masked_softmax(values, usable):
    masked = jnp.where(usable[..., None], values, far_below)
    column_max = lax.optimization_barrier(jnp.max(masked, axis=-2, keepdims=True))
    powers = jnp.where(usable[..., None], jnp.exp(masked - column_max), 0.0)
    return powers / lax.optimization_barrier(jnp.sum(powers, axis=-2, keepdims=True))

def summarize(weights, values):
    return jnp.einsum('...nhj,...nhe->...hje', heads_view(weights), heads_view(values), precision=highest)

def apply_summary(weights, summary):
    mixed_rows = jnp.einsum('...nhj,...hje->...nhe', heads_view(weights), summary, precision=highest)
    return mixed_rows.reshape(weights.shape)

def grouped_heads(values):
    return values.reshape(ITEMS, N_FN, QP_DEV, HEADS, HEAD_DIM)

def sgd_update(weights, momentum, average, gradient, step_rate):
    momentum_new = momentum_decay * momentum + gradient
    weights_new = weights - step_rate * (gradient + momentum_decay * momentum_new)
    average_new = average_decay * average + (1.0 - average_decay) * weights_new
    return (weights_new, momentum_new, average_new, weights_new.astype(jnp.bfloat16))

def reference(points_in, geometry, functions, presence, fn_counts, item_counts, cotangent, shared_weights, shared_momentum, shared_average, branch_weights, branch_momentum, branch_average):
    geo_float = geometry.astype(jnp.float32)
    fn_data = functions.astype(jnp.float32)
    fn_usable = lax.broadcasted_iota(jnp.int32, (F, ITEMS, IN_PTS), 2) < fn_counts[:, :, None]
    item_usable = lax.broadcasted_iota(jnp.int32, (ITEMS, PTS), 1) < item_counts[:, None]
    weighted = (presence * fn_counts).astype(jnp.float32)
    weight_total = lax.optimization_barrier(jnp.sum(weighted, axis=0))

    def forward(shared, branch, inputs):
        gain_one, bias_one, cross_query, cross_output, gain_two, bias_two, self_qkv, self_output, gain_three, bias_three, router, expert_up, expert_down = split_shared(shared)
        branch_gain = branch[:, :D]
        branch_bias = branch[:, D:2 * D]
        branch_kv = branch[:, 2 * D:].reshape(branch.shape[0], D, 2 * D)
        fn_hidden = low(layer_norm(fn_data, branch_gain[:, None, None, :], branch_bias[:, None, None, :]))
        fn_keyval = low_back(jnp.einsum('fipd,fde->fipe', fn_hidden, low(branch_kv), precision=highest))
        fn_probs = masked_softmax(fn_keyval[..., :D], fn_usable)
        fn_summary = low_back(summarize(low(fn_probs), low(fn_keyval[..., D:])))
        mixed_total = lax.optimization_barrier(jnp.sum(weighted[:, :, None, None, None] * fn_summary, axis=0))
        mixed_summary = low(mixed_total / weight_total[:, None, None, None])
        norm_first = low(layer_norm(inputs, gain_one, bias_one))
        cross_q = low_back(jnp.einsum('ind,de->ine', norm_first, low(cross_query), precision=highest))
        cross_out = low(low_back(apply_summary(low(feature_softmax(cross_q)), mixed_summary)))
        after_cross = inputs + low_back(jnp.einsum('ind,de->ine', cross_out, low(cross_output), precision=highest))
        norm_second = low(layer_norm(after_cross, gain_two, bias_two))
        self_qkv_out = low_back(jnp.einsum('ind,de->ine', norm_second, low(self_qkv), precision=highest))
        key_probs = masked_softmax(self_qkv_out[..., D:2 * D], item_usable)
        key_group = grouped_heads(low(key_probs))
        value_group = grouped_heads(low(self_qkv_out[..., 2 * D:]))
        group_terms = jnp.einsum('ignhj,ignhe->ighje', key_group, value_group, precision=highest)
        self_summary = low(low_back(lax.optimization_barrier(jnp.sum(low(group_terms), axis=1))))
        query_group = grouped_heads(low(feature_softmax(self_qkv_out[..., :D])))
        summary_copies = low_back(jnp.broadcast_to(self_summary[:, None], (ITEMS, N_FN, HEADS, HEAD_DIM, HEAD_DIM)))
        self_rows = jnp.einsum('ignhj,ighje->ignhe', query_group, summary_copies, precision=highest).reshape(ITEMS, PTS, D)
        self_out = low(low_back(self_rows))
        after_self = after_cross + low_back(jnp.einsum('ind,de->ine', self_out, low(self_output), precision=highest))
        norm_third = low(layer_norm(after_self, gain_three, bias_three))
        logits = low_back(jnp.einsum('ind,de->ine', geo_float, low(router), precision=highest))
        powers = jnp.exp(logits - lax.optimization_barrier(jnp.max(logits, axis=-1, keepdims=True)))
        gate_probs = powers / lax.optimization_barrier(jnp.sum(powers, axis=-1, keepdims=True))
        expert_pre = low_back(jnp.einsum('ind,edf->inef', norm_third, low(expert_up), precision=highest))
        expert_hidden = low(jax.nn.gelu(expert_pre, approximate=False))
        expert_result = low_back(jnp.einsum('inef,efd->ined', expert_hidden, low(expert_down), precision=highest))
        return after_self + lax.optimization_barrier(jnp.sum(gate_probs[..., None] * expert_result, axis=2))
    outputs, pullback = jax.vjp(forward, shared_weights, branch_weights, points_in.astype(jnp.float32))
    shared_grad, branch_grad, input_grad = pullback(cotangent.astype(jnp.float32))
    grad_pieces = split_shared(shared_grad)
    norm_grads = jnp.stack([grad_pieces[0], grad_pieces[1], grad_pieces[4], grad_pieces[5], grad_pieces[8], grad_pieces[9]])
    shared_new = sgd_update(shared_weights, shared_momentum, shared_average, shared_grad, 0.1 / math.sqrt(ITEMS * PTS))
    branch_new = sgd_update(branch_weights, branch_momentum, branch_average, branch_grad, 0.1 / math.sqrt(ITEMS * IN_PTS))
    return (outputs.astype(jnp.bfloat16), input_grad.astype(jnp.bfloat16), shared_new[0], shared_new[1], shared_new[2], shared_new[3], branch_new[0], branch_new[1], branch_new[2], branch_new[3], norm_grads)
```

```python
import functools
import math

import jax
import jax.numpy as jnp
from jax import lax
from jax.experimental import pallas as pl
from jax.experimental.pallas import tpu as pltpu
from jax.sharding import PartitionSpec as P

D = 128
HEADS = 8
FF = 256
EXPERTS = 4
HEAD_DIM = 16
HIDDEN = EXPERTS * FF

epsilon = 1e-05
far_below = -1e30
momentum_decay = 0.9
average_decay = 0.95

F32 = jnp.float32
BF16 = jnp.bfloat16
MESH = pl.DeviceIdType.MESH

ROW_GAIN_ONE, ROW_BIAS_ONE = 0, 1
ROW_QUERY = 2
ROW_CROSS_OUT = ROW_QUERY + D
ROW_GAIN_TWO = ROW_CROSS_OUT + D
ROW_BIAS_TWO = ROW_GAIN_TWO + 1
ROW_QKV = ROW_BIAS_TWO + 1
ROW_SELF_OUT = ROW_QKV + 3 * D
ROW_GAIN_THREE = ROW_SELF_OUT + D
ROW_BIAS_THREE = ROW_GAIN_THREE + 1
ROW_ROUTER = ROW_BIAS_THREE + 1
ROW_UP = ROW_ROUTER + EXPERTS
ROW_DOWN = ROW_UP + 2 * D * EXPERTS
SHARED_ROWS = ROW_DOWN + HIDDEN
BRANCH_ROWS = 2 + 2 * D

EXPERT_ROWS = 2 * HIDDEN
T_QUERY, T_CROSS_OUT, T_QKV, T_SELF_OUT = 0, D, 2 * D, 5 * D
T_SMALL = 6 * D
TAIL_ROWS = T_SMALL + 32
B_SMALL = 2 * D
BRANCH_SENT = B_SMALL + 16


def dot(a, b):
    return jnp.dot(a, b, preferred_element_type=F32)


def dot_points(a, b):
    return lax.dot_general(a, b, (((1,), (1,)), ((), ())), preferred_element_type=F32)


class Level:
    def __init__(self, size, index, member):
        self.size, self.index, self.member = size, index, member


def split_rows(rows, size):
    step = 16
    while rows % step or rows // step > size:
        step += 16
    return step, rows // step


class Reduction:
    def __init__(self, sizes, rows):
        self.sizes, self.rows = sizes, rows
        self.steps, self.owners = [], []
        for size in sizes:
            step, owners = split_rows(rows, size)
            self.steps.append(step)
            self.owners.append(owners)
            rows = step

    def scratch(self):
        shapes = [pltpu.VMEM((self.rows, D), BF16), pltpu.VMEM((self.rows, D), BF16)]
        for at, size in enumerate(self.sizes):
            shapes.append(pltpu.VMEM((size - 1, self.steps[at], D), BF16))
            shapes.append(pltpu.VMEM((self.steps[at], D), BF16))
            shapes += [pltpu.SemaphoreType.DMA((size - 1,))] * 4
        return shapes

    def bind(self, refs, levels):
        self.source, self.total = refs[0], refs[1]
        self.parts = [refs[2 + 6 * at : 8 + 6 * at] for at in range(len(self.sizes))]
        self.levels = levels

    def base(self, at):
        start = 0
        for upper in range(at):
            start = start + self.levels[upper].index * self.steps[upper]
        return start

    def guard(self, at, own):
        condition = None
        for upper in range(at + 1 if own else at):
            if self.owners[upper] < self.sizes[upper]:
                here = self.levels[upper].index < self.owners[upper]
                condition = here if condition is None else jnp.logical_and(condition, here)
        return condition

    def when(self, condition, body):
        if condition is None:
            body()
        else:
            pl.when(condition)(body)

    def each(self, at, body):
        def step(k, carry):
            body(k)
            return carry

        lax.fori_loop(1, self.sizes[at], step, 0)

    def scatter_copy(self, at, k):
        level, step = self.levels[at], self.steps[at]
        peer = (level.index + k) % level.size
        source = self.source if at == 0 else self.parts[at - 1][1]
        start = jnp.where(peer < self.owners[at], peer, 0) if self.owners[at] < level.size else peer
        received, _, send, receive = self.parts[at][:4]
        return peer, pltpu.make_async_remote_copy(
            src_ref=source.at[pl.ds(pl.multiple_of(start * step, 16), step), :],
            dst_ref=received.at[k - 1],
            send_sem=send.at[k - 1],
            recv_sem=receive.at[k - 1],
            device_id=level.member(peer),
            device_id_type=MESH,
        )

    def peer_guard(self, at, index):
        return None if self.owners[at] == self.sizes[at] else index < self.owners[at]

    def scatter(self, at):
        def go():
            def one(k):
                peer, copy = self.scatter_copy(at, k)
                self.when(self.peer_guard(at, peer), copy.start)

            self.each(at, one)

        self.when(self.guard(at, False), go)

    def add(self, at):
        level, step = self.levels[at], self.steps[at]

        def go():
            self.each(at, lambda k: self.scatter_copy(at, k)[1].wait_recv())
            received = self.parts[at][0]
            source = self.source if at == 0 else self.parts[at - 1][1]
            own = source[pl.ds(pl.multiple_of(level.index * step, 16), step), :].astype(F32)
            total = lax.fori_loop(
                0, level.size - 1, lambda k, so_far: so_far + received[k].astype(F32), own
            ).astype(BF16)
            if at + 1 < len(self.sizes):
                self.parts[at][1][...] = total
            else:
                start = pl.multiple_of(self.base(at) + level.index * step, 16)
                self.total[pl.ds(start, step), :] = total

        self.when(self.guard(at, True), go)

    def gather_copy(self, at, k, owner):
        level, step = self.levels[at], self.steps[at]
        start = pl.multiple_of(self.base(at) + owner * step, 16)
        send, receive = self.parts[at][4:]
        return pltpu.make_async_remote_copy(
            src_ref=self.total.at[pl.ds(start, step), :],
            dst_ref=self.total.at[pl.ds(start, step), :],
            send_sem=send.at[k - 1],
            recv_sem=receive.at[k - 1],
            device_id=level.member((level.index + k) % level.size),
            device_id_type=MESH,
        )

    def gather(self, at):
        def go():
            self.each(at, lambda k: self.gather_copy(at, k, self.levels[at].index).start())

        self.when(self.guard(at, True), go)

    def collect(self, at):
        level = self.levels[at]

        def go():
            def one(k):
                owner = (level.index + level.size - k) % level.size
                self.when(self.peer_guard(at, owner), self.gather_copy(at, k, owner).wait_recv)

            self.each(at, one)

        self.when(self.guard(at, False), go)

    def drain(self):
        for at in range(len(self.sizes)):

            def scattered(at=at):
                def one(k):
                    peer, copy = self.scatter_copy(at, k)
                    self.when(self.peer_guard(at, peer), copy.wait_send)

                self.each(at, one)

            def gathered(at=at):
                self.each(at, lambda k: self.gather_copy(at, k, self.levels[at].index).wait_send())

            self.when(self.guard(at, False), scattered)
            self.when(self.guard(at, True), gathered)


def near(pts):
    return 4 if pts % 4 == 0 else 1


def plan(fns, pts):
    inner = near(pts)
    two = [fns * inner, pts // inner]
    expert = Reduction(two, EXPERT_ROWS)
    if fns * pts <= 32:
        return expert, Reduction([fns * pts], TAIL_ROWS), Reduction([pts], BRANCH_SENT)
    return expert, Reduction(two, TAIL_ROWS), Reduction([inner, pts // inner], BRANCH_SENT)


def layer_norm(values):
    centred = values - jnp.mean(values, axis=0, keepdims=True)
    spread = jnp.mean(centred * centred, axis=0, keepdims=True)
    inverse = lax.rsqrt(spread + epsilon)
    return centred * inverse, inverse


def norm_back(normed, inverse, gain, upstream):
    scaled = upstream * gain
    first = jnp.mean(scaled, axis=0, keepdims=True)
    second = jnp.mean(scaled * normed, axis=0, keepdims=True)
    return (scaled - first - normed * second) * inverse


def heads_view(values):
    return values.reshape(HEADS, HEAD_DIM, values.shape[-1])


def feature_softmax(values):
    shaped = heads_view(values)
    powers = jnp.exp(shaped - jnp.max(shaped, axis=1, keepdims=True))
    return (powers * (1.0 / jnp.sum(powers, axis=1, keepdims=True))).reshape(values.shape)


def feature_softmax_back(soft, upstream):
    shaped, incoming = heads_view(soft), heads_view(upstream)
    inner = jnp.sum(shaped * incoming, axis=1, keepdims=True)
    return (shaped * (incoming - inner)).reshape(soft.shape)


def lane_fold(values, join):
    out = values[:, :D]
    for at in range(D, values.shape[1], D):
        out = join(out, values[:, at : at + D])
    return out


def step_kernel(fns, pts, block, *refs):
    refs = list(refs)

    def take(n):
        got = refs[:n]
        del refs[:n]
        return got

    (
        presence,
        fn_counts,
        item_counts,
        points_hbm,
        geometry_hbm,
        functions_hbm,
        cotangent_hbm,
        shared_hbm,
        branch_hbm,
    ) = take(9)
    output_hbm, input_grad_hbm, shared_grad_hbm, branch_grad_hbm = take(4)
    points_v, geometry_v, functions_v, cotangent_v, shared_v, branch_v = take(6)
    (
        query_w,
        query_t,
        cross_w,
        cross_t,
        qkv_w,
        qkv_t,
        self_w,
        self_t,
        up_w,
        up_t,
        down_w,
        down_t,
        kv_w,
        kv_t,
        router_t,
    ) = take(15)
    (
        fn_hidden,
        fn_powers,
        fn_low,
        fn_values,
        hidden_one,
        cross_soft,
        cross_out,
        after_cross,
        hidden_two,
        self_soft,
        key_powers,
        key_low,
        self_values,
        self_out_v,
        cot_t,
        gates_v,
        g_self,
        g_self_out,
        g_queries,
        g_cross,
        g_cross_out,
        hidden_v,
        pre_v,
    ) = take(23)
    up_sum, down_sum, norm_sums, out_v, in_grad_v, shared_out, branch_out = take(7)
    sent, got = take(2)
    local_sem, x_send, x_recv = take(3)
    expert, tail, branch = plan(fns, pts)
    expert_refs = take(len(expert.scratch()))
    tail_refs = take(len(tail.scratch()))
    branch_refs = take(len(branch.scratch()))
    assert not refs

    fn, pt = lax.axis_index("fn"), lax.axis_index("pts")
    inner = near(pts)
    outer_at, inner_at = pt // inner, pt % inner
    near_level = Level(
        fns * inner, fn * inner + inner_at, lambda j: (j // inner, outer_at * inner + j % inner)
    )
    far_level = Level(pts // inner, outer_at, lambda j: (fn, j * inner + inner_at))
    world = Level(fns * pts, fn * pts + pt, lambda j: (j // pts, j % pts))
    item_level = Level(pts, pt, lambda j: (fn, j))
    core_level = Level(inner, inner_at, lambda j: (fn, outer_at * inner + j))
    expert.bind(expert_refs, [near_level, far_level])
    if fns * pts <= 32:
        tail.bind(tail_refs, [world])
        branch.bind(branch_refs, [item_level])
        greeted = [world]
    else:
        tail.bind(tail_refs, [near_level, far_level])
        branch.bind(branch_refs, [core_level, far_level])
        greeted = [near_level, far_level]

    rows = points_v.shape[0]
    fn_rows = functions_v.shape[0]
    blocks = rows // block
    fn_blocks = fn_rows // block

    loads = []
    for at, (source, target) in enumerate(
        [
            (branch_hbm, branch_v),
            (functions_hbm, functions_v),
            (shared_hbm, shared_v),
            (points_hbm, points_v),
            (geometry_hbm, geometry_v),
            (cotangent_hbm, cotangent_v),
        ]
    ):
        loads.append(pltpu.make_async_copy(source, target, local_sem.at[at]))
        loads[-1].start()

    barrier = pltpu.get_barrier_semaphore()
    for level in greeted:

        def greet(k, carry, level=level):
            pl.semaphore_signal(
                barrier,
                inc=1,
                device_id=level.member((level.index + k) % level.size),
                device_id_type=MESH,
            )
            return carry

        lax.fori_loop(1, level.size, greet, 0)

    def exchange(at):
        return pltpu.make_async_remote_copy(
            src_ref=sent.at[at],
            dst_ref=got.at[at],
            send_sem=x_send.at[at],
            recv_sem=x_recv.at[at],
            device_id=((fn + 1) % fns, pt),
            device_id_type=MESH,
        )

    row_at = lax.broadcasted_iota(jnp.int32, (D, D), 0)
    column_at = lax.broadcasted_iota(jnp.int32, (D, D), 1)
    same_head = row_at // HEAD_DIM == column_at // HEAD_DIM
    diagonal = row_at == column_at

    def diagonal_blocks(full):
        return jnp.where(same_head, full, 0.0)

    def folded(full):
        kept = diagonal_blocks(full)
        out = kept[:HEAD_DIM]
        for head in range(1, HEADS):
            out = out + kept[head * HEAD_DIM : (head + 1) * HEAD_DIM]
        return out

    def unfolded(compact):
        return diagonal_blocks(jnp.concatenate([compact] * HEADS, axis=0))

    def to_row(column):
        return jnp.sum(jnp.where(diagonal, column, 0.0), axis=0, keepdims=True)

    def to_column(row):
        return jnp.sum(jnp.where(diagonal, row, 0.0), axis=1, keepdims=True)

    def span(b):
        return pl.ds(pl.multiple_of(b * block, block), block)

    def zeros(ref):
        ref[...] = jnp.zeros_like(ref)

    loads[0].wait()
    kv = jnp.concatenate(
        [branch_v[pl.ds(2, D, stride=2), :], branch_v[pl.ds(3, D, stride=2), :]], axis=1
    ).astype(BF16)
    kv_w[...] = kv
    kv_t[...] = kv.T
    branch_gain = to_column(branch_v[0:1, :])
    branch_bias = to_column(branch_v[1:2, :])
    fn_count = fn_counts[0, 0]
    fn_weight = (presence[0, 0] * fn_count).astype(F32)
    loads[1].wait()

    def fn_usable(b):
        at = lax.broadcasted_iota(jnp.int32, (1, block), 1) + b * block
        return at < fn_count

    def encode(b, so_far):
        normed, _ = layer_norm(functions_v[span(b), :].astype(F32).T)
        hidden = (normed * branch_gain + branch_bias).astype(BF16)
        fn_hidden[:, span(b)] = hidden
        keyval = dot(kv_t[...], hidden)
        keys = jnp.where(fn_usable(b), keyval[:D], far_below)
        fn_powers[:, span(b)] = keys
        fn_values[:, span(b)] = keyval[D:].astype(BF16)
        return jnp.maximum(so_far, lane_fold(keys, jnp.maximum))

    fn_max = jnp.max(
        lax.fori_loop(0, fn_blocks, encode, jnp.full((D, D), far_below, F32)), axis=1, keepdims=True
    )

    def fn_total(b, so_far):
        powers = jnp.where(fn_usable(b), jnp.exp(fn_powers[:, span(b)] - fn_max), 0.0)
        fn_powers[:, span(b)] = powers
        low = powers.astype(BF16)
        fn_low[:, span(b)] = low
        return (
            so_far[0] + lane_fold(powers, jnp.add),
            so_far[1] + dot_points(low, fn_values[:, span(b)]),
        )

    nothing = jnp.zeros((D, D), F32)
    totals, fn_sum = lax.fori_loop(0, fn_blocks, fn_total, (nothing, nothing))
    fn_scale = 1.0 / jnp.sum(totals, axis=1, keepdims=True)
    fn_summary = diagonal_blocks(fn_sum * fn_scale)
    weighted_summary = fn_weight * folded(fn_summary)
    sent[0, 0:HEAD_DIM, :] = weighted_summary
    sent[0, HEAD_DIM : HEAD_DIM + 8, :] = jnp.full((8, D), fn_weight, F32)
    pl.semaphore_wait(barrier, sum(level.size - 1 for level in greeted))
    exchange(0).start()

    loads[2].wait()

    def shared_rows(start, stride=1):
        return shared_v[pl.ds(start, D, stride=stride), :].astype(BF16)

    query_w[...] = shared_rows(ROW_QUERY)
    query_t[...] = shared_rows(ROW_QUERY).T
    cross_w[...] = shared_rows(ROW_CROSS_OUT)
    cross_t[...] = shared_rows(ROW_CROSS_OUT).T
    self_w[...] = shared_rows(ROW_SELF_OUT)
    self_t[...] = shared_rows(ROW_SELF_OUT).T
    for third in range(3):
        piece = shared_rows(ROW_QKV + third, 3)
        qkv_w[:, third * D : (third + 1) * D] = piece
        qkv_t[third * D : (third + 1) * D, :] = piece.T
    for piece_at in range(2 * EXPERTS):
        number, half = piece_at // 2, piece_at % 2
        piece = shared_rows(ROW_UP + number * FF + half, 2)
        up_w[:, piece_at * D : (piece_at + 1) * D] = piece
        up_t[piece_at * D : (piece_at + 1) * D, :] = piece.T
        piece = shared_rows(ROW_DOWN + piece_at * D)
        down_w[piece_at * D : (piece_at + 1) * D, :] = piece
        down_t[:, piece_at * D : (piece_at + 1) * D] = piece.T

    expert_at = lax.broadcasted_iota(jnp.int32, (8, D), 0)
    router_mask = lax.broadcasted_iota(jnp.int32, (8, D), 1) % EXPERTS == expert_at
    turned = jnp.zeros((8, D), F32)
    pickers = []
    for r in range(EXPERTS):
        picker = jnp.where(column_at == r * (D // EXPERTS) + row_at // EXPERTS, 1.0, 0.0).astype(BF16)
        pickers.append(picker)
        router_row = shared_v[ROW_ROUTER + r : ROW_ROUTER + r + 1, :]
        turned = turned + dot(jnp.where(router_mask, router_row, 0.0).astype(BF16), picker)
    router_t[...] = turned.astype(BF16)

    gain_one = to_column(shared_v[ROW_GAIN_ONE : ROW_GAIN_ONE + 1, :])
    bias_one = to_column(shared_v[ROW_BIAS_ONE : ROW_BIAS_ONE + 1, :])
    gain_two = to_column(shared_v[ROW_GAIN_TWO : ROW_GAIN_TWO + 1, :])
    bias_two = to_column(shared_v[ROW_BIAS_TWO : ROW_BIAS_TWO + 1, :])
    gain_three = to_column(shared_v[ROW_GAIN_THREE : ROW_GAIN_THREE + 1, :])
    bias_three = to_column(shared_v[ROW_BIAS_THREE : ROW_BIAS_THREE + 1, :])

    loads[3].wait()

    @pl.loop(0, blocks)
    def first_norm(b):
        points = points_v[span(b), :].astype(F32).T
        after_cross[:, span(b)] = points
        normed, _ = layer_norm(points)
        hidden = (normed * gain_one + bias_one).astype(BF16)
        hidden_one[:, span(b)] = hidden
        cross_soft[:, span(b)] = feature_softmax(dot(query_t[...], hidden))

    exchange(0).wait_recv()
    weight_total = fn_weight + got[0, HEAD_DIM : HEAD_DIM + 1, :]
    fn_share = fn_weight / weight_total
    mixed = unfolded((weighted_summary + got[0, 0:HEAD_DIM, :]) / weight_total)
    mixed_low = mixed.astype(BF16)
    mixed_t = mixed.T.astype(BF16)
    item_count = item_counts[0]

    def usable(b):
        at = lax.broadcasted_iota(jnp.int32, (1, block), 1) + (b * block + fn * rows)
        return at < item_count

    def cross(b, so_far):
        out = dot(mixed_t, cross_soft[:, span(b)].astype(BF16)).astype(BF16)
        cross_out[:, span(b)] = out
        after = after_cross[:, span(b)] + dot(cross_t[...], out)
        after_cross[:, span(b)] = after
        normed, _ = layer_norm(after)
        hidden = (normed * gain_two + bias_two).astype(BF16)
        hidden_two[:, span(b)] = hidden
        qkv = dot(qkv_t[...], hidden)
        self_soft[:, span(b)] = feature_softmax(qkv[:D])
        keys = jnp.where(usable(b), qkv[D : 2 * D], far_below)
        key_powers[:, span(b)] = keys
        self_values[:, span(b)] = qkv[2 * D :].astype(BF16)
        return jnp.maximum(so_far, lane_fold(keys, jnp.maximum))

    key_max = jnp.max(
        lax.fori_loop(0, blocks, cross, jnp.full((D, D), far_below, F32)), axis=1, keepdims=True
    )

    def key_total(b, so_far):
        powers = jnp.where(usable(b), jnp.exp(key_powers[:, span(b)] - key_max), 0.0)
        key_powers[:, span(b)] = powers
        low = powers.astype(BF16)
        key_low[:, span(b)] = low
        return (
            so_far[0] + lane_fold(powers, jnp.add),
            so_far[1] + dot_points(low, self_values[:, span(b)]),
        )

    totals, key_sum = lax.fori_loop(0, blocks, key_total, (nothing, nothing))
    own_total = jnp.sum(totals, axis=1, keepdims=True)
    sent[1, 0:HEAD_DIM, :] = folded(key_sum)
    own_stats = jnp.concatenate([to_row(key_max), to_row(own_total), jnp.zeros((6, D), F32)], axis=0)
    sent[1, HEAD_DIM : HEAD_DIM + 8, :] = own_stats
    exchange(1).start()

    loads[4].wait()
    loads[5].wait()

    @pl.loop(0, blocks)
    def gates(b):
        cot_t[:, span(b)] = cotangent_v[span(b), :].astype(F32).T.astype(BF16)
        logits = dot_points(router_t[...], geometry_v[span(b), :])[:EXPERTS]
        powers = jnp.exp(logits - jnp.max(logits, axis=0, keepdims=True))
        gates_v[0:EXPERTS, span(b)] = powers * (1.0 / jnp.sum(powers, axis=0, keepdims=True))

    zeros(up_sum)
    zeros(down_sum)
    zeros(norm_sums)

    exchange(1).wait_recv()
    other_max = to_column(got[1, HEAD_DIM : HEAD_DIM + 1, :])
    other_total = to_column(got[1, HEAD_DIM + 1 : HEAD_DIM + 2, :])
    joint_max = jnp.maximum(key_max, other_max)
    own_factor, other_factor = jnp.exp(key_max - joint_max), jnp.exp(other_max - joint_max)
    joint_scale = 1.0 / (own_total * own_factor + other_total * other_factor)
    own_factor, other_factor = own_factor * joint_scale, other_factor * joint_scale
    self_summary = diagonal_blocks(key_sum) * own_factor + unfolded(got[1, 0:HEAD_DIM, :]) * other_factor
    self_low = self_summary.astype(BF16)
    self_summary_t = self_summary.T.astype(BF16)

    def experts(b, sums):
        weights = self_soft[:, span(b)].astype(BF16)
        mixed_rows = dot(self_summary_t, weights).astype(BF16)
        self_out_v[:, span(b)] = mixed_rows
        after = after_cross[:, span(b)] + dot(self_t[...], mixed_rows)
        normed, inverse = layer_norm(after)
        hidden = (normed * gain_three + bias_three).astype(BF16)
        arriving = cot_t[:, span(b)]
        gate_grads = []
        for number in range(EXPERTS):
            rows_of = slice(number * FF, (number + 1) * FF)
            gate = gates_v[number : number + 1, span(b)]
            pre = dot(up_t[rows_of, :], hidden)
            back = dot(down_w[rows_of, :], arriving)
            cdf = 0.5 + 0.5 * lax.erf(pre * math.sqrt(0.5))
            density = jnp.exp2(pre * pre * (-0.5 * math.log2(math.e))) * (1.0 / math.sqrt(2.0 * math.pi))
            active = pre * cdf
            gate_grads.append(jnp.sum(active * back, axis=0, keepdims=True))
            hidden_v[rows_of, :] = (active * gate).astype(BF16)
            pre_v[rows_of, :] = (back * gate * (cdf + pre * density)).astype(BF16)
        out_v[span(b), :] = (after + dot(down_t[...], hidden_v[...])).T.astype(BF16)
        down_sum[...] += dot_points(hidden_v[...], arriving)
        up_sum[...] += dot_points(hidden, pre_v[...])
        gate = gates_v[0:EXPERTS, span(b)]
        g_gates = jnp.concatenate(gate_grads, axis=0)
        g_logits = gate * (g_gates - jnp.sum(gate * g_gates, axis=0, keepdims=True))
        g_logits = jnp.concatenate([g_logits, jnp.zeros_like(g_logits)], axis=0).astype(BF16)
        upstream = dot(up_w[...], pre_v[...])
        norm_sums[4] += lane_fold(upstream * normed, jnp.add)
        norm_sums[5] += lane_fold(upstream, jnp.add)
        g_after = arriving.astype(F32) + norm_back(normed, inverse, gain_three, upstream)
        g_self[:, span(b)] = g_after
        g_proj = g_after.astype(BF16)
        g_out = dot(self_w[...], g_proj).astype(BF16)
        g_self_out[:, span(b)] = g_out
        return (
            sums[0] + dot(g_logits, geometry_v[span(b), :]),
            sums[1] + dot_points(mixed_rows, g_proj),
            sums[2] + dot_points(weights, g_out),
        )

    router_sum, self_out_sum, summary_grad = lax.fori_loop(
        0, blocks, experts, (jnp.zeros((8, D), F32), nothing, nothing)
    )
    own_grad = folded(summary_grad)
    sent[2, 0:HEAD_DIM, :] = own_grad
    exchange(2).start()
    for piece_at in range(2 * EXPERTS):
        expert.source[piece_at * D : (piece_at + 1) * D, :] = up_sum[
            :, piece_at * D : (piece_at + 1) * D
        ].astype(BF16)
    expert.source[HIDDEN:, :] = down_sum[...].astype(BF16)
    expert.scatter(0)
    tail.source[T_SELF_OUT : T_SELF_OUT + D, :] = self_out_sum.astype(BF16)

    @pl.loop(0, blocks)
    def query_grads(b):
        back = dot(self_low, g_self_out[:, span(b)])
        g_queries[:, span(b)] = feature_softmax_back(self_soft[:, span(b)], back).astype(BF16)

    exchange(2).wait_recv()
    joint_grad = unfolded(own_grad + got[2, 0:HEAD_DIM, :])
    scaled_grad = joint_grad * own_factor
    correction = jnp.sum(scaled_grad * self_summary, axis=1, keepdims=True)
    scaled_low = scaled_grad.astype(BF16)
    scaled_t = scaled_grad.T.astype(BF16)

    def self_back(b, sums):
        powers = key_powers[:, span(b)]
        g_keys = powers * (dot(scaled_low, self_values[:, span(b)]) - correction)
        g_values = dot(scaled_t, key_low[:, span(b)])
        g_qkv = jnp.concatenate(
            [g_queries[:, span(b)], g_keys.astype(BF16), g_values.astype(BF16)], axis=0
        )
        upstream = dot(qkv_w[...], g_qkv)
        normed, inverse = layer_norm(after_cross[:, span(b)])
        norm_sums[2] += lane_fold(upstream * normed, jnp.add)
        norm_sums[3] += lane_fold(upstream, jnp.add)
        g_after = g_self[:, span(b)] + norm_back(normed, inverse, gain_two, upstream)
        g_cross[:, span(b)] = g_after
        g_proj = g_after.astype(BF16)
        g_out = dot(cross_w[...], g_proj).astype(BF16)
        g_cross_out[:, span(b)] = g_out
        return (
            sums[0] + dot_points(hidden_two[:, span(b)], g_qkv),
            sums[1] + dot_points(cross_out[:, span(b)], g_proj),
            sums[2] + dot_points(cross_soft[:, span(b)].astype(BF16), g_out),
        )

    qkv_sum, cross_out_sum, mixed_grad = lax.fori_loop(
        0, blocks, self_back, (jnp.zeros((D, 3 * D), F32), nothing, nothing)
    )
    own_mixed = folded(mixed_grad)
    sent[3, 0:HEAD_DIM, :] = own_mixed
    exchange(3).start()
    expert.add(0)
    expert.scatter(1)
    for third in range(3):
        tail.source[T_QKV + third * D : T_QKV + (third + 1) * D, :] = qkv_sum[
            :, third * D : (third + 1) * D
        ].astype(BF16)
    tail.source[T_CROSS_OUT : T_CROSS_OUT + D, :] = cross_out_sum.astype(BF16)

    def query_back(b, query_sum):
        g_query = feature_softmax_back(
            cross_soft[:, span(b)], dot(mixed_low, g_cross_out[:, span(b)])
        ).astype(BF16)
        upstream = dot(query_w[...], g_query)
        normed, inverse = layer_norm(points_v[span(b), :].astype(F32).T)
        norm_sums[0] += lane_fold(upstream * normed, jnp.add)
        norm_sums[1] += lane_fold(upstream, jnp.add)
        total = g_cross[:, span(b)] + norm_back(normed, inverse, gain_one, upstream)
        in_grad_v[span(b), :] = total.T.astype(BF16)
        return query_sum + dot_points(hidden_one[:, span(b)], g_query)

    query_sum = lax.fori_loop(0, blocks, query_back, nothing)
    stores = [
        pltpu.make_async_copy(out_v, output_hbm, local_sem.at[6]),
        pltpu.make_async_copy(in_grad_v, input_grad_hbm, local_sem.at[7]),
    ]
    for store in stores:
        store.start()
    tail.source[T_QUERY : T_QUERY + D, :] = query_sum.astype(BF16)
    small = [to_row(jnp.sum(norm_sums[at], axis=1, keepdims=True)) for at in range(6)]
    tail.source[T_SMALL:, :] = jnp.concatenate(
        [router_sum, *small, jnp.zeros((TAIL_ROWS - T_SMALL - 14, D), F32)], axis=0
    ).astype(BF16)
    tail.scatter(0)

    exchange(3).wait_recv()
    fn_grad = unfolded((own_mixed + got[3, 0:HEAD_DIM, :]) * fn_share).astype(BF16).astype(F32)
    fn_scaled = fn_grad * fn_scale
    fn_correction = jnp.sum(fn_scaled * fn_summary, axis=1, keepdims=True)
    fn_scaled_low = fn_scaled.astype(BF16)
    fn_scaled_t = fn_scaled.T.astype(BF16)
    expert.add(1)
    expert.gather(1)

    def branch_back(b, sums):
        g_keys = fn_powers[:, span(b)] * (dot(fn_scaled_low, fn_values[:, span(b)]) - fn_correction)
        g_values = dot(fn_scaled_t, fn_low[:, span(b)])
        g_keyval = jnp.concatenate([g_keys, g_values], axis=0).astype(BF16)
        upstream = dot(kv_w[...], g_keyval)
        normed, _ = layer_norm(functions_v[span(b), :].astype(F32).T)
        return (
            sums[0] + lane_fold(upstream * normed, jnp.add),
            sums[1] + lane_fold(upstream, jnp.add),
            sums[2] + dot_points(fn_hidden[:, span(b)], g_keyval),
        )

    gain_sum, bias_sum, kv_sum = lax.fori_loop(
        0, fn_blocks, branch_back, (nothing, nothing, jnp.zeros((D, 2 * D), F32))
    )
    for half in range(2):
        branch.source[half * D : (half + 1) * D, :] = kv_sum[:, half * D : (half + 1) * D].astype(BF16)
    branch.source[B_SMALL:, :] = jnp.concatenate(
        [
            to_row(jnp.sum(gain_sum, axis=1, keepdims=True)),
            to_row(jnp.sum(bias_sum, axis=1, keepdims=True)),
            jnp.zeros((14, D), F32),
        ],
        axis=0,
    ).astype(BF16)
    branch.scatter(0)

    expert.collect(1)
    expert.gather(0)
    for at in range(len(tail.sizes)):
        tail.add(at)
        if at + 1 < len(tail.sizes):
            tail.scatter(at + 1)
    tail.gather(len(tail.sizes) - 1)
    for at in range(len(branch.sizes)):
        branch.add(at)
        if at + 1 < len(branch.sizes):
            branch.scatter(at + 1)
    branch.gather(len(branch.sizes) - 1)

    expert.collect(0)
    for piece_at in range(2 * EXPERTS):
        number, half = piece_at // 2, piece_at % 2
        shared_out[pl.ds(ROW_UP + number * FF + half, D, stride=2), :] = expert.total[
            piece_at * D : (piece_at + 1) * D, :
        ].astype(F32)
    shared_out[ROW_DOWN : ROW_DOWN + HIDDEN, :] = expert.total[HIDDEN:, :].astype(F32)

    for at in reversed(range(len(tail.sizes))):
        tail.collect(at)
        if at:
            tail.gather(at - 1)
    for at in reversed(range(len(branch.sizes))):
        branch.collect(at)
        if at:
            branch.gather(at - 1)

    def from_tail(start):
        return tail.total[start : start + D, :].astype(F32)

    shared_out[ROW_QUERY : ROW_QUERY + D, :] = from_tail(T_QUERY)
    shared_out[ROW_CROSS_OUT : ROW_CROSS_OUT + D, :] = from_tail(T_CROSS_OUT)
    shared_out[ROW_SELF_OUT : ROW_SELF_OUT + D, :] = from_tail(T_SELF_OUT)
    for third in range(3):
        shared_out[pl.ds(ROW_QKV + third, D, stride=3), :] = from_tail(T_QKV + third * D)
    rest = tail.total[T_SMALL:, :].astype(F32)
    for at, row in enumerate(
        [ROW_GAIN_ONE, ROW_BIAS_ONE, ROW_GAIN_TWO, ROW_BIAS_TWO, ROW_GAIN_THREE, ROW_BIAS_THREE]
    ):
        shared_out[row : row + 1, :] = rest[8 + at : 9 + at]
    router_low = rest[:8].astype(BF16)
    for r in range(EXPERTS):
        spread = dot_points(router_low, pickers[r])
        shared_out[ROW_ROUTER + r : ROW_ROUTER + r + 1, :] = jnp.sum(
            jnp.where(router_mask, spread, 0.0), axis=0, keepdims=True
        )
    for half in range(2):
        branch_out[pl.ds(2 + half, D, stride=2), :] = branch.total[
            half * D : (half + 1) * D, :
        ].astype(F32)
    branch_out[0:2, :] = branch.total[B_SMALL:, :].astype(F32)[0:2]
    stores.append(pltpu.make_async_copy(shared_out, shared_grad_hbm, local_sem.at[8]))
    stores.append(pltpu.make_async_copy(branch_out, branch_grad_hbm, local_sem.at[9]))
    for store in stores[2:]:
        store.start()

    for at in range(4):
        exchange(at).wait_send()
    for reduction in (expert, tail, branch):
        reduction.drain()
    for store in stores:
        store.wait()


def whole_step(fns, pts, points, geometry, functions, presence, fn_counts, item_counts, cotangent, shared, branch):
    rows, fn_rows = points.shape[0], functions.shape[0]
    block = 512
    smem = pl.BlockSpec(memory_space=pltpu.SMEM)
    anywhere = pl.BlockSpec(memory_space=pl.ANY)

    def low(*shape):
        return pltpu.VMEM(shape, BF16)

    def wide(*shape):
        return pltpu.VMEM(shape, F32)

    scratch = [low(rows, D), low(rows, D), low(fn_rows, D), low(rows, D), wide(SHARED_ROWS, D), wide(BRANCH_ROWS, D)]
    scratch += [low(D, D)] * 4 + [low(D, 3 * D), low(3 * D, D)] + [low(D, D)] * 2
    scratch += [low(D, HIDDEN), low(HIDDEN, D), low(HIDDEN, D), low(D, HIDDEN), low(D, 2 * D), low(2 * D, D), low(8, D)]
    scratch += [
        low(D, fn_rows),
        wide(D, fn_rows),
        low(D, fn_rows),
        low(D, fn_rows),
        low(D, rows),
        wide(D, rows),
        low(D, rows),
        wide(D, rows),
        low(D, rows),
        wide(D, rows),
        wide(D, rows),
        low(D, rows),
        low(D, rows),
        low(D, rows),
        low(D, rows),
        wide(8, rows),
        wide(D, rows),
        low(D, rows),
        low(D, rows),
        wide(D, rows),
        low(D, rows),
        low(HIDDEN, block),
        low(HIDDEN, block),
    ]
    scratch += [
        wide(D, HIDDEN),
        wide(HIDDEN, D),
        wide(6, D, D),
        low(rows, D),
        low(rows, D),
        wide(SHARED_ROWS, D),
        wide(BRANCH_ROWS, D),
    ]
    scratch += [wide(4, HEAD_DIM + 8, D), wide(4, HEAD_DIM + 8, D)]
    scratch += [pltpu.SemaphoreType.DMA((10,)), pltpu.SemaphoreType.DMA((4,)), pltpu.SemaphoreType.DMA((4,))]
    for reduction in plan(fns, pts):
        scratch += reduction.scratch()
    return pl.pallas_call(
        functools.partial(step_kernel, fns, pts, block),
        out_shape=[
            jax.ShapeDtypeStruct((rows, D), BF16),
            jax.ShapeDtypeStruct((rows, D), BF16),
            jax.ShapeDtypeStruct((SHARED_ROWS, D), F32),
            jax.ShapeDtypeStruct((BRANCH_ROWS, D), F32),
        ],
        in_specs=[smem] * 3 + [anywhere] * 6,
        out_specs=[anywhere] * 4,
        scratch_shapes=scratch,
        compiler_params=pltpu.CompilerParams(
            collective_id=0, has_side_effects=True, vmem_limit_bytes=56 << 20
        ),
    )(presence, fn_counts, item_counts, points, geometry, functions, cotangent, shared, branch)


def sgd_update(weights, momentum, average, gradient, step_rate):
    momentum_new = momentum_decay * momentum + gradient
    weights_new = weights - step_rate * (gradient + momentum_decay * momentum_new)
    average_new = average_decay * average + (1.0 - average_decay) * weights_new
    return (weights_new, momentum_new, average_new, weights_new.astype(BF16))


def local(
    fns,
    pts,
    points_in,
    geometry,
    functions,
    presence,
    fn_counts,
    item_counts,
    cotangent,
    shared_weights,
    shared_momentum,
    shared_average,
    branch_weights,
    branch_momentum,
    branch_average,
):
    rows, fn_rows = points_in.shape[1], functions.shape[2]
    output, input_grad, shared_total, branch_total = whole_step(
        fns,
        pts,
        points_in.reshape(rows, D),
        geometry.reshape(rows, D),
        functions.reshape(fn_rows, D),
        presence,
        fn_counts,
        item_counts,
        cotangent.reshape(rows, D),
        shared_weights.reshape(SHARED_ROWS, D),
        branch_weights.reshape(BRANCH_ROWS, D),
    )
    norm_grads = jnp.concatenate(
        [
            shared_total[at : at + 2]
            for at in (ROW_GAIN_ONE, ROW_GAIN_TWO, ROW_GAIN_THREE)
        ],
        axis=0,
    )
    shared_rate = 0.1 / math.sqrt(pts * rows * fns)
    branch_rate = 0.1 / math.sqrt(pts * fn_rows)
    shared_new = sgd_update(
        shared_weights, shared_momentum, shared_average, shared_total.reshape(-1), shared_rate
    )
    branch_new = sgd_update(
        branch_weights, branch_momentum, branch_average, branch_total.reshape(1, -1), branch_rate
    )
    return (
        output.reshape(1, rows, D),
        input_grad.reshape(1, rows, D),
        *shared_new,
        *branch_new,
        norm_grads,
    )


def solution(mesh):
    split = P("pts", "fn", None)
    return jax.shard_map(
        functools.partial(local, mesh.shape["fn"], mesh.shape["pts"]),
        mesh=mesh,
        in_specs=(
            split,
            split,
            P("fn", "pts", None, None),
            P("fn", "pts"),
            P("fn", "pts"),
            P("pts"),
            split,
            P(),
            P(),
            P(),
            P("fn", None),
            P("fn", None),
            P("fn", None),
        ),
        out_specs=(
            split,
            split,
            P(),
            P(),
            P(),
            P(),
            P("fn", None),
            P("fn", None),
            P("fn", None),
            P("fn", None),
            P(),
        ),
        check_vma=False,
    )
```

```python
import functools
import math

import jax
import jax.numpy as jnp
from jax import lax
from jax.experimental import pallas as pl
from jax.experimental.pallas import tpu as pltpu
from jax.sharding import PartitionSpec as P

D = 128
HEADS = 8
FF = 256
EXPERTS = 4
HEAD_DIM = 16
HIDDEN = EXPERTS * FF

epsilon = 1e-05
far_below = -1e30
momentum_decay = 0.9
average_decay = 0.95

F32 = jnp.float32
BF16 = jnp.bfloat16
MESH = pl.DeviceIdType.MESH

ROW_GAIN_ONE, ROW_BIAS_ONE = 0, 1
ROW_QUERY = 2
ROW_CROSS_OUT = ROW_QUERY + D
ROW_GAIN_TWO = ROW_CROSS_OUT + D
ROW_BIAS_TWO = ROW_GAIN_TWO + 1
ROW_QKV = ROW_BIAS_TWO + 1
ROW_SELF_OUT = ROW_QKV + 3 * D
ROW_GAIN_THREE = ROW_SELF_OUT + D
ROW_BIAS_THREE = ROW_GAIN_THREE + 1
ROW_ROUTER = ROW_BIAS_THREE + 1
ROW_UP = ROW_ROUTER + EXPERTS
ROW_DOWN = ROW_UP + 2 * D * EXPERTS
SHARED_ROWS = ROW_DOWN + HIDDEN
BRANCH_ROWS = 2 + 2 * D

EXPERT_ROWS = 2 * FF
MIDDLE_ROWS = 4 * D
LAST_ROWS = 2 * D + 32
BRANCH_SENT = 2 * D


def dot(a, b):
    return jnp.dot(a, b, preferred_element_type=F32)


def dot_points(a, b):
    return lax.dot_general(a, b, (((1,), (1,)), ((), ())), preferred_element_type=F32)


class Level:
    def __init__(self, size, index, member):
        self.size, self.index, self.member = size, index, member


def split_rows(rows, size):
    step = 16
    while rows % step or rows // step > size:
        step += 16
    return step, rows // step


class Reduction:
    def __init__(self, sizes, rows):
        self.sizes, self.rows = sizes, rows
        self.steps, self.owners = [], []
        for size in sizes:
            step, owners = split_rows(rows, size)
            self.steps.append(step)
            self.owners.append(owners)
            rows = step

    def scratch(self):
        shapes = [pltpu.VMEM((self.rows, D), BF16), pltpu.VMEM((self.rows, D), BF16)]
        for at, size in enumerate(self.sizes):
            shapes.append(pltpu.VMEM(((size - 1) * self.steps[at], D), BF16))
            shapes.append(pltpu.VMEM((self.steps[at], D), BF16))
            shapes.append(pltpu.SemaphoreType.DMA((4,)))
        return shapes

    def bind(self, refs, levels):
        self.source, self.total = refs[0], refs[1]
        self.parts = [refs[2 + 3 * at : 5 + 3 * at] for at in range(len(self.sizes))]
        self.levels = levels
        last = len(self.sizes) - 1
        self.steps_left = []
        for at in range(last):
            self.steps_left.append(lambda at=at: (self.add(at), self.scatter(at + 1)))
        self.steps_left.append(lambda: (self.add(last), self.gather(last)))
        for at in range(last, 0, -1):
            self.steps_left.append(lambda at=at: (self.collect(at), self.gather(at - 1)))
        self.steps_left.append(lambda: self.collect(0))

    def begin(self):
        self.scatter(0)

    def advance(self):
        if self.steps_left:
            self.steps_left.pop(0)()

    def base(self, at):
        start = 0
        for upper in range(at):
            start = start + self.levels[upper].index * self.steps[upper]
        return start

    def inside(self, at):
        condition = None
        for upper in range(at):
            if self.owners[upper] < self.sizes[upper]:
                here = self.levels[upper].index < self.owners[upper]
                condition = here if condition is None else jnp.logical_and(condition, here)
        return condition

    def when(self, condition, body):
        if condition is None:
            body()
        else:
            pl.when(condition)(body)

    def split(self, at, owner, other):
        def go():
            if self.owners[at] == self.sizes[at]:
                owner()
            else:
                here = self.levels[at].index < self.owners[at]
                pl.when(here)(owner)
                if other is not None:
                    pl.when(jnp.logical_not(here))(other)

        self.when(self.inside(at), go)

    def rows_from(self, at):
        return self.source if at == 0 else self.parts[at - 1][1]

    def wait(self, at, sem, rows, sending):
        window = self.source if rows <= self.rows else self.parts[at][0]
        copy = pltpu.make_async_remote_copy(
            src_ref=window.at[pl.ds(0, rows), :],
            dst_ref=window.at[pl.ds(0, rows), :],
            send_sem=self.parts[at][2].at[sem],
            recv_sem=self.parts[at][2].at[sem],
            device_id=self.levels[at].member(self.levels[at].index),
            device_id_type=MESH,
        )
        (copy.wait_send if sending else copy.wait_recv)()

    def scatter(self, at):
        level, step, owners = self.levels[at], self.steps[at], self.owners[at]
        received, _, sems = self.parts[at]

        def go():
            def one(k, carry):
                peer = (level.index + k) % level.size

                def start():
                    pltpu.make_async_remote_copy(
                        src_ref=self.rows_from(at).at[pl.ds(pl.multiple_of(peer * step, 16), step), :],
                        dst_ref=received.at[pl.ds(pl.multiple_of((k - 1) * step, 16), step), :],
                        send_sem=sems.at[0],
                        recv_sem=sems.at[1],
                        device_id=level.member(peer),
                        device_id_type=MESH,
                    ).start()

                self.when(None if owners == level.size else peer < owners, start)
                return carry

            lax.fori_loop(1, level.size, one, 0)

        self.when(self.inside(at), go)

    def add(self, at):
        level, step = self.levels[at], self.steps[at]

        def go():
            received, kept, _ = self.parts[at]
            self.wait(at, 1, (level.size - 1) * step, False)
            start = pl.multiple_of(level.index * step, 16)
            total = self.rows_from(at)[pl.ds(start, step), :].astype(F32)
            for k in range(level.size - 1):
                total = total + received[k * step : (k + 1) * step, :].astype(F32)
            if at + 1 < len(self.sizes):
                kept[...] = total.astype(BF16)
            else:
                self.total[pl.ds(pl.multiple_of(self.base(at) + start, 16), step), :] = total.astype(BF16)

        self.split(at, go, None)

    def gather(self, at):
        level, step = self.levels[at], self.steps[at]
        sems = self.parts[at][2]

        def go():
            rows = pl.ds(pl.multiple_of(self.base(at) + level.index * step, 16), step)

            def one(k, carry):
                pltpu.make_async_remote_copy(
                    src_ref=self.total.at[rows, :],
                    dst_ref=self.total.at[rows, :],
                    send_sem=sems.at[2],
                    recv_sem=sems.at[3],
                    device_id=level.member((level.index + k) % level.size),
                    device_id_type=MESH,
                ).start()
                return carry

            lax.fori_loop(1, level.size, one, 0)

        self.split(at, go, None)

    def collect(self, at):
        step, owners = self.steps[at], self.owners[at]
        self.split(
            at,
            lambda: self.wait(at, 3, (owners - 1) * step, False) if owners > 1 else None,
            lambda: self.wait(at, 3, owners * step, False),
        )

    def drain(self):
        for at, size in enumerate(self.sizes):
            step, owners = self.steps[at], self.owners[at]

            def owner():
                if owners > 1:
                    self.wait(at, 0, (owners - 1) * step, True)
                self.wait(at, 2, (size - 1) * step, True)

            self.split(at, owner, lambda: self.wait(at, 0, owners * step, True))


def inner_size(pts):
    return 2 if pts % 2 == 0 else 1


def plan(fns, pts):
    core = inner_size(pts)
    outer = pts // core
    if fns * outer <= 16:
        everyone, items = [core, fns * outer], [core, outer]
    else:
        everyone, items = [core, fns * 4, outer // 4], [core, 4, outer // 4]
    return [Reduction(everyone, EXPERT_ROWS) for _ in range(EXPERTS)] + [
        Reduction(everyone, MIDDLE_ROWS),
        Reduction(everyone, LAST_ROWS),
        Reduction(items, BRANCH_SENT),
    ]


def layer_norm(values):
    centred = values - jnp.mean(values, axis=0, keepdims=True)
    spread = jnp.mean(centred * centred, axis=0, keepdims=True)
    inverse = lax.rsqrt(spread + epsilon)
    return centred * inverse, inverse


def norm_back(normed, inverse, gain, upstream):
    scaled = upstream * gain
    first = jnp.mean(scaled, axis=0, keepdims=True)
    second = jnp.mean(scaled * normed, axis=0, keepdims=True)
    return (scaled - first - normed * second) * inverse


def heads_view(values):
    return values.reshape(HEADS, HEAD_DIM, values.shape[-1])


def feature_softmax(values):
    shaped = heads_view(values)
    powers = jnp.exp(shaped - jnp.max(shaped, axis=1, keepdims=True))
    return (powers * (1.0 / jnp.sum(powers, axis=1, keepdims=True))).reshape(values.shape)


def feature_softmax_back(soft, upstream):
    shaped, incoming = heads_view(soft), heads_view(upstream)
    inner = jnp.sum(shaped * incoming, axis=1, keepdims=True)
    return (shaped * (incoming - inner)).reshape(soft.shape)


def over_points(values):
    return jnp.sum(values, axis=1, keepdims=True)


def step_kernel(fns, pts, *refs):
    refs = list(refs)

    def take(n):
        got = refs[:n]
        del refs[:n]
        return got

    presence, fn_counts, item_counts = take(3)
    points_hbm, geometry_hbm, functions_hbm, cotangent_hbm, shared_hbm, branch_hbm = take(6)
    output, input_grad, shared_out, branch_out = take(4)
    points_v, geometry_v, functions_v, cotangent_v, shared_v, branch_v, branch_rows = take(7)
    fn_powers, fn_low, fn_values, fn_hidden, hidden_v, pre_v = take(6)
    sent, got = take(2)
    local_sem, x_send, x_recv = take(3)
    reductions = plan(fns, pts)
    bound = [take(len(reduction.scratch())) for reduction in reductions]
    assert not refs

    fn, pt = lax.axis_index("fn"), lax.axis_index("pts")
    core_size = inner_size(pts)
    outer_size = pts // core_size
    outer, core = pt // core_size, pt % core_size
    core_level = Level(core_size, core, lambda j: (fn, outer * core_size + j))
    if fns * outer_size <= 16:
        everyone = [
            core_level,
            Level(
                fns * outer_size,
                fn * outer_size + outer,
                lambda j: (j // outer_size, j % outer_size * core_size + core),
            ),
        ]
        items = [core_level, Level(outer_size, outer, lambda j: (fn, j * core_size + core))]
        greeted = everyone
    else:
        far, near = outer // 4, outer % 4
        far_level = Level(outer_size // 4, far, lambda j: (fn, (j * 4 + near) * core_size + core))
        everyone = [
            core_level,
            Level(fns * 4, fn * 4 + near, lambda j: (j // 4, (far * 4 + j % 4) * core_size + core)),
            far_level,
        ]
        items = [core_level, Level(4, near, lambda j: (fn, (far * 4 + j) * core_size + core)), far_level]
        greeted = everyone
    for reduction, scratch in zip(reductions, bound):
        reduction.bind(scratch, items if reduction is reductions[-1] else everyone)
    experts, middle, last, branch = reductions[:EXPERTS], *reductions[EXPERTS:]

    rows, fn_rows = points_v.shape[0], functions_v.shape[0]

    loads = []
    for at, (source, target) in enumerate(
        [
            (branch_hbm, branch_v),
            (functions_hbm, functions_v),
            (shared_hbm, shared_v),
            (points_hbm, points_v),
            (geometry_hbm, geometry_v),
            (cotangent_hbm, cotangent_v),
        ]
    ):
        loads.append(pltpu.make_async_copy(source, target, local_sem.at[at]))
        loads[-1].start()

    barrier = pltpu.get_barrier_semaphore()
    for level in greeted:

        def greet(k, carry, level=level):
            pl.semaphore_signal(
                barrier,
                inc=1,
                device_id=level.member((level.index + k) % level.size),
                device_id_type=MESH,
            )
            return carry

        lax.fori_loop(1, level.size, greet, 0)

    def exchange(at):
        return pltpu.make_async_remote_copy(
            src_ref=sent.at[at],
            dst_ref=got.at[at],
            send_sem=x_send.at[at],
            recv_sem=x_recv.at[at],
            device_id=((fn + 1) % fns, pt),
            device_id_type=MESH,
        )

    row_at = lax.broadcasted_iota(jnp.int32, (D, D), 0)
    column_at = lax.broadcasted_iota(jnp.int32, (D, D), 1)
    same_head = row_at // HEAD_DIM == column_at // HEAD_DIM
    diagonal = row_at == column_at

    def diagonal_blocks(full):
        return jnp.where(same_head, full, 0.0)

    def folded(full):
        kept = diagonal_blocks(full)
        out = kept[:HEAD_DIM]
        for head in range(1, HEADS):
            out = out + kept[head * HEAD_DIM : (head + 1) * HEAD_DIM]
        return out

    def unfolded(compact):
        return diagonal_blocks(jnp.concatenate([compact] * HEADS, axis=0))

    def to_row(column):
        return jnp.sum(jnp.where(diagonal, column, 0.0), axis=0, keepdims=True)

    def to_column(row):
        return jnp.sum(jnp.where(diagonal, row, 0.0), axis=1, keepdims=True)

    loads[0].wait()
    for r in range(BRANCH_ROWS):
        branch_rows[r : r + 1, :] = branch_v[0:1, r * D : (r + 1) * D]
    kv = jnp.concatenate(
        [branch_rows[pl.ds(2, D, stride=2), :], branch_rows[pl.ds(3, D, stride=2), :]], axis=1
    ).astype(BF16)
    branch_gain = to_column(branch_rows[0:1, :])
    branch_bias = to_column(branch_rows[1:2, :])
    fn_count = fn_counts[0, 0]
    fn_weight = (presence[0, 0] * fn_count).astype(F32)
    fn_usable = lax.broadcasted_iota(jnp.int32, (1, fn_rows), 1) < fn_count
    loads[1].wait()
    normed, _ = layer_norm(functions_v[...].astype(F32).T)
    hidden = (normed * branch_gain + branch_bias).astype(BF16)
    fn_hidden[...] = hidden
    keyval = dot(kv.T, hidden)
    keys = jnp.where(fn_usable, keyval[:D], far_below)
    fn_values[...] = keyval[D:].astype(BF16)
    fn_max = jnp.max(keys, axis=1, keepdims=True)
    powers = jnp.where(fn_usable, jnp.exp(keys - fn_max), 0.0)
    fn_powers[...] = powers
    fn_low[...] = powers.astype(BF16)
    fn_scale = 1.0 / over_points(powers)
    fn_summary = diagonal_blocks(dot_points(fn_low[...], fn_values[...]) * fn_scale)
    weighted_summary = fn_weight * folded(fn_summary)
    sent[0, 0:HEAD_DIM, :] = weighted_summary
    sent[0, HEAD_DIM : HEAD_DIM + 8, :] = jnp.full((8, D), fn_weight, F32)
    pl.semaphore_wait(barrier, sum(level.size - 1 for level in greeted))
    exchange(0).start()

    loads[2].wait()

    def shared_rows(start, stride=1):
        return shared_v[pl.ds(start, D, stride=stride), :].astype(BF16)

    query_w = shared_rows(ROW_QUERY)
    cross_w = shared_rows(ROW_CROSS_OUT)
    self_w = shared_rows(ROW_SELF_OUT)
    qkv_w = jnp.concatenate([shared_rows(ROW_QKV + third, 3) for third in range(3)], axis=1)

    expert_at = lax.broadcasted_iota(jnp.int32, (8, D), 0)
    router_mask = lax.broadcasted_iota(jnp.int32, (8, D), 1) % EXPERTS == expert_at
    router_t = jnp.zeros((8, D), F32)
    pickers = []
    for r in range(EXPERTS):
        picker = jnp.where(column_at == r * (D // EXPERTS) + row_at // EXPERTS, 1.0, 0.0).astype(BF16)
        pickers.append(picker)
        router_row = shared_v[ROW_ROUTER + r : ROW_ROUTER + r + 1, :]
        router_t = router_t + dot(jnp.where(router_mask, router_row, 0.0).astype(BF16), picker)
    router_t = router_t.astype(BF16)

    def shared_column(row):
        return to_column(shared_v[row : row + 1, :])

    gain_one, bias_one = shared_column(ROW_GAIN_ONE), shared_column(ROW_BIAS_ONE)
    gain_two, bias_two = shared_column(ROW_GAIN_TWO), shared_column(ROW_BIAS_TWO)
    gain_three, bias_three = shared_column(ROW_GAIN_THREE), shared_column(ROW_BIAS_THREE)

    loads[3].wait()
    points = points_v[...].astype(F32).T
    normed_one, inverse_one = layer_norm(points)
    hidden_one = (normed_one * gain_one + bias_one).astype(BF16)
    cross_soft = feature_softmax(dot(query_w.T, hidden_one))
    cross_low = cross_soft.astype(BF16)

    exchange(0).wait_recv()
    weight_total = fn_weight + got[0, HEAD_DIM : HEAD_DIM + 1, :]
    fn_share = fn_weight / weight_total
    mixed = unfolded((weighted_summary + got[0, 0:HEAD_DIM, :]) / weight_total)
    mixed_low = mixed.astype(BF16)
    cross_out = dot(mixed.T.astype(BF16), cross_low).astype(BF16)
    after_cross = points + dot(cross_w.T, cross_out)
    normed_two, inverse_two = layer_norm(after_cross)
    hidden_two = (normed_two * gain_two + bias_two).astype(BF16)
    qkv = dot(qkv_w.T, hidden_two)
    usable = lax.broadcasted_iota(jnp.int32, (1, rows), 1) + fn * rows < item_counts[0]
    keys = jnp.where(usable, qkv[D : 2 * D], far_below)
    self_values = qkv[2 * D :].astype(BF16)
    key_max = jnp.max(keys, axis=1, keepdims=True)
    key_powers = jnp.where(usable, jnp.exp(keys - key_max), 0.0)
    key_low = key_powers.astype(BF16)
    own_total = over_points(key_powers)
    key_sum = dot_points(key_low, self_values)
    sent[1, 0:HEAD_DIM, :] = folded(key_sum)
    sent[1, HEAD_DIM : HEAD_DIM + 8, :] = jnp.concatenate(
        [to_row(key_max), to_row(own_total), jnp.zeros((6, D), F32)], axis=0
    )
    exchange(1).start()

    self_soft = feature_softmax(qkv[:D])
    self_weights = self_soft.astype(BF16)
    loads[4].wait()
    logits = dot_points(router_t, geometry_v[...])[:EXPERTS]
    powers = jnp.exp(logits - jnp.max(logits, axis=0, keepdims=True))
    gates = powers * (1.0 / jnp.sum(powers, axis=0, keepdims=True))
    half_gates = 0.5 * gates
    loads[5].wait()
    arriving = cotangent_v[...].astype(F32).T
    arriving_low = arriving.astype(BF16)

    exchange(1).wait_recv()
    other_max = to_column(got[1, HEAD_DIM : HEAD_DIM + 1, :])
    other_total = to_column(got[1, HEAD_DIM + 1 : HEAD_DIM + 2, :])
    joint_max = jnp.maximum(key_max, other_max)
    own_factor, other_factor = jnp.exp(key_max - joint_max), jnp.exp(other_max - joint_max)
    joint_scale = 1.0 / (own_total * own_factor + other_total * other_factor)
    own_factor, other_factor = own_factor * joint_scale, other_factor * joint_scale
    self_summary = diagonal_blocks(key_sum) * own_factor + unfolded(got[1, 0:HEAD_DIM, :]) * other_factor
    self_low = self_summary.astype(BF16)

    self_out = dot(self_summary.T.astype(BF16), self_weights).astype(BF16)
    after_self = after_cross + dot(self_w.T, self_out)
    normed_three, inverse_three = layer_norm(after_self)
    hidden_three = (normed_three * gain_three + bias_three).astype(BF16)

    result, upstream, gate_grads = after_self, None, []
    for number in range(EXPERTS):
        up = jnp.concatenate([shared_rows(ROW_UP + number * FF + half, 2) for half in range(2)], axis=1)
        down = jnp.concatenate(
            [shared_rows(ROW_DOWN + number * FF + half * D) for half in range(2)], axis=0
        )
        gate = half_gates[number : number + 1]
        argument = dot(up.T, hidden_three)
        back = dot(down, arriving_low)
        scaled = argument * math.sqrt(0.5)
        twice_cdf = 1.0 + lax.erf(scaled)
        bell = jnp.exp2(scaled * scaled * -math.log2(math.e)) * (2.0 / math.sqrt(math.pi))
        active = argument * twice_cdf
        gate_grads.append(0.5 * jnp.sum(active * back, axis=0, keepdims=True))
        hidden_v[...] = (active * gate).astype(BF16)
        pre_v[...] = (back * gate * (twice_cdf + scaled * bell)).astype(BF16)
        result = result + dot(down.T, hidden_v[...])
        part = dot(up, pre_v[...])
        upstream = part if upstream is None else upstream + part
        sums = experts[number]
        up_sum = dot_points(hidden_three, pre_v[...])
        sums.source[0:D, :] = up_sum[:, :D].astype(BF16)
        sums.source[D : 2 * D, :] = up_sum[:, D:].astype(BF16)
        sums.source[FF:, :] = dot_points(hidden_v[...], arriving_low).astype(BF16)
        sums.begin()
        for earlier in experts[:number]:
            earlier.advance()
    output[...] = result.T.astype(BF16)

    gate_grads = jnp.concatenate(gate_grads, axis=0)
    g_logits = gates * (gate_grads - jnp.sum(gates * gate_grads, axis=0, keepdims=True))
    g_logits = jnp.concatenate([g_logits, jnp.zeros_like(g_logits)], axis=0).astype(BF16)
    router_sum = dot(g_logits, geometry_v[...])
    small = [None] * 6
    small[4] = to_row(over_points(upstream * normed_three))
    small[5] = to_row(over_points(upstream))
    g_after_self = arriving + norm_back(normed_three, inverse_three, gain_three, upstream)
    g_proj = g_after_self.astype(BF16)
    g_self_out = dot(self_w, g_proj).astype(BF16)
    own_grad = folded(dot_points(self_weights, g_self_out))
    sent[2, 0:HEAD_DIM, :] = own_grad
    exchange(2).start()
    for earlier in experts:
        earlier.advance()
    last.source[D : 2 * D, :] = dot_points(self_out, g_proj).astype(BF16)
    g_queries = feature_softmax_back(self_soft, dot(self_low, g_self_out)).astype(BF16)

    exchange(2).wait_recv()
    scaled_grad = unfolded(own_grad + got[2, 0:HEAD_DIM, :]) * own_factor
    correction = over_points(scaled_grad * self_summary)
    g_keys = key_powers * (dot(scaled_grad.astype(BF16), self_values) - correction)
    g_values = dot(scaled_grad.T.astype(BF16), key_low)
    g_qkv = jnp.concatenate([g_queries, g_keys.astype(BF16), g_values.astype(BF16)], axis=0)
    upstream = dot(qkv_w, g_qkv)
    small[2] = to_row(over_points(upstream * normed_two))
    small[3] = to_row(over_points(upstream))
    g_after_cross = g_after_self + norm_back(normed_two, inverse_two, gain_two, upstream)
    g_proj = g_after_cross.astype(BF16)
    g_cross_out = dot(cross_w, g_proj).astype(BF16)
    own_mixed = folded(dot_points(cross_low, g_cross_out))
    sent[3, 0:HEAD_DIM, :] = own_mixed
    exchange(3).start()
    qkv_sum = dot_points(hidden_two, g_qkv)
    for third in range(3):
        middle.source[third * D : (third + 1) * D, :] = qkv_sum[:, third * D : (third + 1) * D].astype(BF16)
    middle.source[3 * D :, :] = dot_points(cross_out, g_proj).astype(BF16)
    middle.begin()
    for earlier in experts:
        earlier.advance()

    g_query = feature_softmax_back(cross_soft, dot(mixed_low, g_cross_out)).astype(BF16)
    upstream = dot(query_w, g_query)
    small[0] = to_row(over_points(upstream * normed_one))
    small[1] = to_row(over_points(upstream))
    total = g_after_cross + norm_back(normed_one, inverse_one, gain_one, upstream)
    input_grad[...] = total.T.astype(BF16)
    last.source[0:D, :] = dot_points(hidden_one, g_query).astype(BF16)
    for earlier in [middle, *experts]:
        earlier.advance()

    exchange(3).wait_recv()
    fn_grad = unfolded((own_mixed + got[3, 0:HEAD_DIM, :]) * fn_share)
    fn_scaled = fn_grad * fn_scale
    fn_correction = over_points(fn_scaled * fn_summary)
    g_keys = fn_powers[...] * (dot(fn_scaled.astype(BF16), fn_values[...]) - fn_correction)
    g_values = dot(fn_scaled.T.astype(BF16), fn_low[...])
    g_keyval = jnp.concatenate([g_keys, g_values], axis=0).astype(BF16)
    kv_sum = dot_points(fn_hidden[...], g_keyval)
    for half in range(2):
        branch.source[half * D : (half + 1) * D, :] = kv_sum[:, half * D : (half + 1) * D].astype(BF16)
    branch.begin()
    upstream = dot(kv, g_keyval)
    normed, _ = layer_norm(functions_v[...].astype(F32).T)
    own_norm = [to_row(over_points(upstream * normed)), to_row(over_points(upstream))]
    branch_norms = [jnp.where(fn == number, row, 0.0) for number in range(fns) for row in own_norm]
    filled = 8 + len(small) + len(branch_norms)
    last.source[2 * D :, :] = jnp.concatenate(
        [router_sum, *small, *branch_norms, jnp.zeros((32 - filled, D), F32)], axis=0
    ).astype(BF16)
    last.begin()

    waiting = [branch, last, middle, *experts]
    while any(reduction.steps_left for reduction in waiting):
        for reduction in waiting:
            reduction.advance()

    for number, sums in enumerate(experts):
        for half in range(2):
            shared_out[pl.ds(ROW_UP + number * FF + half, D, stride=2), :] = sums.total[
                half * D : (half + 1) * D, :
            ].astype(F32)
        start = ROW_DOWN + number * FF
        shared_out[start : start + FF, :] = sums.total[FF:, :].astype(F32)
    for third in range(3):
        shared_out[pl.ds(ROW_QKV + third, D, stride=3), :] = middle.total[
            third * D : (third + 1) * D, :
        ].astype(F32)
    shared_out[ROW_CROSS_OUT : ROW_CROSS_OUT + D, :] = middle.total[3 * D :, :].astype(F32)
    shared_out[ROW_QUERY : ROW_QUERY + D, :] = last.total[0:D, :].astype(F32)
    shared_out[ROW_SELF_OUT : ROW_SELF_OUT + D, :] = last.total[D : 2 * D, :].astype(F32)
    rest = last.total[2 * D :, :].astype(F32)
    for at, row in enumerate(
        [ROW_GAIN_ONE, ROW_BIAS_ONE, ROW_GAIN_TWO, ROW_BIAS_TWO, ROW_GAIN_THREE, ROW_BIAS_THREE]
    ):
        shared_out[row : row + 1, :] = rest[8 + at : 9 + at]
    router_low = rest[:8].astype(BF16)
    for r in range(EXPERTS):
        spread = dot_points(router_low, pickers[r])
        shared_out[ROW_ROUTER + r : ROW_ROUTER + r + 1, :] = jnp.sum(
            jnp.where(router_mask, spread, 0.0), axis=0, keepdims=True
        )
    for half in range(2):
        branch_rows[pl.ds(2 + half, D, stride=2), :] = branch.total[
            half * D : (half + 1) * D, :
        ].astype(F32)
    own_norm = rest[14:16]
    for number in range(1, fns):
        own_norm = jnp.where(fn == number, rest[14 + 2 * number : 16 + 2 * number], own_norm)
    branch_rows[0:2, :] = own_norm
    for r in range(BRANCH_ROWS):
        branch_out[0:1, r * D : (r + 1) * D] = branch_rows[r : r + 1, :]

    for at in range(4):
        exchange(at).wait_send()
    for reduction in reductions:
        reduction.drain()


def whole_step(fns, pts, points, geometry, functions, presence, fn_counts, item_counts, cotangent, shared, branch):
    rows, fn_rows = points.shape[0], functions.shape[0]
    smem = pl.BlockSpec(memory_space=pltpu.SMEM)
    vmem = pl.BlockSpec(memory_space=pltpu.VMEM)
    anywhere = pl.BlockSpec(memory_space=pl.ANY)
    arrays = (points, geometry, functions, cotangent, shared, branch)

    def low(*shape):
        return pltpu.VMEM(shape, BF16)

    def wide(*shape):
        return pltpu.VMEM(shape, F32)

    scratch = [low(rows, D), low(rows, D), low(fn_rows, D), low(rows, D)]
    scratch += [wide(SHARED_ROWS, D), wide(1, BRANCH_ROWS * D), wide(BRANCH_ROWS, D)]
    scratch += [wide(D, fn_rows), low(D, fn_rows), low(D, fn_rows), low(D, fn_rows), low(FF, rows), low(FF, rows)]
    scratch += [wide(4, HEAD_DIM + 8, D), wide(4, HEAD_DIM + 8, D)]
    scratch += [pltpu.SemaphoreType.DMA((6,)), pltpu.SemaphoreType.DMA((4,)), pltpu.SemaphoreType.DMA((4,))]
    for reduction in plan(fns, pts):
        scratch += reduction.scratch()
    return pl.pallas_call(
        functools.partial(step_kernel, fns, pts),
        out_shape=[low(rows, D), low(rows, D), wide(SHARED_ROWS, D), wide(1, BRANCH_ROWS * D)],
        in_specs=[smem] * 3 + [anywhere] * 6,
        out_specs=[vmem] * 4,
        scratch_shapes=scratch,
        compiler_params=pltpu.CompilerParams(
            collective_id=0, has_side_effects=True, vmem_limit_bytes=36 << 20
        ),
    )(presence, fn_counts, item_counts, *(pltpu.with_memory_space_constraint(value, pltpu.HBM) for value in arrays))


def sgd_update(weights, momentum, average, gradient, step_rate):
    momentum_new = momentum_decay * momentum + gradient
    weights_new = weights - step_rate * (gradient + momentum_decay * momentum_new)
    average_new = average_decay * average + (1.0 - average_decay) * weights_new
    return (weights_new, momentum_new, average_new, weights_new.astype(BF16))


UPDATE_ROWS = 480


def update_kernel(shared_rate, branch_rate, *refs):
    output, input_grad, shared_grad, branch_grad = refs[:4]
    shared_old, branch_old = refs[4:7], refs[7:10]
    output_hbm, input_grad_hbm = refs[10:12]
    shared_new, branch_new, norms_hbm = refs[12:16], refs[16:20], refs[20]
    shared_v, branch_v, norms_v, sems = refs[21:25], refs[25:29], refs[29], refs[30]
    copies = []

    def store(source, target):
        copies.append(pltpu.make_async_copy(source, target, sems.at[len(copies)]))
        copies[-1].start()

    store(output, output_hbm)
    store(input_grad, input_grad_hbm)
    for start in range(0, SHARED_ROWS, UPDATE_ROWS):
        part = slice(start, min(start + UPDATE_ROWS, SHARED_ROWS))
        new = sgd_update(*(ref[part, :] for ref in shared_old), shared_grad[part, :], shared_rate)
        for value, held, target in zip(new, shared_v, shared_new):
            held[part, :] = value
            store(held.at[part, :], target.at[part, :])
    new = sgd_update(*(ref[...] for ref in branch_old), branch_grad[...], branch_rate)
    for value, held, target in zip(new, branch_v, branch_new):
        held[...] = value
        store(held, target)
    norms_v[...] = jnp.concatenate(
        [shared_grad[row : row + 2, :] for row in (ROW_GAIN_ONE, ROW_GAIN_TWO, ROW_GAIN_THREE)], axis=0
    )
    store(norms_v, norms_hbm)
    for copy in copies:
        copy.wait()


def update(shared_rate, branch_rate, output, input_grad, shared_grad, branch_grad, shared_old, branch_old):
    vmem = pl.BlockSpec(memory_space=pltpu.VMEM)
    kinds = [F32, F32, F32, BF16]
    branch_shape = branch_old[0].shape
    outs = [jax.ShapeDtypeStruct(value.shape, BF16) for value in (output, input_grad)]
    outs += [jax.ShapeDtypeStruct((SHARED_ROWS, D), kind) for kind in kinds]
    outs += [jax.ShapeDtypeStruct(branch_shape, kind) for kind in kinds]
    outs += [jax.ShapeDtypeStruct((6, D), F32)]
    parts = -(-SHARED_ROWS // UPDATE_ROWS)
    return pl.pallas_call(
        functools.partial(update_kernel, shared_rate, branch_rate),
        out_shape=outs,
        in_specs=[vmem] * 10,
        out_specs=[pl.BlockSpec(memory_space=pl.ANY)] * len(outs),
        scratch_shapes=[pltpu.VMEM((SHARED_ROWS, D), kind) for kind in kinds]
        + [pltpu.VMEM(branch_shape, kind) for kind in kinds]
        + [pltpu.VMEM((6, D), F32), pltpu.SemaphoreType.DMA((4 * parts + 7,))],
        compiler_params=pltpu.CompilerParams(vmem_limit_bytes=16 << 20),
    )(output, input_grad, shared_grad, branch_grad, *shared_old, *branch_old)


def local(
    fns,
    pts,
    points_in,
    geometry,
    functions,
    presence,
    fn_counts,
    item_counts,
    cotangent,
    shared_weights,
    shared_momentum,
    shared_average,
    branch_weights,
    branch_momentum,
    branch_average,
):
    rows, fn_rows = points_in.shape[1], functions.shape[2]
    shared_old = [value.reshape(SHARED_ROWS, D) for value in (shared_weights, shared_momentum, shared_average)]
    branch_old = [branch_weights, branch_momentum, branch_average]
    step = whole_step(
        fns,
        pts,
        points_in.reshape(rows, D),
        geometry.reshape(rows, D),
        functions.reshape(fn_rows, D),
        presence,
        fn_counts,
        item_counts,
        cotangent.reshape(rows, D),
        shared_old[0],
        branch_weights,
    )
    shared_rate = 0.1 / math.sqrt(pts * rows * fns)
    branch_rate = 0.1 / math.sqrt(pts * fn_rows)
    new = update(shared_rate, branch_rate, *step, shared_old, branch_old)
    return (
        new[0].reshape(1, rows, D),
        new[1].reshape(1, rows, D),
        *(value.reshape(-1) for value in new[2:6]),
        *new[6:10],
        new[10],
    )


def solution(mesh):
    split = P("pts", "fn", None)
    return jax.shard_map(
        functools.partial(local, mesh.shape["fn"], mesh.shape["pts"]),
        mesh=mesh,
        in_specs=(
            split,
            split,
            P("fn", "pts", None, None),
            P("fn", "pts"),
            P("fn", "pts"),
            P("pts"),
            split,
            P(),
            P(),
            P(),
            P("fn", None),
            P("fn", None),
            P("fn", None),
        ),
        out_specs=(
            split,
            split,
            P(),
            P(),
            P(),
            P(),
            P("fn", None),
            P("fn", None),
            P("fn", None),
            P("fn", None),
            P(),
        ),
        check_vma=False,
    )
```

```python
import functools
import math

import jax
import jax.numpy as jnp
from jax import lax
from jax.experimental import pallas as pl
from jax.experimental.pallas import tpu as pltpu
from jax.sharding import PartitionSpec as P

D = 128
HEADS = 8
FF = 256
EXPERTS = 4
HEAD_DIM = 16
HIDDEN = EXPERTS * FF

epsilon = 1e-05
far_below = -1e30
momentum_decay = 0.9
average_decay = 0.95

F32 = jnp.float32
BF16 = jnp.bfloat16
MESH = pl.DeviceIdType.MESH

ROW_GAIN_ONE, ROW_BIAS_ONE = 0, 1
ROW_QUERY = 2
ROW_CROSS_OUT = ROW_QUERY + D
ROW_GAIN_TWO = ROW_CROSS_OUT + D
ROW_BIAS_TWO = ROW_GAIN_TWO + 1
ROW_QKV = ROW_BIAS_TWO + 1
ROW_SELF_OUT = ROW_QKV + 3 * D
ROW_GAIN_THREE = ROW_SELF_OUT + D
ROW_BIAS_THREE = ROW_GAIN_THREE + 1
ROW_ROUTER = ROW_BIAS_THREE + 1
ROW_UP = ROW_ROUTER + EXPERTS
ROW_DOWN = ROW_UP + 2 * D * EXPERTS
SHARED_ROWS = ROW_DOWN + HIDDEN
BRANCH_ROWS = 2 + 2 * D

EXPERT_ROWS = 2 * FF
MIDDLE_ROWS = 4 * D
LAST_ROWS = 2 * D + 32
BRANCH_SENT = 2 * D

EARLY_BACK = 2
VMEM_LIMIT = 46


def dot(a, b):
    return jnp.dot(a, b, preferred_element_type=F32)


def dot_points(a, b):
    return lax.dot_general(a, b, (((1,), (1,)), ((), ())), preferred_element_type=F32)


class Level:
    def __init__(self, size, index, member):
        self.size, self.index, self.member = size, index, member


def split_rows(rows, size):
    step = 16
    while rows % step or rows // step > size:
        step += 16
    return step, rows // step


class Reduction:
    def __init__(self, sizes, rows):
        self.sizes, self.rows = sizes, rows
        self.steps, self.owners = [], []
        for size in sizes:
            step, owners = split_rows(rows, size)
            self.steps.append(step)
            self.owners.append(owners)
            rows = step

    def scratch(self):
        shapes = [pltpu.VMEM((self.rows, D), BF16), pltpu.VMEM((self.rows, D), BF16)]
        for at, size in enumerate(self.sizes):
            shapes.append(pltpu.VMEM(((size - 1) * self.steps[at], D), BF16))
            shapes.append(pltpu.VMEM((self.steps[at], D), BF16))
            shapes.append(pltpu.SemaphoreType.DMA((4,)))
        return shapes

    def bind(self, refs, levels):
        self.source, self.total = refs[0], refs[1]
        self.parts = [refs[2 + 3 * at : 5 + 3 * at] for at in range(len(self.sizes))]
        self.levels = levels
        last = len(self.sizes) - 1
        self.steps_left = []
        for at in range(last):
            self.steps_left.append(lambda at=at: (self.add(at), self.scatter(at + 1)))
        self.steps_left.append(lambda: (self.add(last), self.gather(last)))
        for at in range(last, 0, -1):
            self.steps_left.append(lambda at=at: (self.collect(at), self.gather(at - 1)))
        self.steps_left.append(lambda: self.collect(0))

    def begin(self):
        self.scatter(0)

    def advance(self):
        if self.steps_left:
            self.steps_left.pop(0)()

    def base(self, at):
        start = 0
        for upper in range(at):
            start = start + self.levels[upper].index * self.steps[upper]
        return start

    def inside(self, at):
        condition = None
        for upper in range(at):
            if self.owners[upper] < self.sizes[upper]:
                here = self.levels[upper].index < self.owners[upper]
                condition = here if condition is None else jnp.logical_and(condition, here)
        return condition

    def when(self, condition, body):
        if condition is None:
            body()
        else:
            pl.when(condition)(body)

    def split(self, at, owner, other):
        def go():
            if self.owners[at] == self.sizes[at]:
                owner()
            else:
                here = self.levels[at].index < self.owners[at]
                pl.when(here)(owner)
                if other is not None:
                    pl.when(jnp.logical_not(here))(other)

        self.when(self.inside(at), go)

    def rows_from(self, at):
        return self.source if at == 0 else self.parts[at - 1][1]

    def wait(self, at, sem, rows, sending):
        window = self.source if rows <= self.rows else self.parts[at][0]
        copy = pltpu.make_async_remote_copy(
            src_ref=window.at[pl.ds(0, rows), :],
            dst_ref=window.at[pl.ds(0, rows), :],
            send_sem=self.parts[at][2].at[sem],
            recv_sem=self.parts[at][2].at[sem],
            device_id=self.levels[at].member(self.levels[at].index),
            device_id_type=MESH,
        )
        (copy.wait_send if sending else copy.wait_recv)()

    def scatter(self, at):
        level, step, owners = self.levels[at], self.steps[at], self.owners[at]
        received, _, sems = self.parts[at]

        def go():
            def one(k, carry):
                peer = (level.index + k) % level.size

                def start():
                    pltpu.make_async_remote_copy(
                        src_ref=self.rows_from(at).at[pl.ds(pl.multiple_of(peer * step, 16), step), :],
                        dst_ref=received.at[pl.ds(pl.multiple_of((k - 1) * step, 16), step), :],
                        send_sem=sems.at[0],
                        recv_sem=sems.at[1],
                        device_id=level.member(peer),
                        device_id_type=MESH,
                    ).start()

                self.when(None if owners == level.size else peer < owners, start)
                return carry

            lax.fori_loop(1, level.size, one, 0)

        self.when(self.inside(at), go)

    def add(self, at):
        level, step = self.levels[at], self.steps[at]

        def go():
            received, kept, _ = self.parts[at]
            self.wait(at, 1, (level.size - 1) * step, False)
            start = pl.multiple_of(level.index * step, 16)
            total = self.rows_from(at)[pl.ds(start, step), :].astype(F32)
            for k in range(level.size - 1):
                total = total + received[k * step : (k + 1) * step, :].astype(F32)
            if at + 1 < len(self.sizes):
                kept[...] = total.astype(BF16)
            else:
                self.total[pl.ds(pl.multiple_of(self.base(at) + start, 16), step), :] = total.astype(BF16)

        self.split(at, go, None)

    def gather(self, at):
        level, step = self.levels[at], self.steps[at]
        sems = self.parts[at][2]

        def go():
            rows = pl.ds(pl.multiple_of(self.base(at) + level.index * step, 16), step)

            def one(k, carry):
                pltpu.make_async_remote_copy(
                    src_ref=self.total.at[rows, :],
                    dst_ref=self.total.at[rows, :],
                    send_sem=sems.at[2],
                    recv_sem=sems.at[3],
                    device_id=level.member((level.index + k) % level.size),
                    device_id_type=MESH,
                ).start()
                return carry

            lax.fori_loop(1, level.size, one, 0)

        self.split(at, go, None)

    def collect(self, at):
        step, owners = self.steps[at], self.owners[at]
        self.split(
            at,
            lambda: self.wait(at, 3, (owners - 1) * step, False) if owners > 1 else None,
            lambda: self.wait(at, 3, owners * step, False),
        )

    def drain(self):
        for at, size in enumerate(self.sizes):
            step, owners = self.steps[at], self.owners[at]

            def owner():
                if owners > 1:
                    self.wait(at, 0, (owners - 1) * step, True)
                self.wait(at, 2, (size - 1) * step, True)

            self.split(at, owner, lambda: self.wait(at, 0, owners * step, True))


def inner_size(pts):
    return 2 if pts % 2 == 0 else 1


def middle_size(pts):
    outer = pts // inner_size(pts)
    return 2 if outer % 2 == 0 else 1


def plan(fns, pts):
    core, middle = inner_size(pts), middle_size(pts)
    far = pts // (core * middle)
    stepwise = [core, fns * middle, far]
    at_once = fns * pts <= 32
    return [Reduction(stepwise, EXPERT_ROWS) for _ in range(EXPERTS)] + [
        Reduction(stepwise, MIDDLE_ROWS),
        Reduction([fns * pts] if at_once else stepwise, LAST_ROWS),
        Reduction([pts] if at_once else [core * middle, far], BRANCH_SENT),
    ]


def layer_norm(values):
    centred = values - jnp.mean(values, axis=0, keepdims=True)
    spread = jnp.mean(centred * centred, axis=0, keepdims=True)
    inverse = lax.rsqrt(spread + epsilon)
    return centred * inverse, inverse


def norm_back(normed, inverse, gain, upstream):
    scaled = upstream * gain
    first = jnp.mean(scaled, axis=0, keepdims=True)
    second = jnp.mean(scaled * normed, axis=0, keepdims=True)
    return (scaled - first - normed * second) * inverse


def heads_view(values):
    return values.reshape(HEADS, HEAD_DIM, values.shape[-1])


def feature_softmax(values):
    shaped = heads_view(values)
    powers = jnp.exp(shaped - jnp.max(shaped, axis=1, keepdims=True))
    return (powers * (1.0 / jnp.sum(powers, axis=1, keepdims=True))).reshape(values.shape)


def feature_softmax_back(soft, upstream):
    shaped, incoming = heads_view(soft), heads_view(upstream)
    inner = jnp.sum(shaped * incoming, axis=1, keepdims=True)
    return (shaped * (incoming - inner)).reshape(soft.shape)


def over_points(values):
    return jnp.sum(values, axis=1, keepdims=True)


def step_kernel(fns, pts, shared_rate, branch_rate, *refs):
    refs = list(refs)

    def take(n):
        got = refs[:n]
        del refs[:n]
        return got

    presence, fn_counts, item_counts = take(3)
    points_hbm, geometry_hbm, functions_hbm, cotangent_hbm, shared_hbm, branch_hbm = take(6)
    momenta_hbm = take(4)
    output, input_grad = take(2)
    shared_new, branch_new, norms_out = take(4), take(4), take(1)[0]
    shared_v, branch_v = shared_new[0], branch_new[0]
    points_v, geometry_v, functions_v, cotangent_v, branch_rows, shared_sum, branch_sum = take(7)
    fn_powers, fn_low, fn_values, fn_hidden, hidden_v, pre_v, back_v, up_t, down_t = take(9)
    sent, got = take(2)
    local_sem, x_send, x_recv = take(3)
    reductions = plan(fns, pts)
    bound = [take(len(reduction.scratch())) for reduction in reductions]
    assert not refs

    fn, pt = lax.axis_index("fn"), lax.axis_index("pts")
    core_size, middle_size_ = inner_size(pts), middle_size(pts)
    near_size = core_size * middle_size_
    far, near = pt // near_size, pt % near_size
    middle_at, core = near // core_size, near % core_size
    far_level = Level(pts // near_size, far, lambda j: (fn, j * near_size + near))
    stepwise = [
        Level(core_size, core, lambda j: (fn, pt - core + j)),
        Level(
            fns * middle_size_,
            fn * middle_size_ + middle_at,
            lambda j: (j // middle_size_, far * near_size + j % middle_size_ * core_size + core),
        ),
        far_level,
    ]
    if fns * pts <= 32:
        everyone = [Level(fns * pts, fn * pts + pt, lambda j: (j // pts, j % pts))]
        items = [Level(pts, pt, lambda j: (fn, j))]
        greeted = everyone
    else:
        everyone = stepwise
        items = [Level(near_size, near, lambda j: (fn, far * near_size + j)), far_level]
        greeted = [
            Level(
                fns * near_size,
                fn * near_size + near,
                lambda j: (j // near_size, far * near_size + j % near_size),
            ),
            far_level,
        ]
    for at, (reduction, scratch) in enumerate(zip(reductions, bound)):
        reduction.bind(scratch, stepwise if at <= EXPERTS else everyone if at == EXPERTS + 1 else items)
    experts, middle, last, branch = reductions[:EXPERTS], *reductions[EXPERTS:]

    rows, fn_rows = points_v.shape[0], functions_v.shape[0]

    loads = []
    for at, (source, target) in enumerate(
        [
            (branch_hbm, branch_v),
            (functions_hbm, functions_v),
            (shared_hbm, shared_v),
            (points_hbm, points_v),
            (geometry_hbm, geometry_v),
            (cotangent_hbm, cotangent_v),
            *zip(momenta_hbm, [*shared_new[1:3], *branch_new[1:3]]),
        ]
    ):
        loads.append(pltpu.make_async_copy(source, target, local_sem.at[at]))
        loads[-1].start()

    barrier = pltpu.get_barrier_semaphore()
    for level in greeted:

        def greet(k, carry, level=level):
            pl.semaphore_signal(
                barrier,
                inc=1,
                device_id=level.member((level.index + k) % level.size),
                device_id_type=MESH,
            )
            return carry

        lax.fori_loop(1, level.size, greet, 0)

    def exchange(at):
        return pltpu.make_async_remote_copy(
            src_ref=sent.at[at],
            dst_ref=got.at[at],
            send_sem=x_send.at[at],
            recv_sem=x_recv.at[at],
            device_id=((fn + 1) % fns, pt),
            device_id_type=MESH,
        )

    row_at = lax.broadcasted_iota(jnp.int32, (D, D), 0)
    column_at = lax.broadcasted_iota(jnp.int32, (D, D), 1)
    same_head = row_at // HEAD_DIM == column_at // HEAD_DIM
    diagonal = row_at == column_at

    def diagonal_blocks(full):
        return jnp.where(same_head, full, 0.0)

    def folded(full):
        kept = diagonal_blocks(full)
        out = kept[:HEAD_DIM]
        for head in range(1, HEADS):
            out = out + kept[head * HEAD_DIM : (head + 1) * HEAD_DIM]
        return out

    def unfolded(compact):
        return diagonal_blocks(jnp.concatenate([compact] * HEADS, axis=0))

    def to_row(column):
        return jnp.sum(jnp.where(diagonal, column, 0.0), axis=0, keepdims=True)

    def to_column(row):
        return jnp.sum(jnp.where(diagonal, row, 0.0), axis=1, keepdims=True)

    loads[0].wait()
    for r in range(BRANCH_ROWS):
        branch_rows[r : r + 1, :] = branch_v[0:1, r * D : (r + 1) * D]
    kv = jnp.concatenate(
        [branch_rows[pl.ds(2, D, stride=2), :], branch_rows[pl.ds(3, D, stride=2), :]], axis=1
    ).astype(BF16)
    branch_gain = to_column(branch_rows[0:1, :])
    branch_bias = to_column(branch_rows[1:2, :])
    fn_count = fn_counts[0, 0]
    fn_weight = (presence[0, 0] * fn_count).astype(F32)
    fn_usable = lax.broadcasted_iota(jnp.int32, (1, fn_rows), 1) < fn_count
    loads[1].wait()
    normed, _ = layer_norm(functions_v[...].astype(F32).T)
    hidden = (normed * branch_gain + branch_bias).astype(BF16)
    fn_hidden[...] = hidden
    keyval = dot(kv.T, hidden)
    keys = jnp.where(fn_usable, keyval[:D], far_below)
    fn_values[...] = keyval[D:].astype(BF16)
    fn_max = jnp.max(keys, axis=1, keepdims=True)
    powers = jnp.where(fn_usable, jnp.exp(keys - fn_max), 0.0)
    fn_powers[...] = powers
    fn_low[...] = powers.astype(BF16)
    fn_scale = 1.0 / over_points(powers)
    fn_summary = diagonal_blocks(dot_points(fn_low[...], fn_values[...]) * fn_scale)
    weighted_summary = fn_weight * folded(fn_summary)
    sent[0, 0:HEAD_DIM, :] = weighted_summary
    sent[0, HEAD_DIM : HEAD_DIM + 8, :] = jnp.full((8, D), fn_weight, F32)
    pl.semaphore_wait(barrier, sum(level.size - 1 for level in greeted))
    exchange(0).start()

    loads[2].wait()

    def shared_rows(start, stride=1):
        return shared_v[pl.ds(start, D, stride=stride), :].astype(BF16)

    query_w = shared_rows(ROW_QUERY)
    cross_w = shared_rows(ROW_CROSS_OUT)
    self_w = shared_rows(ROW_SELF_OUT)
    qkv_w = jnp.concatenate([shared_rows(ROW_QKV + third, 3) for third in range(3)], axis=1)

    for piece_at in range(2 * EXPERTS):
        number, half = piece_at // 2, piece_at % 2
        up_t[piece_at * D : (piece_at + 1) * D, :] = shared_rows(ROW_UP + number * FF + half, 2).T
        down_t[:, piece_at * D : (piece_at + 1) * D] = shared_rows(ROW_DOWN + piece_at * D).T

    expert_at = lax.broadcasted_iota(jnp.int32, (8, D), 0)
    router_mask = lax.broadcasted_iota(jnp.int32, (8, D), 1) % EXPERTS == expert_at
    router_t = jnp.zeros((8, D), F32)
    pickers = []
    for r in range(EXPERTS):
        picker = jnp.where(column_at == r * (D // EXPERTS) + row_at // EXPERTS, 1.0, 0.0).astype(BF16)
        pickers.append(picker)
        router_row = shared_v[ROW_ROUTER + r : ROW_ROUTER + r + 1, :]
        router_t = router_t + dot(jnp.where(router_mask, router_row, 0.0).astype(BF16), picker)
    router_t = router_t.astype(BF16)

    def shared_column(row):
        return to_column(shared_v[row : row + 1, :])

    gain_one, bias_one = shared_column(ROW_GAIN_ONE), shared_column(ROW_BIAS_ONE)
    gain_two, bias_two = shared_column(ROW_GAIN_TWO), shared_column(ROW_BIAS_TWO)
    gain_three, bias_three = shared_column(ROW_GAIN_THREE), shared_column(ROW_BIAS_THREE)

    loads[3].wait()
    points = points_v[...].astype(F32).T
    normed_one, inverse_one = layer_norm(points)
    hidden_one = (normed_one * gain_one + bias_one).astype(BF16)
    cross_soft = feature_softmax(dot(query_w.T, hidden_one))
    cross_low = cross_soft.astype(BF16)

    exchange(0).wait_recv()
    weight_total = fn_weight + got[0, HEAD_DIM : HEAD_DIM + 1, :]
    fn_share = fn_weight / weight_total
    mixed = unfolded((weighted_summary + got[0, 0:HEAD_DIM, :]) / weight_total)
    mixed_low = mixed.astype(BF16)
    cross_out = dot(mixed.T.astype(BF16), cross_low).astype(BF16)
    after_cross = points + dot(cross_w.T, cross_out)
    normed_two, inverse_two = layer_norm(after_cross)
    hidden_two = (normed_two * gain_two + bias_two).astype(BF16)
    qkv = dot(qkv_w.T, hidden_two)
    usable = lax.broadcasted_iota(jnp.int32, (1, rows), 1) + fn * rows < item_counts[0]
    keys = jnp.where(usable, qkv[D : 2 * D], far_below)
    self_values = qkv[2 * D :].astype(BF16)
    key_max = jnp.max(keys, axis=1, keepdims=True)
    key_powers = jnp.where(usable, jnp.exp(keys - key_max), 0.0)
    key_low = key_powers.astype(BF16)
    own_total = over_points(key_powers)
    key_sum = dot_points(key_low, self_values)
    sent[1, 0:HEAD_DIM, :] = folded(key_sum)
    sent[1, HEAD_DIM : HEAD_DIM + 8, :] = jnp.concatenate(
        [to_row(key_max), to_row(own_total), jnp.zeros((6, D), F32)], axis=0
    )
    exchange(1).start()

    self_soft = feature_softmax(qkv[:D])
    self_weights = self_soft.astype(BF16)
    loads[4].wait()
    logits = dot_points(router_t, geometry_v[...])[:EXPERTS]
    powers = jnp.exp(logits - jnp.max(logits, axis=0, keepdims=True))
    gates = powers * (1.0 / jnp.sum(powers, axis=0, keepdims=True))
    half_gates = 0.5 * gates
    loads[5].wait()
    arriving = cotangent_v[...].astype(F32).T
    arriving_low = arriving.astype(BF16)
    for number in range(EARLY_BACK):
        down = shared_v[ROW_DOWN + number * FF : ROW_DOWN + (number + 1) * FF, :].astype(BF16)
        back_v[number * FF : (number + 1) * FF, :] = dot(down, arriving_low)

    exchange(1).wait_recv()
    other_max = to_column(got[1, HEAD_DIM : HEAD_DIM + 1, :])
    other_total = to_column(got[1, HEAD_DIM + 1 : HEAD_DIM + 2, :])
    joint_max = jnp.maximum(key_max, other_max)
    own_factor, other_factor = jnp.exp(key_max - joint_max), jnp.exp(other_max - joint_max)
    joint_scale = 1.0 / (own_total * own_factor + other_total * other_factor)
    own_factor, other_factor = own_factor * joint_scale, other_factor * joint_scale
    self_summary = diagonal_blocks(key_sum) * own_factor + unfolded(got[1, 0:HEAD_DIM, :]) * other_factor
    self_low = self_summary.astype(BF16)

    self_out = dot(self_summary.T.astype(BF16), self_weights).astype(BF16)
    after_self = after_cross + dot(self_w.T, self_out)
    normed_three, inverse_three = layer_norm(after_self)
    hidden_three = (normed_three * gain_three + bias_three).astype(BF16)

    def expert_sums(number):
        part = slice(number * FF, (number + 1) * FF)
        source = experts[number].source
        up_sum = dot_points(hidden_three, pre_v[part, :])
        source[0:D, :] = up_sum[:, :D].astype(BF16)
        source[D : 2 * D, :] = up_sum[:, D:].astype(BF16)
        source[FF:, :] = dot_points(hidden_v[part, :], arriving_low).astype(BF16)
        experts[number].begin()

    def advance(*numbers):
        for number in numbers:
            reductions[number].advance()

    upstream, gate_grads = None, []
    for number in range(EXPERTS):
        part = slice(number * FF, (number + 1) * FF)
        gate = half_gates[number : number + 1]
        argument = dot(up_t[part, :], hidden_three)
        if number < EARLY_BACK:
            back = back_v[part, :]
        else:
            back = dot(shared_v[ROW_DOWN + number * FF : ROW_DOWN + (number + 1) * FF, :].astype(BF16), arriving_low)
        scaled = argument * math.sqrt(0.5)
        twice_cdf = 1.0 + lax.erf(scaled)
        bell = jnp.exp2(scaled * scaled * -math.log2(math.e)) * (2.0 / math.sqrt(math.pi))
        active = argument * twice_cdf
        gate_grads.append(0.5 * jnp.sum(active * back, axis=0, keepdims=True))
        hidden_v[part, :] = (active * gate).astype(BF16)
        pre_v[part, :] = (back * gate * (twice_cdf + scaled * bell)).astype(BF16)
        up = jnp.concatenate([shared_rows(ROW_UP + number * FF + half, 2) for half in range(2)], axis=1)
        more = dot(up, pre_v[part, :])
        upstream = more if upstream is None else upstream + more
        if number + 1 < EXPERTS:
            expert_sums(number)
            if number:
                advance(number - 1)

    gate_grads = jnp.concatenate(gate_grads, axis=0)
    g_logits = gates * (gate_grads - jnp.sum(gates * gate_grads, axis=0, keepdims=True))
    g_logits = jnp.concatenate([g_logits, jnp.zeros_like(g_logits)], axis=0).astype(BF16)
    g_after_self = arriving + norm_back(normed_three, inverse_three, gain_three, upstream)
    g_proj = g_after_self.astype(BF16)
    g_self_out = dot(self_w, g_proj).astype(BF16)
    own_grad = folded(dot_points(self_weights, g_self_out))
    sent[2, 0:HEAD_DIM, :] = own_grad
    exchange(2).start()
    expert_sums(EXPERTS - 1)
    advance(2, 0)
    router_sum = dot(g_logits, geometry_v[...])
    small = [None] * 6
    small[4] = to_row(over_points(upstream * normed_three))
    small[5] = to_row(over_points(upstream))
    last.source[D : 2 * D, :] = dot_points(self_out, g_proj).astype(BF16)
    g_queries = feature_softmax_back(self_soft, dot(self_low, g_self_out)).astype(BF16)
    advance(3, 1)

    exchange(2).wait_recv()
    scaled_grad = unfolded(own_grad + got[2, 0:HEAD_DIM, :]) * own_factor
    correction = over_points(scaled_grad * self_summary)
    g_keys = key_powers * (dot(scaled_grad.astype(BF16), self_values) - correction)
    g_values = dot(scaled_grad.T.astype(BF16), key_low)
    g_qkv = jnp.concatenate([g_queries, g_keys.astype(BF16), g_values.astype(BF16)], axis=0)
    upstream = dot(qkv_w, g_qkv)
    g_after_cross = g_after_self + norm_back(normed_two, inverse_two, gain_two, upstream)
    g_proj = g_after_cross.astype(BF16)
    g_cross_out = dot(cross_w, g_proj).astype(BF16)
    own_mixed = folded(dot_points(cross_low, g_cross_out))
    sent[3, 0:HEAD_DIM, :] = own_mixed
    exchange(3).start()
    advance(0, 2)
    qkv_sum = dot_points(hidden_two, g_qkv)
    for third in range(3):
        middle.source[third * D : (third + 1) * D, :] = qkv_sum[:, third * D : (third + 1) * D].astype(BF16)
    middle.source[3 * D :, :] = dot_points(cross_out, g_proj).astype(BF16)
    middle.begin()
    small[2] = to_row(over_points(upstream * normed_two))
    small[3] = to_row(over_points(upstream))

    g_query = feature_softmax_back(cross_soft, dot(mixed_low, g_cross_out)).astype(BF16)
    advance(1, 3)
    upstream_one = dot(query_w, g_query)
    last.source[0:D, :] = dot_points(hidden_one, g_query).astype(BF16)
    small[0] = to_row(over_points(upstream_one * normed_one))
    small[1] = to_row(over_points(upstream_one))
    advance(4)

    exchange(3).wait_recv()
    fn_grad = unfolded((own_mixed + got[3, 0:HEAD_DIM, :]) * fn_share)
    fn_scaled = fn_grad * fn_scale
    fn_correction = over_points(fn_scaled * fn_summary)
    g_keys = fn_powers[...] * (dot(fn_scaled.astype(BF16), fn_values[...]) - fn_correction)
    g_values = dot(fn_scaled.T.astype(BF16), fn_low[...])
    g_keyval = jnp.concatenate([g_keys, g_values], axis=0).astype(BF16)
    kv_sum = dot_points(fn_hidden[...], g_keyval)
    for half in range(2):
        branch.source[half * D : (half + 1) * D, :] = kv_sum[:, half * D : (half + 1) * D].astype(BF16)
    branch.begin()
    upstream = dot(kv, g_keyval)
    normed, _ = layer_norm(functions_v[...].astype(F32).T)
    own_norm = [to_row(over_points(upstream * normed)), to_row(over_points(upstream))]
    branch_norms = [jnp.where(fn == number, row, 0.0) for number in range(fns) for row in own_norm]
    filled = 8 + len(small) + len(branch_norms)
    last.source[2 * D :, :] = jnp.concatenate(
        [router_sum, *small, *branch_norms, jnp.zeros((32 - filled, D), F32)], axis=0
    ).astype(BF16)
    last.begin()

    total = g_after_cross + norm_back(normed_one, inverse_one, gain_one, upstream_one)
    input_grad[...] = total.T.astype(BF16)
    advance(0, 2, 1, 3)
    branch.advance()
    last.advance()
    result = after_self + dot(down_t[...], hidden_v[...])
    output[...] = result.T.astype(BF16)
    advance(4, 0, 1, 2, 3, 4, 0, 1, 2, 3, 4, 0, 1)

    for load in loads[6:]:
        load.wait()
    waiting = [*experts, middle, branch, last]

    def finish(reduction):
        while reduction.steps_left:
            for other in waiting:
                if other is reduction or len(other.steps_left) > 1:
                    other.advance()

    def renew(start, count):
        part = slice(start, start + count)
        new = sgd_update(*(ref[part, :] for ref in shared_new[:3]), shared_sum[part, :], shared_rate)
        for value, target in zip(new, shared_new):
            target[part, :] = value

    for number, sums in enumerate(experts):
        finish(sums)
        for half in range(2):
            shared_sum[pl.ds(ROW_UP + number * FF + half, D, stride=2), :] = sums.total[
                half * D : (half + 1) * D, :
            ].astype(F32)
        start = ROW_DOWN + number * FF
        shared_sum[start : start + FF, :] = sums.total[FF:, :].astype(F32)
    whole = -(-ROW_UP // 16) * 16
    renew(whole, SHARED_ROWS - whole)
    finish(middle)
    for third in range(3):
        shared_sum[pl.ds(ROW_QKV + third, D, stride=3), :] = middle.total[
            third * D : (third + 1) * D, :
        ].astype(F32)
    shared_sum[ROW_CROSS_OUT : ROW_CROSS_OUT + D, :] = middle.total[3 * D :, :].astype(F32)
    finish(branch)
    for half in range(2):
        branch_rows[pl.ds(2 + half, D, stride=2), :] = branch.total[
            half * D : (half + 1) * D, :
        ].astype(F32)
    for r in range(2, BRANCH_ROWS):
        branch_sum[0:1, r * D : (r + 1) * D] = branch_rows[r : r + 1, :]
    finish(last)
    shared_sum[ROW_QUERY : ROW_QUERY + D, :] = last.total[0:D, :].astype(F32)
    shared_sum[ROW_SELF_OUT : ROW_SELF_OUT + D, :] = last.total[D : 2 * D, :].astype(F32)
    rest = last.total[2 * D :, :].astype(F32)
    for at, row in enumerate(
        [ROW_GAIN_ONE, ROW_BIAS_ONE, ROW_GAIN_TWO, ROW_BIAS_TWO, ROW_GAIN_THREE, ROW_BIAS_THREE]
    ):
        shared_sum[row : row + 1, :] = rest[8 + at : 9 + at]
    norms_out[...] = rest[8:14]
    router_low = rest[:8].astype(BF16)
    for r in range(EXPERTS):
        spread = dot_points(router_low, pickers[r])
        shared_sum[ROW_ROUTER + r : ROW_ROUTER + r + 1, :] = jnp.sum(
            jnp.where(router_mask, spread, 0.0), axis=0, keepdims=True
        )
    renew(0, whole)
    own_norm = rest[14:16]
    for number in range(1, fns):
        own_norm = jnp.where(fn == number, rest[14 + 2 * number : 16 + 2 * number], own_norm)
    for r in range(2):
        branch_sum[0:1, r * D : (r + 1) * D] = own_norm[r : r + 1]
    new = sgd_update(*(ref[...] for ref in branch_new[:3]), branch_sum[...], branch_rate)
    for value, target in zip(new, branch_new):
        target[...] = value

    for at in range(4):
        exchange(at).wait_send()
    for reduction in reductions:
        reduction.drain()


def sgd_update(weights, momentum, average, gradient, step_rate):
    momentum_new = momentum_decay * momentum + gradient
    weights_new = weights - step_rate * (gradient + momentum_decay * momentum_new)
    average_new = average_decay * average + (1.0 - average_decay) * weights_new
    return (weights_new, momentum_new, average_new, weights_new.astype(BF16))


def low(*shape):
    return pltpu.VMEM(shape, BF16)


def wide(*shape):
    return pltpu.VMEM(shape, F32)


def whole_step(fns, pts, rates, counts, arrays, momenta):
    points, _, functions = arrays[:3]
    rows, fn_rows = points.shape[0], functions.shape[0]
    smem = pl.BlockSpec(memory_space=pltpu.SMEM)
    vmem = pl.BlockSpec(memory_space=pltpu.VMEM)
    anywhere = pl.BlockSpec(memory_space=pl.ANY)
    branch = (1, BRANCH_ROWS * D)

    outs = [low(rows, D), low(rows, D)]
    outs += [wide(SHARED_ROWS, D)] * 3 + [low(SHARED_ROWS, D)] + [wide(*branch)] * 3 + [low(*branch)] + [wide(6, D)]
    scratch = [low(rows, D), low(rows, D), low(fn_rows, D), low(rows, D)]
    scratch += [wide(BRANCH_ROWS, D), wide(SHARED_ROWS, D), wide(*branch)]
    scratch += [wide(D, fn_rows), low(D, fn_rows), low(D, fn_rows), low(D, fn_rows), low(HIDDEN, rows), low(HIDDEN, rows)]
    scratch += [wide(max(EARLY_BACK, 1) * FF, rows), low(HIDDEN, D), low(D, HIDDEN)]
    scratch += [wide(4, HEAD_DIM + 8, D), wide(4, HEAD_DIM + 8, D)]
    scratch += [pltpu.SemaphoreType.DMA((10,)), pltpu.SemaphoreType.DMA((4,)), pltpu.SemaphoreType.DMA((4,))]
    for reduction in plan(fns, pts):
        scratch += reduction.scratch()
    return pl.pallas_call(
        functools.partial(step_kernel, fns, pts, *rates),
        out_shape=outs,
        in_specs=[smem] * 3 + [anywhere] * (len(arrays) + len(momenta)),
        out_specs=[vmem] * len(outs),
        scratch_shapes=scratch,
        compiler_params=pltpu.CompilerParams(
            collective_id=0, has_side_effects=True, vmem_limit_bytes=VMEM_LIMIT << 20
        ),
    )(*counts, *(pltpu.with_memory_space_constraint(value, pltpu.HBM) for value in (*arrays, *momenta)))


def store_kernel(count, *refs):
    copies = [
        pltpu.make_async_copy(source, target, refs[-1].at[at])
        for at, (source, target) in enumerate(zip(refs[:count], refs[count:]))
    ]
    for copy in copies:
        copy.start()
    for copy in copies:
        copy.wait()


def stored(values):
    count = len(values)
    return pl.pallas_call(
        functools.partial(store_kernel, count),
        out_shape=[jax.ShapeDtypeStruct(value.shape, value.dtype) for value in values],
        in_specs=[pl.BlockSpec(memory_space=pltpu.VMEM)] * count,
        out_specs=[pl.BlockSpec(memory_space=pl.ANY)] * count,
        scratch_shapes=[pltpu.SemaphoreType.DMA((count,))],
        compiler_params=pltpu.CompilerParams(vmem_limit_bytes=4 << 20),
    )(*values)


def local(
    fns,
    pts,
    points_in,
    geometry,
    functions,
    presence,
    fn_counts,
    item_counts,
    cotangent,
    shared_weights,
    shared_momentum,
    shared_average,
    branch_weights,
    branch_momentum,
    branch_average,
):
    rows, fn_rows = points_in.shape[1], functions.shape[2]
    rates = (0.1 / math.sqrt(pts * rows * fns), 0.1 / math.sqrt(pts * fn_rows))
    arrays = [
        points_in.reshape(rows, D),
        geometry.reshape(rows, D),
        functions.reshape(fn_rows, D),
        cotangent.reshape(rows, D),
        shared_weights.reshape(SHARED_ROWS, D),
        branch_weights,
    ]
    momenta = [value.reshape(SHARED_ROWS, D) for value in (shared_momentum, shared_average)]
    momenta += [branch_momentum, branch_average]
    new = stored(whole_step(fns, pts, rates, (presence, fn_counts, item_counts), arrays, momenta))
    return (
        new[0].reshape(1, rows, D),
        new[1].reshape(1, rows, D),
        *(value.reshape(-1) for value in new[2:6]),
        *new[6:],
    )


def solution(mesh):
    split = P("pts", "fn", None)
    return jax.shard_map(
        functools.partial(local, mesh.shape["fn"], mesh.shape["pts"]),
        mesh=mesh,
        in_specs=(
            split,
            split,
            P("fn", "pts", None, None),
            P("fn", "pts"),
            P("fn", "pts"),
            P("pts"),
            split,
            P(),
            P(),
            P(),
            P("fn", None),
            P("fn", None),
            P("fn", None),
        ),
        out_specs=(
            split,
            split,
            P(),
            P(),
            P(),
            P(),
            P("fn", None),
            P("fn", None),
            P("fn", None),
            P("fn", None),
            P(),
        ),
        check_vma=False,
    )
```

```python
import functools
import math

import jax
import jax.numpy as jnp
from jax import lax
from jax.experimental import pallas as pl
from jax.experimental.pallas import tpu as pltpu
from jax.sharding import PartitionSpec as P

D = 128
HEADS = 8
FF = 256
EXPERTS = 4
HEAD_DIM = 16
HIDDEN = EXPERTS * FF

epsilon = 1e-05
far_below = -1e30
momentum_decay = 0.9
average_decay = 0.95

F32 = jnp.float32
BF16 = jnp.bfloat16
MESH = pl.DeviceIdType.MESH

ROW_GAIN_ONE, ROW_BIAS_ONE = 0, 1
ROW_QUERY = 2
ROW_CROSS_OUT = ROW_QUERY + D
ROW_GAIN_TWO = ROW_CROSS_OUT + D
ROW_BIAS_TWO = ROW_GAIN_TWO + 1
ROW_QKV = ROW_BIAS_TWO + 1
ROW_SELF_OUT = ROW_QKV + 3 * D
ROW_GAIN_THREE = ROW_SELF_OUT + D
ROW_BIAS_THREE = ROW_GAIN_THREE + 1
ROW_ROUTER = ROW_BIAS_THREE + 1
ROW_UP = ROW_ROUTER + EXPERTS
ROW_DOWN = ROW_UP + 2 * D * EXPERTS
SHARED_ROWS = ROW_DOWN + HIDDEN
BRANCH_ROWS = 2 + 2 * D

EXPERT_ROWS = 2 * FF
EARLY_ROWS = 2 * D
MIDDLE_ROWS = 2 * D
LAST_ROWS = 2 * D + 32
BRANCH_SENT = 2 * D + 32

VMEM_LIMIT = 52


def dot(a, b):
    return jnp.dot(a, b, preferred_element_type=F32)


def dot_points(a, b):
    return lax.dot_general(a, b, (((1,), (1,)), ((), ())), preferred_element_type=F32)


class Level:
    def __init__(self, size, index, member):
        self.size, self.index, self.member = size, index, member


def split_rows(rows, size):
    step = 16
    while rows % step or rows // step > size:
        step += 16
    return step, rows // step


class Reduction:
    def __init__(self, sizes, rows):
        self.sizes, self.rows = sizes, rows
        self.steps, self.owners = [], []
        for size in sizes:
            step, owners = split_rows(rows, size)
            self.steps.append(step)
            self.owners.append(owners)
            rows = step

    def scratch(self):
        shapes = [pltpu.VMEM((self.rows, D), BF16), pltpu.VMEM((self.rows, D), BF16)]
        for at, size in enumerate(self.sizes):
            shapes.append(pltpu.VMEM(((size - 1) * self.steps[at], D), BF16))
            shapes.append(pltpu.VMEM((self.steps[at], D), BF16))
            shapes.append(pltpu.SemaphoreType.DMA((4,)))
        return shapes

    def bind(self, refs, levels):
        self.source, self.total = refs[0], refs[1]
        self.parts = [refs[2 + 3 * at : 5 + 3 * at] for at in range(len(self.sizes))]
        self.levels = levels
        last = len(self.sizes) - 1
        self.steps_left = []
        for at in range(last):
            self.steps_left.append(lambda at=at: (self.add(at), self.scatter(at + 1)))
        self.steps_left.append(lambda: (self.add(last), self.gather(last)))
        for at in range(last, 0, -1):
            self.steps_left.append(lambda at=at: (self.collect(at), self.gather(at - 1)))
        self.steps_left.append(lambda: self.collect(0))

    def begin(self):
        self.scatter(0)

    def advance(self):
        if self.steps_left:
            self.steps_left.pop(0)()

    def base(self, at):
        start = 0
        for upper in range(at):
            start = start + self.levels[upper].index * self.steps[upper]
        return start

    def inside(self, at):
        condition = None
        for upper in range(at):
            if self.owners[upper] < self.sizes[upper]:
                here = self.levels[upper].index < self.owners[upper]
                condition = here if condition is None else jnp.logical_and(condition, here)
        return condition

    def when(self, condition, body):
        if condition is None:
            body()
        else:
            pl.when(condition)(body)

    def split(self, at, owner, other):
        def go():
            if self.owners[at] == self.sizes[at]:
                owner()
            else:
                here = self.levels[at].index < self.owners[at]
                pl.when(here)(owner)
                if other is not None:
                    pl.when(jnp.logical_not(here))(other)

        self.when(self.inside(at), go)

    def rows_from(self, at):
        return self.source if at == 0 else self.parts[at - 1][1]

    def wait(self, at, sem, rows, sending):
        window = self.source if rows <= self.rows else self.parts[at][0]
        copy = pltpu.make_async_remote_copy(
            src_ref=window.at[pl.ds(0, rows), :],
            dst_ref=window.at[pl.ds(0, rows), :],
            send_sem=self.parts[at][2].at[sem],
            recv_sem=self.parts[at][2].at[sem],
            device_id=self.levels[at].member(self.levels[at].index),
            device_id_type=MESH,
        )
        (copy.wait_send if sending else copy.wait_recv)()

    def scatter(self, at):
        level, step, owners = self.levels[at], self.steps[at], self.owners[at]
        received, _, sems = self.parts[at]

        def go():
            def one(k, carry):
                peer = (level.index + k) % level.size

                def start():
                    pltpu.make_async_remote_copy(
                        src_ref=self.rows_from(at).at[pl.ds(pl.multiple_of(peer * step, 16), step), :],
                        dst_ref=received.at[pl.ds(pl.multiple_of((k - 1) * step, 16), step), :],
                        send_sem=sems.at[0],
                        recv_sem=sems.at[1],
                        device_id=level.member(peer),
                        device_id_type=MESH,
                    ).start()

                self.when(None if owners == level.size else peer < owners, start)
                return carry

            lax.fori_loop(1, level.size, one, 0)

        self.when(self.inside(at), go)

    def add(self, at):
        level, step = self.levels[at], self.steps[at]

        def go():
            received, kept, _ = self.parts[at]
            self.wait(at, 1, (level.size - 1) * step, False)
            start = pl.multiple_of(level.index * step, 16)
            total = self.rows_from(at)[pl.ds(start, step), :].astype(F32)
            for k in range(level.size - 1):
                total = total + received[k * step : (k + 1) * step, :].astype(F32)
            if at + 1 < len(self.sizes):
                kept[...] = total.astype(BF16)
            else:
                self.total[pl.ds(pl.multiple_of(self.base(at) + start, 16), step), :] = total.astype(BF16)

        self.split(at, go, None)

    def gather(self, at):
        level, step = self.levels[at], self.steps[at]
        sems = self.parts[at][2]

        def go():
            rows = pl.ds(pl.multiple_of(self.base(at) + level.index * step, 16), step)

            def one(k, carry):
                pltpu.make_async_remote_copy(
                    src_ref=self.total.at[rows, :],
                    dst_ref=self.total.at[rows, :],
                    send_sem=sems.at[2],
                    recv_sem=sems.at[3],
                    device_id=level.member((level.index + k) % level.size),
                    device_id_type=MESH,
                ).start()
                return carry

            lax.fori_loop(1, level.size, one, 0)

        self.split(at, go, None)

    def collect(self, at):
        step, owners = self.steps[at], self.owners[at]
        self.split(
            at,
            lambda: self.wait(at, 3, (owners - 1) * step, False) if owners > 1 else None,
            lambda: self.wait(at, 3, owners * step, False),
        )

    def drain(self):
        for at, size in enumerate(self.sizes):
            step, owners = self.steps[at], self.owners[at]

            def owner():
                if owners > 1:
                    self.wait(at, 0, (owners - 1) * step, True)
                self.wait(at, 2, (size - 1) * step, True)

            self.split(at, owner, lambda: self.wait(at, 0, owners * step, True))


def inner_size(pts):
    return 2 if pts % 2 == 0 else 1


def middle_size(pts):
    outer = pts // inner_size(pts)
    return 2 if outer % 2 == 0 else 1


def plan(fns, pts):
    core, middle = inner_size(pts), middle_size(pts)
    far = pts // (core * middle)
    stepwise = [core, fns * middle, far]
    small = fns * pts <= 32
    halved = [core, fns * middle * far] if small else stepwise
    at_once = [fns * pts] if small else stepwise
    items = [pts] if small else [core * middle, far]
    return [
        Reduction(stepwise, EXPERT_ROWS),
        Reduction(stepwise, EXPERT_ROWS),
        Reduction(halved, EXPERT_ROWS),
        Reduction(halved, EXPERT_ROWS),
        Reduction(halved, EARLY_ROWS),
        Reduction(halved, MIDDLE_ROWS),
        Reduction(at_once, LAST_ROWS),
        Reduction(items, BRANCH_SENT),
    ]


def layer_norm(values):
    centred = values - jnp.mean(values, axis=0, keepdims=True)
    spread = jnp.mean(centred * centred, axis=0, keepdims=True)
    inverse = lax.rsqrt(spread + epsilon)
    return centred * inverse, inverse


def norm_back(normed, inverse, gain, upstream):
    scaled = upstream * gain
    first = jnp.mean(scaled, axis=0, keepdims=True)
    second = jnp.mean(scaled * normed, axis=0, keepdims=True)
    return (scaled - first - normed * second) * inverse


def heads_view(values):
    return values.reshape(HEADS, HEAD_DIM, values.shape[-1])


def feature_softmax(values):
    shaped = heads_view(values)
    powers = jnp.exp(shaped - jnp.max(shaped, axis=1, keepdims=True))
    return (powers * (1.0 / jnp.sum(powers, axis=1, keepdims=True))).reshape(values.shape)


def feature_softmax_back(soft, upstream):
    shaped, incoming = heads_view(soft), heads_view(upstream)
    inner = jnp.sum(shaped * incoming, axis=1, keepdims=True)
    return (shaped * (incoming - inner)).reshape(soft.shape)


def over_points(values):
    return jnp.sum(values, axis=1, keepdims=True)


def step_kernel(fns, pts, shared_rate, branch_rate, *refs):
    refs = list(refs)

    def take(n):
        got = refs[:n]
        del refs[:n]
        return got

    presence, fn_counts, item_counts = take(3)
    points_hbm, geometry_hbm, functions_hbm, cotangent_hbm, shared_hbm, branch_hbm = take(6)
    momenta_hbm = take(4)
    output, input_grad = take(2)
    shared_new, branch_new, norms_out = take(4), take(4), take(1)[0]
    shared_v, branch_v = shared_new[0], branch_new[0]
    points_v, geometry_v, functions_v, cotangent_v, branch_rows, shared_sum, branch_sum = take(7)
    fn_powers, fn_low, fn_values, fn_normed, hidden_v, pre_v, back_v, g_expert_v, up_t, down_t = take(10)
    sent, got = take(2)
    local_sem, x_send, x_recv = take(3)
    reductions = plan(fns, pts)
    bound = [take(len(reduction.scratch())) for reduction in reductions]
    assert not refs

    fn, pt = lax.axis_index("fn"), lax.axis_index("pts")
    core_size, middle_size_ = inner_size(pts), middle_size(pts)
    near_size = core_size * middle_size_
    far, near = pt // near_size, pt % near_size
    middle_at, core = near // core_size, near % core_size
    far_level = Level(pts // near_size, far, lambda j: (fn, j * near_size + near))
    stepwise = [
        Level(core_size, core, lambda j: (fn, pt - core + j)),
        Level(
            fns * middle_size_,
            fn * middle_size_ + middle_at,
            lambda j: (j // middle_size_, far * near_size + j % middle_size_ * core_size + core),
        ),
        far_level,
    ]
    if fns * pts <= 32:
        outer = pts // core_size
        halved = [
            stepwise[0],
            Level(
                fns * outer,
                fn * outer + pt // core_size,
                lambda j: (j // outer, j % outer * core_size + core),
            ),
        ]
        at_once = [Level(fns * pts, fn * pts + pt, lambda j: (j // pts, j % pts))]
        items = [Level(pts, pt, lambda j: (fn, j))]
        greeted = at_once
    else:
        halved = at_once = stepwise
        items = [Level(near_size, near, lambda j: (fn, far * near_size + j)), far_level]
        greeted = [
            Level(
                fns * near_size,
                fn * near_size + near,
                lambda j: (j // near_size, far * near_size + j % near_size),
            ),
            far_level,
        ]
    ways = [stepwise, stepwise, halved, halved, halved, halved, at_once, items]
    for reduction, scratch, levels in zip(reductions, bound, ways):
        reduction.bind(scratch, levels)
    experts = reductions[:EXPERTS]
    early, middle, last, branch = reductions[EXPERTS:]

    rows, fn_rows = points_v.shape[0], functions_v.shape[0]

    loads = []
    for at, (source, target) in enumerate(
        [
            (branch_hbm, branch_v),
            (functions_hbm, functions_v),
            (shared_hbm, shared_v),
            (points_hbm, points_v),
            (geometry_hbm, geometry_v),
            (cotangent_hbm, cotangent_v),
            *zip(momenta_hbm, [*shared_new[1:3], *branch_new[1:3]]),
        ]
    ):
        loads.append(pltpu.make_async_copy(source, target, local_sem.at[at]))
        loads[-1].start()

    barrier = pltpu.get_barrier_semaphore()
    for level in greeted:

        def greet(k, carry, level=level):
            pl.semaphore_signal(
                barrier,
                inc=1,
                device_id=level.member((level.index + k) % level.size),
                device_id_type=MESH,
            )
            return carry

        lax.fori_loop(1, level.size, greet, 0)

    def exchange(at):
        return pltpu.make_async_remote_copy(
            src_ref=sent.at[at],
            dst_ref=got.at[at],
            send_sem=x_send.at[at],
            recv_sem=x_recv.at[at],
            device_id=((fn + 1) % fns, pt),
            device_id_type=MESH,
        )

    row_at = lax.broadcasted_iota(jnp.int32, (D, D), 0)
    column_at = lax.broadcasted_iota(jnp.int32, (D, D), 1)
    same_head = row_at // HEAD_DIM == column_at // HEAD_DIM
    diagonal = row_at == column_at

    def diagonal_blocks(full):
        return jnp.where(same_head, full, 0.0)

    def folded(full):
        kept = diagonal_blocks(full)
        out = kept[:HEAD_DIM]
        for head in range(1, HEADS):
            out = out + kept[head * HEAD_DIM : (head + 1) * HEAD_DIM]
        return out

    def unfolded(compact):
        return diagonal_blocks(jnp.concatenate([compact] * HEADS, axis=0))

    def to_row(column):
        return jnp.sum(jnp.where(diagonal, column, 0.0), axis=0, keepdims=True)

    def to_column(row):
        return jnp.sum(jnp.where(diagonal, row, 0.0), axis=1, keepdims=True)

    loads[0].wait()
    for r in range(BRANCH_ROWS):
        branch_rows[r : r + 1, :] = branch_v[0:1, r * D : (r + 1) * D]
    kv = jnp.concatenate(
        [branch_rows[pl.ds(2, D, stride=2), :], branch_rows[pl.ds(3, D, stride=2), :]], axis=1
    ).astype(BF16)
    branch_gain = to_column(branch_rows[0:1, :])
    branch_bias = to_column(branch_rows[1:2, :])
    fn_count = fn_counts[0, 0]
    fn_weight = (presence[0, 0] * fn_count).astype(F32)
    fn_usable = lax.broadcasted_iota(jnp.int32, (1, fn_rows), 1) < fn_count
    loads[1].wait()
    normed, _ = layer_norm(functions_v[...].astype(F32).T)
    hidden = (normed * branch_gain + branch_bias).astype(BF16)
    fn_normed[...] = normed.astype(BF16)
    keyval = dot(kv.T, hidden)
    keys = jnp.where(fn_usable, keyval[:D], far_below)
    fn_values[...] = keyval[D:].astype(BF16)
    fn_max = jnp.max(keys, axis=1, keepdims=True)
    powers = jnp.where(fn_usable, jnp.exp(keys - fn_max), 0.0)
    fn_powers[...] = powers
    fn_low[...] = powers.astype(BF16)
    fn_scale = 1.0 / over_points(powers)
    fn_summary = diagonal_blocks(dot_points(fn_low[...], fn_values[...]) * fn_scale)
    weighted_summary = fn_weight * folded(fn_summary)
    sent[0, 0:HEAD_DIM, :] = weighted_summary
    sent[0, HEAD_DIM : HEAD_DIM + 8, :] = jnp.full((8, D), fn_weight, F32)
    pl.semaphore_wait(barrier, sum(level.size - 1 for level in greeted))
    exchange(0).start()

    loads[2].wait()

    def shared_rows(start, stride=1):
        return shared_v[pl.ds(start, D, stride=stride), :].astype(BF16)

    query_w = shared_rows(ROW_QUERY)
    cross_w = shared_rows(ROW_CROSS_OUT)
    self_w = shared_rows(ROW_SELF_OUT)
    qkv_w = jnp.concatenate([shared_rows(ROW_QKV + third, 3) for third in range(3)], axis=1)

    for piece_at in range(2 * EXPERTS):
        number, half = piece_at // 2, piece_at % 2
        up_t[piece_at * D : (piece_at + 1) * D, :] = shared_rows(ROW_UP + number * FF + half, 2).T
        down_t[:, piece_at * D : (piece_at + 1) * D] = shared_rows(ROW_DOWN + piece_at * D).T

    expert_at = lax.broadcasted_iota(jnp.int32, (8, D), 0)
    router_mask = lax.broadcasted_iota(jnp.int32, (8, D), 1) % EXPERTS == expert_at
    router_t = jnp.zeros((8, D), F32)
    pickers = []
    for r in range(EXPERTS):
        picker = jnp.where(column_at == r * (D // EXPERTS) + row_at // EXPERTS, 1.0, 0.0).astype(BF16)
        pickers.append(picker)
        router_row = shared_v[ROW_ROUTER + r : ROW_ROUTER + r + 1, :]
        router_t = router_t + dot(jnp.where(router_mask, router_row, 0.0).astype(BF16), picker)
    router_t = router_t.astype(BF16)

    def shared_column(row):
        return to_column(shared_v[row : row + 1, :])

    gain_one, bias_one = shared_column(ROW_GAIN_ONE), shared_column(ROW_BIAS_ONE)
    gain_two, bias_two = shared_column(ROW_GAIN_TWO), shared_column(ROW_BIAS_TWO)
    gain_three, bias_three = shared_column(ROW_GAIN_THREE), shared_column(ROW_BIAS_THREE)

    loads[3].wait()
    points = points_v[...].astype(F32).T
    normed_one, inverse_one = layer_norm(points)
    hidden_one = (normed_one * gain_one + bias_one).astype(BF16)
    cross_soft = feature_softmax(dot(query_w.T, hidden_one))
    cross_low = cross_soft.astype(BF16)

    exchange(0).wait_recv()
    weight_total = fn_weight + got[0, HEAD_DIM : HEAD_DIM + 1, :]
    fn_share = fn_weight / weight_total
    mixed = unfolded((weighted_summary + got[0, 0:HEAD_DIM, :]) / weight_total)
    mixed_low = mixed.astype(BF16)
    cross_out = dot(mixed.T.astype(BF16), cross_low).astype(BF16)
    after_cross = points + dot(cross_w.T, cross_out)
    normed_two, inverse_two = layer_norm(after_cross)
    hidden_two = (normed_two * gain_two + bias_two).astype(BF16)
    qkv = dot(qkv_w.T, hidden_two)
    usable = lax.broadcasted_iota(jnp.int32, (1, rows), 1) + fn * rows < item_counts[0]
    keys = jnp.where(usable, qkv[D : 2 * D], far_below)
    self_values = qkv[2 * D :].astype(BF16)
    key_max = jnp.max(keys, axis=1, keepdims=True)
    key_powers = jnp.where(usable, jnp.exp(keys - key_max), 0.0)
    key_low = key_powers.astype(BF16)
    own_total = over_points(key_powers)
    key_sum = dot_points(key_low, self_values)
    sent[1, 0:HEAD_DIM, :] = folded(key_sum)
    sent[1, HEAD_DIM : HEAD_DIM + 8, :] = jnp.concatenate(
        [to_row(key_max), to_row(own_total), jnp.zeros((6, D), F32)], axis=0
    )
    exchange(1).start()

    self_soft = feature_softmax(qkv[:D])
    self_weights = self_soft.astype(BF16)
    loads[4].wait()
    logits = dot_points(router_t, geometry_v[...])[:EXPERTS]
    powers = jnp.exp(logits - jnp.max(logits, axis=0, keepdims=True))
    gates = powers * (1.0 / jnp.sum(powers, axis=0, keepdims=True))
    half_gates = 0.5 * gates
    loads[5].wait()
    arriving = cotangent_v[...].astype(F32).T
    for number in range(EXPERTS):
        g_expert = (half_gates[number : number + 1] * arriving).astype(BF16)
        g_expert_v[number * D : (number + 1) * D, :] = g_expert
        down = shared_v[ROW_DOWN + number * FF : ROW_DOWN + (number + 1) * FF, :].astype(BF16)
        back_v[number * FF : (number + 1) * FF, :] = dot(down, g_expert)

    exchange(1).wait_recv()
    other_max = to_column(got[1, HEAD_DIM : HEAD_DIM + 1, :])
    other_total = to_column(got[1, HEAD_DIM + 1 : HEAD_DIM + 2, :])
    joint_max = jnp.maximum(key_max, other_max)
    own_factor, other_factor = jnp.exp(key_max - joint_max), jnp.exp(other_max - joint_max)
    joint_scale = 1.0 / (own_total * own_factor + other_total * other_factor)
    own_factor, other_factor = own_factor * joint_scale, other_factor * joint_scale
    self_summary = diagonal_blocks(key_sum) * own_factor + unfolded(got[1, 0:HEAD_DIM, :]) * other_factor
    self_low = self_summary.astype(BF16)

    self_out = dot(self_summary.T.astype(BF16), self_weights).astype(BF16)
    after_self = after_cross + dot(self_w.T, self_out)
    normed_three, inverse_three = layer_norm(after_self)
    hidden_three = (normed_three * gain_three + bias_three).astype(BF16)

    def expert_sums(number):
        part = slice(number * FF, (number + 1) * FF)
        source = experts[number].source
        up_sum = dot_points(hidden_three, pre_v[part, :])
        source[0:D, :] = up_sum[:, :D].astype(BF16)
        source[D : 2 * D, :] = up_sum[:, D:].astype(BF16)
        source[FF:, :] = dot_points(hidden_v[part, :], g_expert_v[number * D : (number + 1) * D, :]).astype(BF16)
        experts[number].begin()

    def advance(*numbers):
        for number in numbers:
            reductions[number].advance()

    upstream, gated_grads = None, []
    for number in range(EXPERTS):
        part = slice(number * FF, (number + 1) * FF)
        argument = dot(up_t[part, :], hidden_three)
        back = back_v[part, :]
        twice_cdf = 1.0 + lax.erf(argument * math.sqrt(0.5))
        bell = jnp.exp2(argument * argument * (-0.5 * math.log2(math.e)) + 0.5 * math.log2(2.0 / math.pi))
        active = argument * twice_cdf
        gated_grads.append(jnp.sum(active * back, axis=0, keepdims=True))
        hidden_v[part, :] = active.astype(BF16)
        pre_v[part, :] = (back * (twice_cdf + argument * bell)).astype(BF16)
        up = jnp.concatenate([shared_rows(ROW_UP + number * FF + half, 2) for half in range(2)], axis=1)
        more = dot(up, pre_v[part, :])
        upstream = more if upstream is None else upstream + more
        if 0 < number < 3:
            expert_sums(number - 1)
        if number == 2:
            advance(0)
        if number == 3:
            advance(1)

    gated_grads = jnp.concatenate(gated_grads, axis=0)
    g_logits = gated_grads - gates * jnp.sum(gated_grads, axis=0, keepdims=True)
    g_logits = jnp.concatenate([g_logits, jnp.zeros_like(g_logits)], axis=0).astype(BF16)
    g_after_self = arriving + norm_back(normed_three, inverse_three, gain_three, upstream)
    g_proj = g_after_self.astype(BF16)
    g_self_out = dot(self_w, g_proj).astype(BF16)
    own_grad = folded(dot_points(self_weights, g_self_out))
    sent[2, 0:HEAD_DIM, :] = own_grad
    exchange(2).start()
    expert_sums(2)
    advance(0)
    expert_sums(3)
    g_queries = feature_softmax_back(self_soft, dot(self_low, g_self_out)).astype(BF16)
    early.source[0:D, :] = dot_points(self_out, g_proj).astype(BF16)
    early.source[D:, :] = dot_points(hidden_two, g_queries).astype(BF16)
    early.begin()
    advance(1, 2)
    router_sum = dot(g_logits, geometry_v[...])
    small = [None] * 6
    small[4] = to_row(over_points(upstream * normed_three))
    small[5] = to_row(over_points(upstream))
    query_part = dot(qkv_w[:, :D], g_queries)
    advance(3, 4)

    exchange(2).wait_recv()
    scaled_grad = unfolded(own_grad + got[2, 0:HEAD_DIM, :]) * own_factor
    correction = over_points(scaled_grad * self_summary)
    g_keys = key_powers * (dot(scaled_grad.astype(BF16), self_values) - correction)
    g_values = dot(scaled_grad.T.astype(BF16), key_low)
    g_keyval = jnp.concatenate([g_keys.astype(BF16), g_values.astype(BF16)], axis=0)
    upstream = query_part + dot(qkv_w[:, D:], g_keyval)
    keyval_sum = dot_points(hidden_two, g_keyval)
    for half in range(2):
        middle.source[half * D : (half + 1) * D, :] = keyval_sum[:, half * D : (half + 1) * D].astype(BF16)
    middle.begin()
    g_after_cross = g_after_self + norm_back(normed_two, inverse_two, gain_two, upstream)
    g_proj = g_after_cross.astype(BF16)
    g_cross_out = dot(cross_w, g_proj).astype(BF16)
    own_mixed = folded(dot_points(cross_low, g_cross_out))
    sent[3, 0:HEAD_DIM, :] = own_mixed
    exchange(3).start()
    advance(0, 1)
    last.source[D : 2 * D, :] = dot_points(cross_out, g_proj).astype(BF16)
    small[2] = to_row(over_points(upstream * normed_two))
    small[3] = to_row(over_points(upstream))
    g_query = feature_softmax_back(cross_soft, dot(mixed_low, g_cross_out)).astype(BF16)
    advance(5, 2)
    upstream_one = dot(query_w, g_query)
    last.source[0:D, :] = dot_points(hidden_one, g_query).astype(BF16)
    small[0] = to_row(over_points(upstream_one * normed_one))
    small[1] = to_row(over_points(upstream_one))
    last.source[2 * D :, :] = jnp.concatenate(
        [router_sum, *small, jnp.zeros((32 - 8 - len(small), D), F32)], axis=0
    ).astype(BF16)
    last.begin()
    advance(3, 4)

    exchange(3).wait_recv()
    fn_grad = unfolded((own_mixed + got[3, 0:HEAD_DIM, :]) * fn_share)
    fn_scaled = fn_grad * fn_scale
    fn_correction = over_points(fn_scaled * fn_summary)
    g_keys = fn_powers[...] * (dot(fn_scaled.astype(BF16), fn_values[...]) - fn_correction)
    g_values = dot(fn_scaled.T.astype(BF16), fn_low[...])
    g_keyval = jnp.concatenate([g_keys, g_values], axis=0).astype(BF16)
    normed_sum = dot_points(fn_normed[...], g_keyval)
    plain_sum = dot_points(jnp.ones((8, fn_rows), BF16), g_keyval)[0:1]
    kv_sum = branch_gain * normed_sum + branch_bias * plain_sum
    for half in range(2):
        branch.source[half * D : (half + 1) * D, :] = kv_sum[:, half * D : (half + 1) * D].astype(BF16)
    kv_wide = kv.astype(F32)
    branch.source[2 * D :, :] = jnp.concatenate(
        [to_row(over_points(kv_wide * normed_sum)), to_row(over_points(kv_wide * plain_sum)), jnp.zeros((30, D), F32)],
        axis=0,
    ).astype(BF16)
    branch.begin()
    total = g_after_cross + norm_back(normed_one, inverse_one, gain_one, upstream_one)
    input_grad[...] = total.T.astype(BF16)
    advance(0, 1)
    result = after_self
    for number in range(EXPERTS):
        part = slice(number * FF, (number + 1) * FF)
        result = result + half_gates[number : number + 1] * dot(down_t[:, part], hidden_v[part, :])
    output[...] = result.T.astype(BF16)
    advance(5, 0, 2, 3, 4, 1)
    last.advance()
    branch.advance()
    advance(0, 1, 2, 3, 4)

    for load in loads[6:]:
        load.wait()
    waiting = [*experts, early, middle, last, branch]

    def finish(reduction):
        while reduction.steps_left:
            for other in waiting:
                if other is reduction or len(other.steps_left) > 1:
                    other.advance()

    def renew(start, count):
        part = slice(start, start + count)
        new = sgd_update(*(ref[part, :] for ref in shared_new[:3]), shared_sum[part, :], shared_rate)
        for value, target in zip(new, shared_new):
            target[part, :] = value

    for number, sums in enumerate(experts):
        finish(sums)
        for half in range(2):
            shared_sum[pl.ds(ROW_UP + number * FF + half, D, stride=2), :] = sums.total[
                half * D : (half + 1) * D, :
            ].astype(F32)
        start = ROW_DOWN + number * FF
        shared_sum[start : start + FF, :] = sums.total[FF:, :].astype(F32)
    whole = -(-ROW_UP // 16) * 16
    renew(whole, SHARED_ROWS - whole)
    finish(early)
    finish(middle)
    shared_sum[ROW_SELF_OUT : ROW_SELF_OUT + D, :] = early.total[0:D, :].astype(F32)
    for third, held in enumerate([early.total[D:, :], middle.total[:D, :], middle.total[D:, :]]):
        shared_sum[pl.ds(ROW_QKV + third, D, stride=3), :] = held.astype(F32)
    finish(last)
    shared_sum[ROW_QUERY : ROW_QUERY + D, :] = last.total[0:D, :].astype(F32)
    shared_sum[ROW_CROSS_OUT : ROW_CROSS_OUT + D, :] = last.total[D : 2 * D, :].astype(F32)
    rest = last.total[2 * D :, :].astype(F32)
    for at, row in enumerate(
        [ROW_GAIN_ONE, ROW_BIAS_ONE, ROW_GAIN_TWO, ROW_BIAS_TWO, ROW_GAIN_THREE, ROW_BIAS_THREE]
    ):
        shared_sum[row : row + 1, :] = rest[8 + at : 9 + at]
    norms_out[...] = rest[8:14]
    router_low = rest[:8].astype(BF16)
    for r in range(EXPERTS):
        spread = dot_points(router_low, pickers[r])
        shared_sum[ROW_ROUTER + r : ROW_ROUTER + r + 1, :] = jnp.sum(
            jnp.where(router_mask, spread, 0.0), axis=0, keepdims=True
        )
    renew(0, whole)
    finish(branch)
    for half in range(2):
        branch_rows[pl.ds(2 + half, D, stride=2), :] = branch.total[
            half * D : (half + 1) * D, :
        ].astype(F32)
    branch_rows[0:2, :] = branch.total[2 * D :, :].astype(F32)[0:2]
    for r in range(BRANCH_ROWS):
        branch_sum[0:1, r * D : (r + 1) * D] = branch_rows[r : r + 1, :]
    new = sgd_update(*(ref[...] for ref in branch_new[:3]), branch_sum[...], branch_rate)
    for value, target in zip(new, branch_new):
        target[...] = value

    for at in range(4):
        exchange(at).wait_send()
    for reduction in reductions:
        reduction.drain()


def sgd_update(weights, momentum, average, gradient, step_rate):
    momentum_new = momentum_decay * momentum + gradient
    weights_new = weights - step_rate * (gradient + momentum_decay * momentum_new)
    average_new = average_decay * average + (1.0 - average_decay) * weights_new
    return (weights_new, momentum_new, average_new, weights_new.astype(BF16))


def low(*shape):
    return pltpu.VMEM(shape, BF16)


def wide(*shape):
    return pltpu.VMEM(shape, F32)


def whole_step(fns, pts, rates, counts, arrays, momenta):
    points, _, functions = arrays[:3]
    rows, fn_rows = points.shape[0], functions.shape[0]
    smem = pl.BlockSpec(memory_space=pltpu.SMEM)
    vmem = pl.BlockSpec(memory_space=pltpu.VMEM)
    anywhere = pl.BlockSpec(memory_space=pl.ANY)
    branch = (1, BRANCH_ROWS * D)

    outs = [low(rows, D), low(rows, D)]
    outs += [wide(SHARED_ROWS, D)] * 3 + [low(SHARED_ROWS, D)] + [wide(*branch)] * 3 + [low(*branch)] + [wide(6, D)]
    scratch = [low(rows, D), low(rows, D), low(fn_rows, D), low(rows, D)]
    scratch += [wide(BRANCH_ROWS, D), wide(SHARED_ROWS, D), wide(*branch)]
    scratch += [wide(D, fn_rows), low(D, fn_rows), low(D, fn_rows), low(D, fn_rows), low(HIDDEN, rows), low(HIDDEN, rows)]
    scratch += [wide(HIDDEN, rows), low(EXPERTS * D, rows), low(HIDDEN, D), low(D, HIDDEN)]
    scratch += [wide(4, HEAD_DIM + 8, D), wide(4, HEAD_DIM + 8, D)]
    scratch += [pltpu.SemaphoreType.DMA((10,)), pltpu.SemaphoreType.DMA((4,)), pltpu.SemaphoreType.DMA((4,))]
    for reduction in plan(fns, pts):
        scratch += reduction.scratch()
    return pl.pallas_call(
        functools.partial(step_kernel, fns, pts, *rates),
        out_shape=outs,
        in_specs=[smem] * 3 + [anywhere] * (len(arrays) + len(momenta)),
        out_specs=[vmem] * len(outs),
        scratch_shapes=scratch,
        compiler_params=pltpu.CompilerParams(
            collective_id=0, has_side_effects=True, vmem_limit_bytes=VMEM_LIMIT << 20
        ),
    )(*counts, *(pltpu.with_memory_space_constraint(value, pltpu.HBM) for value in (*arrays, *momenta)))


def store_kernel(count, *refs):
    copies = [
        pltpu.make_async_copy(source, target, refs[-1].at[at])
        for at, (source, target) in enumerate(zip(refs[:count], refs[count:]))
    ]
    for copy in copies:
        copy.start()
    for copy in copies:
        copy.wait()


def stored(values):
    count = len(values)
    return pl.pallas_call(
        functools.partial(store_kernel, count),
        out_shape=[jax.ShapeDtypeStruct(value.shape, value.dtype) for value in values],
        in_specs=[pl.BlockSpec(memory_space=pltpu.VMEM)] * count,
        out_specs=[pl.BlockSpec(memory_space=pl.ANY)] * count,
        scratch_shapes=[pltpu.SemaphoreType.DMA((count,))],
        compiler_params=pltpu.CompilerParams(vmem_limit_bytes=4 << 20),
    )(*values)


def local(
    fns,
    pts,
    points_in,
    geometry,
    functions,
    presence,
    fn_counts,
    item_counts,
    cotangent,
    shared_weights,
    shared_momentum,
    shared_average,
    branch_weights,
    branch_momentum,
    branch_average,
):
    rows, fn_rows = points_in.shape[1], functions.shape[2]
    rates = (0.1 / math.sqrt(pts * rows * fns), 0.1 / math.sqrt(pts * fn_rows))
    arrays = [
        points_in.reshape(rows, D),
        geometry.reshape(rows, D),
        functions.reshape(fn_rows, D),
        cotangent.reshape(rows, D),
        shared_weights.reshape(SHARED_ROWS, D),
        branch_weights,
    ]
    momenta = [value.reshape(SHARED_ROWS, D) for value in (shared_momentum, shared_average)]
    momenta += [branch_momentum, branch_average]
    new = stored(whole_step(fns, pts, rates, (presence, fn_counts, item_counts), arrays, momenta))
    return (
        new[0].reshape(1, rows, D),
        new[1].reshape(1, rows, D),
        *(value.reshape(-1) for value in new[2:6]),
        *new[6:],
    )


def solution(mesh):
    split = P("pts", "fn", None)
    return jax.shard_map(
        functools.partial(local, mesh.shape["fn"], mesh.shape["pts"]),
        mesh=mesh,
        in_specs=(
            split,
            split,
            P("fn", "pts", None, None),
            P("fn", "pts"),
            P("fn", "pts"),
            P("pts"),
            split,
            P(),
            P(),
            P(),
            P("fn", None),
            P("fn", None),
            P("fn", None),
        ),
        out_specs=(
            split,
            split,
            P(),
            P(),
            P(),
            P(),
            P("fn", None),
            P("fn", None),
            P("fn", None),
            P("fn", None),
            P(),
        ),
        check_vma=False,
    )
```

```python
import functools
import math

import jax
import jax.numpy as jnp
from jax import lax
from jax.experimental import pallas as pl
from jax.experimental.pallas import tpu as pltpu
from jax.sharding import PartitionSpec as P

D = 128
HEADS = 8
FF = 256
EXPERTS = 4
HEAD_DIM = 16
HIDDEN = EXPERTS * FF

epsilon = 1e-05
far_below = -1e30
momentum_decay = 0.9
average_decay = 0.95

F32 = jnp.float32
BF16 = jnp.bfloat16
MESH = pl.DeviceIdType.MESH

ROW_GAIN_ONE, ROW_BIAS_ONE = 0, 1
ROW_QUERY = 2
ROW_CROSS_OUT = ROW_QUERY + D
ROW_GAIN_TWO = ROW_CROSS_OUT + D
ROW_BIAS_TWO = ROW_GAIN_TWO + 1
ROW_QKV = ROW_BIAS_TWO + 1
ROW_SELF_OUT = ROW_QKV + 3 * D
ROW_GAIN_THREE = ROW_SELF_OUT + D
ROW_BIAS_THREE = ROW_GAIN_THREE + 1
ROW_ROUTER = ROW_BIAS_THREE + 1
ROW_UP = ROW_ROUTER + EXPERTS
ROW_DOWN = ROW_UP + 2 * D * EXPERTS
SHARED_ROWS = ROW_DOWN + HIDDEN
BRANCH_ROWS = 2 + 2 * D

EXPERT_ROWS = 2 * FF
MIDDLE_ROWS = 4 * D
LAST_ROWS = 2 * D + 16
BRANCH_SENT = 2 * D + 32

VMEM_LIMIT = 52


def dot(a, b):
    return jnp.dot(a, b, preferred_element_type=F32)


def dot_points(a, b):
    return lax.dot_general(a, b, (((1,), (1,)), ((), ())), preferred_element_type=F32)


class Level:
    def __init__(self, grid, member):
        sizes = [size for size, _ in grid]
        self.size = math.prod(sizes)
        shifted = [
            [at if by == 0 else lax.rem(at + by, size) for by in range(size)] if size > 1 else [0]
            for size, at in grid
        ]
        self.peers = []
        for k in range(self.size):
            place, index, left = [], 0, k
            for size, moved in zip(reversed(sizes), reversed(shifted)):
                place.append(moved[left % size])
                left //= size
            place.reverse()
            for size, at in zip(sizes, place):
                index = index * size + at
            self.peers.append((index, member(*place)))
        self.index = self.peers[0][0]


TILE = 16


def split_rows(rows, size):
    step = TILE
    while rows % step or rows // step > size:
        step += TILE
    return step, rows // step


class Reduction:
    def __init__(self, sizes, rows):
        self.sizes, self.rows = sizes, rows
        self.steps, self.owners = [], []
        for size in sizes:
            step, owners = split_rows(rows, size)
            self.steps.append(step)
            self.owners.append(owners)
            rows = step

    def scratch(self):
        shapes = [pltpu.VMEM((self.rows, D), BF16), pltpu.VMEM((self.rows, D), BF16)]
        for at, size in enumerate(self.sizes):
            shapes.append(pltpu.VMEM(((size - 1) * self.steps[at], D), BF16))
            shapes.append(pltpu.VMEM((self.steps[at], D), BF16))
            shapes.append(pltpu.SemaphoreType.DMA((4,)))
        return shapes

    def bind(self, refs, levels):
        self.source, self.total = refs[0], refs[1]
        self.parts = [refs[2 + 3 * at : 5 + 3 * at] for at in range(len(self.sizes))]
        self.levels = levels
        last = len(self.sizes) - 1
        self.steps_left = []
        for at in range(last):
            self.steps_left.append(lambda at=at: (self.add(at), self.scatter(at + 1)))
        self.steps_left.append(lambda: (self.add(last), self.gather(last)))
        for at in range(last, 0, -1):
            self.steps_left.append(lambda at=at: (self.collect(at), self.gather(at - 1)))
        self.steps_left.append(lambda: self.collect(0))

    def begin(self):
        self.scatter(0)

    def advance(self):
        if self.steps_left:
            self.steps_left.pop(0)()

    def base(self, at):
        start = 0
        for upper in range(at):
            start = start + self.levels[upper].index * self.steps[upper]
        return start

    def inside(self, at):
        condition = None
        for upper in range(at):
            if self.owners[upper] < self.sizes[upper]:
                here = self.levels[upper].index < self.owners[upper]
                condition = here if condition is None else jnp.logical_and(condition, here)
        return condition

    def when(self, condition, body):
        if condition is None:
            body()
        else:
            pl.when(condition)(body)

    def split(self, at, owner, other):
        def go():
            if self.owners[at] == self.sizes[at]:
                owner()
            else:
                here = self.levels[at].index < self.owners[at]
                pl.when(here)(owner)
                if other is not None:
                    pl.when(jnp.logical_not(here))(other)

        self.when(self.inside(at), go)

    def rows_from(self, at):
        return self.source if at == 0 else self.parts[at - 1][1]

    def wait(self, at, sem, rows, sending):
        window = self.source if rows <= self.rows else self.parts[at][0]
        copy = pltpu.make_async_remote_copy(
            src_ref=window.at[pl.ds(0, rows), :],
            dst_ref=window.at[pl.ds(0, rows), :],
            send_sem=self.parts[at][2].at[sem],
            recv_sem=self.parts[at][2].at[sem],
            device_id=self.levels[at].peers[0][1],
            device_id_type=MESH,
        )
        (copy.wait_send if sending else copy.wait_recv)()

    def scatter(self, at):
        level, step, owners = self.levels[at], self.steps[at], self.owners[at]
        received, _, sems = self.parts[at]

        def go():
            for k in range(1, level.size):
                peer, device = level.peers[k]

                def start():
                    pltpu.make_async_remote_copy(
                        src_ref=self.rows_from(at).at[pl.ds(pl.multiple_of(peer * step, TILE), step), :],
                        dst_ref=received.at[pl.ds((k - 1) * step, step), :],
                        send_sem=sems.at[0],
                        recv_sem=sems.at[1],
                        device_id=device,
                        device_id_type=MESH,
                    ).start()

                self.when(None if owners == level.size else peer < owners, start)

        self.when(self.inside(at), go)

    def add(self, at):
        level, step = self.levels[at], self.steps[at]

        def go():
            received, kept, _ = self.parts[at]
            self.wait(at, 1, (level.size - 1) * step, False)
            start = pl.multiple_of(level.index * step, TILE)
            total = self.rows_from(at)[pl.ds(start, step), :].astype(F32)
            for k in range(level.size - 1):
                total = total + received[k * step : (k + 1) * step, :].astype(F32)
            if at + 1 < len(self.sizes):
                kept[...] = total.astype(BF16)
            else:
                self.total[pl.ds(pl.multiple_of(self.base(at) + start, TILE), step), :] = total.astype(BF16)

        self.split(at, go, None)

    def gather(self, at):
        level, step = self.levels[at], self.steps[at]
        sems = self.parts[at][2]

        def go():
            rows = pl.ds(pl.multiple_of(self.base(at) + level.index * step, TILE), step)

            for _, device in level.peers[1:]:
                pltpu.make_async_remote_copy(
                    src_ref=self.total.at[rows, :],
                    dst_ref=self.total.at[rows, :],
                    send_sem=sems.at[2],
                    recv_sem=sems.at[3],
                    device_id=device,
                    device_id_type=MESH,
                ).start()

        self.split(at, go, None)

    def collect(self, at):
        step, owners = self.steps[at], self.owners[at]
        self.split(
            at,
            lambda: self.wait(at, 3, (owners - 1) * step, False) if owners > 1 else None,
            lambda: self.wait(at, 3, owners * step, False),
        )

    def drain(self):
        for at, size in enumerate(self.sizes):
            step, owners = self.steps[at], self.owners[at]

            def owner():
                if owners > 1:
                    self.wait(at, 0, (owners - 1) * step, True)
                self.wait(at, 2, (size - 1) * step, True)

            self.split(at, owner, lambda: self.wait(at, 0, owners * step, True))


def inner_size(pts):
    return 2 if pts % 2 == 0 else 1


def middle_size(pts):
    outer = pts // inner_size(pts)
    return 2 if outer % 2 == 0 else 1


def plan(fns, pts):
    core, middle = inner_size(pts), middle_size(pts)
    far = pts // (core * middle)
    stepwise = [core, fns * middle, far]
    small = fns * pts <= 32
    halved = [core, fns * middle * far] if small else stepwise
    at_once = [fns * pts] if small else stepwise
    items = [pts] if small else [core * middle, far]
    return [
        Reduction(stepwise, EXPERT_ROWS),
        Reduction(stepwise, EXPERT_ROWS),
        Reduction(halved, EXPERT_ROWS),
        Reduction(halved, EXPERT_ROWS),
        Reduction(halved, MIDDLE_ROWS),
        Reduction(at_once, LAST_ROWS),
        Reduction(items, BRANCH_SENT),
    ]


def layer_norm(values):
    centred = values - jnp.mean(values, axis=0, keepdims=True)
    spread = jnp.mean(centred * centred, axis=0, keepdims=True)
    inverse = lax.rsqrt(spread + epsilon)
    return centred * inverse, inverse


def norm_back(normed, inverse, gain, upstream):
    scaled = upstream * gain
    first = jnp.mean(scaled, axis=0, keepdims=True)
    second = jnp.mean(scaled * normed, axis=0, keepdims=True)
    return (scaled - first - normed * second) * inverse


def heads_view(values):
    return values.reshape(HEADS, HEAD_DIM, values.shape[-1])


def feature_softmax(values):
    shaped = heads_view(values)
    powers = jnp.exp(shaped - jnp.max(shaped, axis=1, keepdims=True))
    return (powers * (1.0 / jnp.sum(powers, axis=1, keepdims=True))).reshape(values.shape)


def feature_softmax_back(soft, upstream):
    shaped, incoming = heads_view(soft), heads_view(upstream)
    inner = jnp.sum(shaped * incoming, axis=1, keepdims=True)
    return (shaped * (incoming - inner)).reshape(soft.shape)


def over_points(values):
    return jnp.sum(values, axis=1, keepdims=True)


def step_kernel(fns, pts, shared_rate, branch_rate, *refs):
    refs = list(refs)

    def take(n):
        got = refs[:n]
        del refs[:n]
        return got

    presence, fn_counts, item_counts = take(3)
    points_hbm, geometry_hbm, functions_hbm, cotangent_hbm, shared_hbm, branch_hbm = take(6)
    momenta_hbm = take(4)
    output, input_grad = take(2)
    shared_new, branch_new, norms_out = take(4), take(4), take(1)[0]
    shared_v, branch_v = shared_new[0], branch_new[0]
    points_v, geometry_v, functions_v, cotangent_v, branch_rows, shared_sum, branch_sum = take(7)
    fn_powers, fn_low, fn_values, fn_normed, hidden_v, pre_v, back_v, g_expert_v, up_t, down_t = take(10)
    sent, got = take(2)
    local_sem, x_send, x_recv = take(3)
    reductions = plan(fns, pts)
    bound = [take(len(reduction.scratch())) for reduction in reductions]
    assert not refs

    fn, pt = lax.axis_index("fn"), lax.axis_index("pts")
    core_size, mid_size = inner_size(pts), middle_size(pts)
    near_size = core_size * mid_size
    far, near = lax.div(pt, near_size), lax.rem(pt, near_size)
    mid, core = lax.div(near, core_size), lax.rem(near, core_size)

    def item(far_at, mid_at, core_at):
        return far_at * near_size + mid_at * core_size + core_at

    fn_axis, far_axis, mid_axis, core_axis = (fns, fn), (pts // near_size, far), (mid_size, mid), (core_size, core)
    far_level = Level([far_axis], lambda z: (fn, item(z, mid, core)))
    stepwise = [
        Level([core_axis], lambda c: (fn, item(far, mid, c))),
        Level([fn_axis, mid_axis], lambda f, m: (f, item(far, m, core))),
        far_level,
    ]
    if fns * pts <= 32:
        halved = [stepwise[0], Level([fn_axis, far_axis, mid_axis], lambda f, z, m: (f, item(z, m, core)))]
        at_once = [Level([fn_axis, far_axis, mid_axis, core_axis], lambda f, z, m, c: (f, item(z, m, c)))]
        items = [Level([far_axis, mid_axis, core_axis], lambda z, m, c: (fn, item(z, m, c)))]
        greeted = at_once
    else:
        halved = at_once = stepwise
        items = [Level([mid_axis, core_axis], lambda m, c: (fn, item(far, m, c))), far_level]
        greeted = [Level([fn_axis, mid_axis, core_axis], lambda f, m, c: (f, item(far, m, c))), far_level]
    ways = [stepwise, stepwise, halved, halved, halved, at_once, items]
    for reduction, scratch, levels in zip(reductions, bound, ways):
        reduction.bind(scratch, levels)
    experts = reductions[:EXPERTS]
    middle, last, branch = reductions[EXPERTS:]

    rows, fn_rows = points_v.shape[0], functions_v.shape[0]

    loads = []
    for at, (source, target) in enumerate(
        [
            (branch_hbm, branch_v),
            (functions_hbm, functions_v),
            (shared_hbm, shared_v),
            (points_hbm, points_v),
            (geometry_hbm, geometry_v),
            (cotangent_hbm, cotangent_v),
            *zip(momenta_hbm, [*shared_new[1:3], *branch_new[1:3]]),
        ]
    ):
        loads.append(pltpu.make_async_copy(source, target, local_sem.at[at]))
        loads[-1].start()

    barrier = pltpu.get_barrier_semaphore()
    for level in greeted:
        for _, device in level.peers[1:]:
            pl.semaphore_signal(barrier, inc=1, device_id=device, device_id_type=MESH)

    def exchange(at):
        return pltpu.make_async_remote_copy(
            src_ref=sent.at[at],
            dst_ref=got.at[at],
            send_sem=x_send.at[at],
            recv_sem=x_recv.at[at],
            device_id=(lax.rem(fn + 1, fns), pt),
            device_id_type=MESH,
        )

    row_at = lax.broadcasted_iota(jnp.int32, (D, D), 0)
    column_at = lax.broadcasted_iota(jnp.int32, (D, D), 1)
    same_head = row_at // HEAD_DIM == column_at // HEAD_DIM
    diagonal = row_at == column_at

    def diagonal_blocks(full):
        return jnp.where(same_head, full, 0.0)

    def folded(full):
        kept = diagonal_blocks(full)
        out = kept[:HEAD_DIM]
        for head in range(1, HEADS):
            out = out + kept[head * HEAD_DIM : (head + 1) * HEAD_DIM]
        return out

    def unfolded(compact):
        return diagonal_blocks(jnp.concatenate([compact] * HEADS, axis=0))

    def to_row(column):
        return jnp.sum(jnp.where(diagonal, column, 0.0), axis=0, keepdims=True)

    def to_column(row):
        return jnp.sum(jnp.where(diagonal, row, 0.0), axis=1, keepdims=True)

    loads[0].wait()
    for r in range(BRANCH_ROWS):
        branch_rows[r : r + 1, :] = branch_v[0:1, r * D : (r + 1) * D]
    kv = jnp.concatenate(
        [branch_rows[pl.ds(2, D, stride=2), :], branch_rows[pl.ds(3, D, stride=2), :]], axis=1
    ).astype(BF16)
    branch_gain = to_column(branch_rows[0:1, :])
    branch_bias = to_column(branch_rows[1:2, :])
    fn_count = fn_counts[0, 0]
    fn_weight = (presence[0, 0] * fn_count).astype(F32)
    fn_usable = lax.broadcasted_iota(jnp.int32, (1, fn_rows), 1) < fn_count
    loads[1].wait()
    normed, _ = layer_norm(functions_v[...].astype(F32).T)
    hidden = (normed * branch_gain + branch_bias).astype(BF16)
    fn_normed[...] = normed.astype(BF16)
    keyval = dot(kv.T, hidden)
    keys = jnp.where(fn_usable, keyval[:D], far_below)
    fn_values[...] = keyval[D:].astype(BF16)
    fn_max = jnp.max(keys, axis=1, keepdims=True)
    powers = jnp.where(fn_usable, jnp.exp(keys - fn_max), 0.0)
    fn_powers[...] = powers
    fn_low[...] = powers.astype(BF16)
    fn_scale = 1.0 / over_points(powers)
    fn_summary = diagonal_blocks(dot_points(fn_low[...], fn_values[...]) * fn_scale)
    weighted_summary = fn_weight * folded(fn_summary)
    sent[0, 0:HEAD_DIM, :] = weighted_summary
    sent[0, HEAD_DIM : HEAD_DIM + 8, :] = jnp.full((8, D), fn_weight, F32)
    pl.semaphore_wait(barrier, sum(level.size - 1 for level in greeted))
    exchange(0).start()

    loads[2].wait()

    def shared_rows(start, stride=1):
        return shared_v[pl.ds(start, D, stride=stride), :].astype(BF16)

    query_w = shared_rows(ROW_QUERY)
    cross_w = shared_rows(ROW_CROSS_OUT)
    self_w = shared_rows(ROW_SELF_OUT)
    qkv_w = jnp.concatenate([shared_rows(ROW_QKV + third, 3) for third in range(3)], axis=1)

    for piece_at in range(2 * EXPERTS):
        number, half = piece_at // 2, piece_at % 2
        up_t[piece_at * D : (piece_at + 1) * D, :] = shared_rows(ROW_UP + number * FF + half, 2).T
        down_t[:, piece_at * D : (piece_at + 1) * D] = shared_rows(ROW_DOWN + piece_at * D).T

    expert_at = lax.broadcasted_iota(jnp.int32, (8, D), 0)
    router_mask = lax.broadcasted_iota(jnp.int32, (8, D), 1) % EXPERTS == expert_at
    router_t = jnp.zeros((8, D), F32)
    pickers = []
    for r in range(EXPERTS):
        picker = jnp.where(column_at == r * (D // EXPERTS) + row_at // EXPERTS, 1.0, 0.0).astype(BF16)
        pickers.append(picker)
        router_row = shared_v[ROW_ROUTER + r : ROW_ROUTER + r + 1, :]
        router_t = router_t + dot(jnp.where(router_mask, router_row, 0.0).astype(BF16), picker)
    router_t = router_t.astype(BF16)

    def shared_column(row):
        return to_column(shared_v[row : row + 1, :])

    gain_one, bias_one = shared_column(ROW_GAIN_ONE), shared_column(ROW_BIAS_ONE)
    gain_two, bias_two = shared_column(ROW_GAIN_TWO), shared_column(ROW_BIAS_TWO)
    gain_three, bias_three = shared_column(ROW_GAIN_THREE), shared_column(ROW_BIAS_THREE)

    loads[3].wait()
    points = points_v[...].astype(F32).T
    normed_one, inverse_one = layer_norm(points)
    hidden_one = (normed_one * gain_one + bias_one).astype(BF16)
    cross_soft = feature_softmax(dot(query_w.T, hidden_one))
    cross_low = cross_soft.astype(BF16)

    exchange(0).wait_recv()
    weight_total = fn_weight + got[0, HEAD_DIM : HEAD_DIM + 1, :]
    fn_share = fn_weight / weight_total
    mixed = unfolded((weighted_summary + got[0, 0:HEAD_DIM, :]) / weight_total)
    mixed_low = mixed.astype(BF16)
    cross_out = dot(mixed.T.astype(BF16), cross_low).astype(BF16)
    after_cross = points + dot(cross_w.T, cross_out)
    normed_two, inverse_two = layer_norm(after_cross)
    hidden_two = (normed_two * gain_two + bias_two).astype(BF16)
    qkv = dot(qkv_w.T, hidden_two)
    usable = lax.broadcasted_iota(jnp.int32, (1, rows), 1) + fn * rows < item_counts[0]
    keys = jnp.where(usable, qkv[D : 2 * D], far_below)
    self_values = qkv[2 * D :].astype(BF16)
    key_max = jnp.max(keys, axis=1, keepdims=True)
    key_powers = jnp.where(usable, jnp.exp(keys - key_max), 0.0)
    key_low = key_powers.astype(BF16)
    own_total = over_points(key_powers)
    key_sum = dot_points(key_low, self_values)
    sent[1, 0:HEAD_DIM, :] = folded(key_sum)
    sent[1, HEAD_DIM : HEAD_DIM + 8, :] = jnp.concatenate(
        [to_row(key_max), to_row(own_total), jnp.zeros((6, D), F32)], axis=0
    )
    exchange(1).start()

    self_soft = feature_softmax(qkv[:D])
    self_weights = self_soft.astype(BF16)
    loads[4].wait()
    logits = dot_points(router_t, geometry_v[...])[:EXPERTS]
    powers = jnp.exp(logits - jnp.max(logits, axis=0, keepdims=True))
    gates = powers * (1.0 / jnp.sum(powers, axis=0, keepdims=True))
    half_gates = 0.5 * gates
    loads[5].wait()
    arriving = cotangent_v[...].astype(F32).T
    for number in range(EXPERTS):
        g_expert = (half_gates[number : number + 1] * arriving).astype(BF16)
        g_expert_v[number * D : (number + 1) * D, :] = g_expert
        down = shared_v[ROW_DOWN + number * FF : ROW_DOWN + (number + 1) * FF, :].astype(BF16)
        back_v[number * FF : (number + 1) * FF, :] = dot(down, g_expert)

    exchange(1).wait_recv()
    other_max = to_column(got[1, HEAD_DIM : HEAD_DIM + 1, :])
    other_total = to_column(got[1, HEAD_DIM + 1 : HEAD_DIM + 2, :])
    joint_max = jnp.maximum(key_max, other_max)
    own_factor, other_factor = jnp.exp(key_max - joint_max), jnp.exp(other_max - joint_max)
    joint_scale = 1.0 / (own_total * own_factor + other_total * other_factor)
    own_factor, other_factor = own_factor * joint_scale, other_factor * joint_scale
    self_summary = diagonal_blocks(key_sum) * own_factor + unfolded(got[1, 0:HEAD_DIM, :]) * other_factor
    self_low = self_summary.astype(BF16)

    self_out = dot(self_summary.T.astype(BF16), self_weights).astype(BF16)
    after_self = after_cross + dot(self_w.T, self_out)
    normed_three, inverse_three = layer_norm(after_self)
    hidden_three = (normed_three * gain_three + bias_three).astype(BF16)

    def expert_sums(number):
        part = slice(number * FF, (number + 1) * FF)
        source = experts[number].source
        up_sum = dot_points(hidden_three, pre_v[part, :])
        source[0:D, :] = up_sum[:, :D].astype(BF16)
        source[D : 2 * D, :] = up_sum[:, D:].astype(BF16)
        source[FF:, :] = dot_points(hidden_v[part, :], g_expert_v[number * D : (number + 1) * D, :]).astype(BF16)
        experts[number].begin()

    def advance(*numbers):
        for number in numbers:
            reductions[number].advance()

    upstream, gated_grads = None, []
    for number in range(EXPERTS):
        part = slice(number * FF, (number + 1) * FF)
        argument = dot(up_t[part, :], hidden_three)
        back = back_v[part, :]
        twice_cdf = 1.0 + lax.erf(argument * math.sqrt(0.5))
        bell = jnp.exp2(argument * argument * (-0.5 * math.log2(math.e)) + 0.5 * math.log2(2.0 / math.pi))
        active = argument * twice_cdf
        gated_grads.append(jnp.sum(active * back, axis=0, keepdims=True))
        hidden_v[part, :] = active.astype(BF16)
        pre_v[part, :] = (back * (twice_cdf + argument * bell)).astype(BF16)
        up = jnp.concatenate([shared_rows(ROW_UP + number * FF + half, 2) for half in range(2)], axis=1)
        more = dot(up, pre_v[part, :])
        upstream = more if upstream is None else upstream + more
        if 0 < number < 3:
            expert_sums(number - 1)
        if number == 2:
            advance(0)
        if number == 3:
            advance(1)

    gated_grads = jnp.concatenate(gated_grads, axis=0)
    g_logits = gated_grads - gates * jnp.sum(gated_grads, axis=0, keepdims=True)
    g_logits = jnp.concatenate([g_logits, jnp.zeros_like(g_logits)], axis=0).astype(BF16)
    g_after_self = arriving + norm_back(normed_three, inverse_three, gain_three, upstream)
    g_proj = g_after_self.astype(BF16)
    g_self_out = dot(self_w, g_proj).astype(BF16)
    own_grad = folded(dot_points(self_weights, g_self_out))
    sent[2, 0:HEAD_DIM, :] = own_grad
    exchange(2).start()
    expert_sums(2)
    advance(0)
    expert_sums(3)
    g_queries = feature_softmax_back(self_soft, dot(self_low, g_self_out)).astype(BF16)
    middle.source[2 * D : 3 * D, :] = dot_points(self_out, g_proj).astype(BF16)
    middle.source[3 * D :, :] = dot_points(hidden_two, g_queries).astype(BF16)
    advance(1, 2)
    router_sum = dot(g_logits, geometry_v[...])
    small = [None] * 6
    small[4] = to_row(over_points(upstream * normed_three))
    small[5] = to_row(over_points(upstream))
    query_part = dot(qkv_w[:, :D], g_queries)
    advance(3)

    exchange(2).wait_recv()
    scaled_grad = unfolded(own_grad + got[2, 0:HEAD_DIM, :]) * own_factor
    correction = over_points(scaled_grad * self_summary)
    g_keys = key_powers * (dot(scaled_grad.astype(BF16), self_values) - correction)
    g_values = dot(scaled_grad.T.astype(BF16), key_low)
    g_keyval = jnp.concatenate([g_keys.astype(BF16), g_values.astype(BF16)], axis=0)
    upstream = query_part + dot(qkv_w[:, D:], g_keyval)
    keyval_sum = dot_points(hidden_two, g_keyval)
    for half in range(2):
        middle.source[half * D : (half + 1) * D, :] = keyval_sum[:, half * D : (half + 1) * D].astype(BF16)
    middle.begin()
    g_after_cross = g_after_self + norm_back(normed_two, inverse_two, gain_two, upstream)
    g_proj = g_after_cross.astype(BF16)
    g_cross_out = dot(cross_w, g_proj).astype(BF16)
    own_mixed = folded(dot_points(cross_low, g_cross_out))
    sent[3, 0:HEAD_DIM, :] = own_mixed
    exchange(3).start()
    advance(0)
    last.source[D : 2 * D, :] = dot_points(cross_out, g_proj).astype(BF16)
    small[2] = to_row(over_points(upstream * normed_two))
    small[3] = to_row(over_points(upstream))
    g_query = feature_softmax_back(cross_soft, dot(mixed_low, g_cross_out)).astype(BF16)
    advance(4)
    upstream_one = dot(query_w, g_query)
    last.source[0:D, :] = dot_points(hidden_one, g_query).astype(BF16)
    small[0] = to_row(over_points(upstream_one * normed_one))
    small[1] = to_row(over_points(upstream_one))
    last.source[2 * D :, :] = jnp.concatenate(
        [router_sum, *small, jnp.zeros((2, D), F32)], axis=0
    ).astype(BF16)
    last.begin()
    advance(1)

    exchange(3).wait_recv()
    fn_grad = unfolded((own_mixed + got[3, 0:HEAD_DIM, :]) * fn_share)
    fn_scaled = fn_grad * fn_scale
    fn_correction = over_points(fn_scaled * fn_summary)
    g_keys = fn_powers[...] * (dot(fn_scaled.astype(BF16), fn_values[...]) - fn_correction)
    g_values = dot(fn_scaled.T.astype(BF16), fn_low[...])
    g_keyval = jnp.concatenate([g_keys, g_values], axis=0).astype(BF16)
    normed_sum = dot_points(fn_normed[...], g_keyval)
    plain_sum = dot_points(jnp.ones((8, fn_rows), BF16), g_keyval)[0:1]
    kv_sum = branch_gain * normed_sum + branch_bias * plain_sum
    for half in range(2):
        branch.source[half * D : (half + 1) * D, :] = kv_sum[:, half * D : (half + 1) * D].astype(BF16)
    kv_wide = kv.astype(F32)
    branch.source[2 * D :, :] = jnp.concatenate(
        [to_row(over_points(kv_wide * normed_sum)), to_row(over_points(kv_wide * plain_sum)), jnp.zeros((30, D), F32)],
        axis=0,
    ).astype(BF16)
    branch.begin()
    total = g_after_cross + norm_back(normed_one, inverse_one, gain_one, upstream_one)
    input_grad[...] = total.T.astype(BF16)
    result = after_self
    for number in range(EXPERTS):
        part = slice(number * FF, (number + 1) * FF)
        result = result + half_gates[number : number + 1] * dot(down_t[:, part], hidden_v[part, :])
    output[...] = result.T.astype(BF16)
    advance(2, 3, 0, 1, 4)
    last.advance()
    branch.advance()
    advance(0, 1, 2, 3)

    for load in loads[6:]:
        load.wait()
    waiting = [*experts, middle, last, branch]

    def finish(reduction):
        while reduction.steps_left:
            for other in waiting:
                if other is reduction or len(other.steps_left) > 1:
                    other.advance()

    def renew(start, count):
        part = slice(start, start + count)
        new = sgd_update(*(ref[part, :] for ref in shared_new[:3]), shared_sum[part, :], shared_rate)
        for value, target in zip(new, shared_new):
            target[part, :] = value

    for number, sums in enumerate(experts):
        finish(sums)
        for half in range(2):
            shared_sum[pl.ds(ROW_UP + number * FF + half, D, stride=2), :] = sums.total[
                half * D : (half + 1) * D, :
            ].astype(F32)
        start = ROW_DOWN + number * FF
        shared_sum[start : start + FF, :] = sums.total[FF:, :].astype(F32)
    whole = -(-ROW_UP // 16) * 16
    renew(whole, SHARED_ROWS - whole)
    finish(middle)
    shared_sum[ROW_SELF_OUT : ROW_SELF_OUT + D, :] = middle.total[2 * D : 3 * D, :].astype(F32)
    for third, held in enumerate([middle.total[3 * D :, :], middle.total[:D, :], middle.total[D : 2 * D, :]]):
        shared_sum[pl.ds(ROW_QKV + third, D, stride=3), :] = held.astype(F32)
    finish(last)
    shared_sum[ROW_QUERY : ROW_QUERY + D, :] = last.total[0:D, :].astype(F32)
    shared_sum[ROW_CROSS_OUT : ROW_CROSS_OUT + D, :] = last.total[D : 2 * D, :].astype(F32)
    rest = last.total[2 * D :, :].astype(F32)
    for at, row in enumerate(
        [ROW_GAIN_ONE, ROW_BIAS_ONE, ROW_GAIN_TWO, ROW_BIAS_TWO, ROW_GAIN_THREE, ROW_BIAS_THREE]
    ):
        shared_sum[row : row + 1, :] = rest[8 + at : 9 + at]
    norms_out[...] = rest[8:14]
    router_low = rest[:8].astype(BF16)
    for r in range(EXPERTS):
        spread = dot_points(router_low, pickers[r])
        shared_sum[ROW_ROUTER + r : ROW_ROUTER + r + 1, :] = jnp.sum(
            jnp.where(router_mask, spread, 0.0), axis=0, keepdims=True
        )
    renew(0, whole)
    finish(branch)
    for half in range(2):
        branch_rows[pl.ds(2 + half, D, stride=2), :] = branch.total[
            half * D : (half + 1) * D, :
        ].astype(F32)
    branch_rows[0:2, :] = branch.total[2 * D :, :].astype(F32)[0:2]
    for r in range(BRANCH_ROWS):
        branch_sum[0:1, r * D : (r + 1) * D] = branch_rows[r : r + 1, :]
    new = sgd_update(*(ref[...] for ref in branch_new[:3]), branch_sum[...], branch_rate)
    for value, target in zip(new, branch_new):
        target[...] = value

    for at in range(4):
        exchange(at).wait_send()
    for reduction in reductions:
        reduction.drain()


def sgd_update(weights, momentum, average, gradient, step_rate):
    momentum_new = momentum_decay * momentum + gradient
    weights_new = weights - step_rate * (gradient + momentum_decay * momentum_new)
    average_new = average_decay * average + (1.0 - average_decay) * weights_new
    return (weights_new, momentum_new, average_new, weights_new.astype(BF16))


def low(*shape):
    return pltpu.VMEM(shape, BF16)


def wide(*shape):
    return pltpu.VMEM(shape, F32)


def whole_step(fns, pts, rates, counts, arrays, momenta):
    points, _, functions = arrays[:3]
    rows, fn_rows = points.shape[0], functions.shape[0]
    smem = pl.BlockSpec(memory_space=pltpu.SMEM)
    vmem = pl.BlockSpec(memory_space=pltpu.VMEM)
    anywhere = pl.BlockSpec(memory_space=pl.ANY)
    branch = (1, BRANCH_ROWS * D)

    outs = [low(rows, D), low(rows, D)]
    outs += [wide(SHARED_ROWS, D)] * 3 + [low(SHARED_ROWS, D)] + [wide(*branch)] * 3 + [low(*branch)] + [wide(6, D)]
    scratch = [low(rows, D), low(rows, D), low(fn_rows, D), low(rows, D)]
    scratch += [wide(BRANCH_ROWS, D), wide(SHARED_ROWS, D), wide(*branch)]
    scratch += [wide(D, fn_rows), low(D, fn_rows), low(D, fn_rows), low(D, fn_rows), low(HIDDEN, rows), low(HIDDEN, rows)]
    scratch += [wide(HIDDEN, rows), low(EXPERTS * D, rows), low(HIDDEN, D), low(D, HIDDEN)]
    scratch += [wide(4, HEAD_DIM + 8, D), wide(4, HEAD_DIM + 8, D)]
    scratch += [pltpu.SemaphoreType.DMA((10,)), pltpu.SemaphoreType.DMA((4,)), pltpu.SemaphoreType.DMA((4,))]
    for reduction in plan(fns, pts):
        scratch += reduction.scratch()
    return pl.pallas_call(
        functools.partial(step_kernel, fns, pts, *rates),
        out_shape=outs,
        in_specs=[smem] * 3 + [anywhere] * (len(arrays) + len(momenta)),
        out_specs=[vmem] * len(outs),
        scratch_shapes=scratch,
        compiler_params=pltpu.CompilerParams(
            collective_id=0, has_side_effects=True, vmem_limit_bytes=VMEM_LIMIT << 20
        ),
    )(*counts, *(pltpu.with_memory_space_constraint(value, pltpu.HBM) for value in (*arrays, *momenta)))


def store_kernel(count, *refs):
    copies = [
        pltpu.make_async_copy(source, target, refs[-1].at[at])
        for at, (source, target) in enumerate(zip(refs[:count], refs[count:]))
    ]
    for copy in copies:
        copy.start()
    for copy in copies:
        copy.wait()


def stored(values):
    count = len(values)
    return pl.pallas_call(
        functools.partial(store_kernel, count),
        out_shape=[jax.ShapeDtypeStruct(value.shape, value.dtype) for value in values],
        in_specs=[pl.BlockSpec(memory_space=pltpu.VMEM)] * count,
        out_specs=[pl.BlockSpec(memory_space=pl.ANY)] * count,
        scratch_shapes=[pltpu.SemaphoreType.DMA((count,))],
        compiler_params=pltpu.CompilerParams(vmem_limit_bytes=4 << 20),
    )(*values)


def local(
    fns,
    pts,
    points_in,
    geometry,
    functions,
    presence,
    fn_counts,
    item_counts,
    cotangent,
    shared_weights,
    shared_momentum,
    shared_average,
    branch_weights,
    branch_momentum,
    branch_average,
):
    rows, fn_rows = points_in.shape[1], functions.shape[2]
    rates = (0.1 / math.sqrt(pts * rows * fns), 0.1 / math.sqrt(pts * fn_rows))
    arrays = [
        points_in.reshape(rows, D),
        geometry.reshape(rows, D),
        functions.reshape(fn_rows, D),
        cotangent.reshape(rows, D),
        shared_weights.reshape(SHARED_ROWS, D),
        branch_weights,
    ]
    momenta = [value.reshape(SHARED_ROWS, D) for value in (shared_momentum, shared_average)]
    momenta += [branch_momentum, branch_average]
    new = stored(whole_step(fns, pts, rates, (presence, fn_counts, item_counts), arrays, momenta))
    return (
        new[0].reshape(1, rows, D),
        new[1].reshape(1, rows, D),
        *(value.reshape(-1) for value in new[2:6]),
        *new[6:],
    )


def solution(mesh):
    split = P("pts", "fn", None)
    return jax.shard_map(
        functools.partial(local, mesh.shape["fn"], mesh.shape["pts"]),
        mesh=mesh,
        in_specs=(
            split,
            split,
            P("fn", "pts", None, None),
            P("fn", "pts"),
            P("fn", "pts"),
            P("pts"),
            split,
            P(),
            P(),
            P(),
            P("fn", None),
            P("fn", None),
            P("fn", None),
        ),
        out_specs=(
            split,
            split,
            P(),
            P(),
            P(),
            P(),
            P("fn", None),
            P("fn", None),
            P("fn", None),
            P("fn", None),
            P(),
        ),
        check_vma=False,
    )
```

```python
import functools
import math

import jax
import jax.numpy as jnp
from jax import lax
from jax.experimental import pallas as pl
from jax.experimental.pallas import tpu as pltpu
from jax.sharding import PartitionSpec as P

D = 128
HEADS = 8
FF = 256
EXPERTS = 4
HEAD_DIM = 16
HIDDEN = EXPERTS * FF

epsilon = 1e-05
far_below = -1e30
momentum_decay = 0.9
average_decay = 0.95

F32 = jnp.float32
BF16 = jnp.bfloat16
MESH = pl.DeviceIdType.MESH

ROW_GAIN_ONE, ROW_BIAS_ONE = 0, 1
ROW_QUERY = 2
ROW_CROSS_OUT = ROW_QUERY + D
ROW_GAIN_TWO = ROW_CROSS_OUT + D
ROW_BIAS_TWO = ROW_GAIN_TWO + 1
ROW_QKV = ROW_BIAS_TWO + 1
ROW_SELF_OUT = ROW_QKV + 3 * D
ROW_GAIN_THREE = ROW_SELF_OUT + D
ROW_BIAS_THREE = ROW_GAIN_THREE + 1
ROW_ROUTER = ROW_BIAS_THREE + 1
ROW_UP = ROW_ROUTER + EXPERTS
ROW_DOWN = ROW_UP + 2 * D * EXPERTS
SHARED_ROWS = ROW_DOWN + HIDDEN
BRANCH_ROWS = 2 + 2 * D

EXPERT_ROWS = 2 * FF
MIDDLE_ROWS = 4 * D
LAST_ROWS = 2 * D + 16
BRANCH_SENT = 2 * D + 32

VMEM_LIMIT = 52


def dot(a, b):
    return jnp.dot(a, b, preferred_element_type=F32)


def dot_points(a, b):
    return lax.dot_general(a, b, (((1,), (1,)), ((), ())), preferred_element_type=F32)


class Level:
    def __init__(self, grid, member):
        sizes = [size for size, _ in grid]
        self.size = math.prod(sizes)
        shifted = [
            [at if by == 0 else lax.rem(at + by, size) for by in range(size)] if size > 1 else [0]
            for size, at in grid
        ]
        self.peers = []
        for k in range(self.size):
            place, index, left = [], 0, k
            for size, moved in zip(reversed(sizes), reversed(shifted)):
                place.append(moved[left % size])
                left //= size
            place.reverse()
            for size, at in zip(sizes, place):
                index = index * size + at
            self.peers.append((index, member(*place)))
        self.index = self.peers[0][0]


TILE = 16


def split_rows(rows, size):
    step = TILE
    while rows % step or rows // step > size:
        step += TILE
    return step, rows // step


class Reduction:
    def __init__(self, sizes, rows):
        self.sizes, self.rows = sizes, rows
        self.steps, self.owners = [], []
        for size in sizes:
            step, owners = split_rows(rows, size)
            self.steps.append(step)
            self.owners.append(owners)
            rows = step

    def scratch(self):
        shapes = [pltpu.VMEM((self.rows, D), BF16), pltpu.VMEM((self.rows, D), BF16)]
        for at, size in enumerate(self.sizes):
            shapes.append(pltpu.VMEM(((size - 1) * self.steps[at], D), BF16))
            shapes.append(pltpu.VMEM((self.steps[at], D), BF16))
            shapes.append(pltpu.SemaphoreType.DMA((4,)))
        return shapes

    def bind(self, refs, levels):
        self.source, self.total = refs[0], refs[1]
        self.parts = [refs[2 + 3 * at : 5 + 3 * at] for at in range(len(self.sizes))]
        self.levels = levels
        last = len(self.sizes) - 1
        self.steps_left = []
        for at in range(last):
            self.steps_left.append(lambda at=at: (self.add(at), self.scatter(at + 1)))
        self.steps_left.append(lambda: (self.add(last), self.gather(last)))
        for at in range(last, 0, -1):
            self.steps_left.append(lambda at=at: (self.collect(at), self.gather(at - 1)))
        self.steps_left.append(lambda: self.collect(0))

    def begin(self):
        self.scatter(0)

    def advance(self):
        if self.steps_left:
            self.steps_left.pop(0)()

    def base(self, at):
        start = 0
        for upper in range(at):
            start = start + self.levels[upper].index * self.steps[upper]
        return start

    def inside(self, at):
        condition = None
        for upper in range(at):
            if self.owners[upper] < self.sizes[upper]:
                here = self.levels[upper].index < self.owners[upper]
                condition = here if condition is None else jnp.logical_and(condition, here)
        return condition

    def when(self, condition, body):
        if condition is None:
            body()
        else:
            pl.when(condition)(body)

    def split(self, at, owner, other):
        def go():
            if self.owners[at] == self.sizes[at]:
                owner()
            else:
                here = self.levels[at].index < self.owners[at]
                pl.when(here)(owner)
                if other is not None:
                    pl.when(jnp.logical_not(here))(other)

        self.when(self.inside(at), go)

    def rows_from(self, at):
        return self.source if at == 0 else self.parts[at - 1][1]

    def wait(self, at, sem, rows, sending):
        window = self.source if rows <= self.rows else self.parts[at][0]
        copy = pltpu.make_async_remote_copy(
            src_ref=window.at[pl.ds(0, rows), :],
            dst_ref=window.at[pl.ds(0, rows), :],
            send_sem=self.parts[at][2].at[sem],
            recv_sem=self.parts[at][2].at[sem],
            device_id=self.levels[at].peers[0][1],
            device_id_type=MESH,
        )
        (copy.wait_send if sending else copy.wait_recv)()

    def scatter(self, at):
        level, step, owners = self.levels[at], self.steps[at], self.owners[at]
        received, _, sems = self.parts[at]

        def go():
            for k in range(1, level.size):
                peer, device = level.peers[k]

                def start():
                    pltpu.make_async_remote_copy(
                        src_ref=self.rows_from(at).at[pl.ds(pl.multiple_of(peer * step, TILE), step), :],
                        dst_ref=received.at[pl.ds((k - 1) * step, step), :],
                        send_sem=sems.at[0],
                        recv_sem=sems.at[1],
                        device_id=device,
                        device_id_type=MESH,
                    ).start()

                self.when(None if owners == level.size else peer < owners, start)

        self.when(self.inside(at), go)

    def add(self, at):
        level, step = self.levels[at], self.steps[at]

        def go():
            received, kept, _ = self.parts[at]
            self.wait(at, 1, (level.size - 1) * step, False)
            start = pl.multiple_of(level.index * step, TILE)
            total = self.rows_from(at)[pl.ds(start, step), :].astype(F32)
            for k in range(level.size - 1):
                total = total + received[k * step : (k + 1) * step, :].astype(F32)
            if at + 1 < len(self.sizes):
                kept[...] = total.astype(BF16)
            else:
                self.total[pl.ds(pl.multiple_of(self.base(at) + start, TILE), step), :] = total.astype(BF16)

        self.split(at, go, None)

    def gather(self, at):
        level, step = self.levels[at], self.steps[at]
        sems = self.parts[at][2]

        def go():
            rows = pl.ds(pl.multiple_of(self.base(at) + level.index * step, TILE), step)

            for _, device in level.peers[1:]:
                pltpu.make_async_remote_copy(
                    src_ref=self.total.at[rows, :],
                    dst_ref=self.total.at[rows, :],
                    send_sem=sems.at[2],
                    recv_sem=sems.at[3],
                    device_id=device,
                    device_id_type=MESH,
                ).start()

        self.split(at, go, None)

    def collect(self, at):
        step, owners = self.steps[at], self.owners[at]
        self.split(
            at,
            lambda: self.wait(at, 3, (owners - 1) * step, False) if owners > 1 else None,
            lambda: self.wait(at, 3, owners * step, False),
        )

    def drain(self):
        for at, size in enumerate(self.sizes):
            step, owners = self.steps[at], self.owners[at]

            def owner():
                if owners > 1:
                    self.wait(at, 0, (owners - 1) * step, True)
                self.wait(at, 2, (size - 1) * step, True)

            self.split(at, owner, lambda: self.wait(at, 0, owners * step, True))


def inner_size(pts):
    return 2 if pts % 2 == 0 else 1


def middle_size(pts):
    outer = pts // inner_size(pts)
    return 2 if outer % 2 == 0 else 1


def plan(fns, pts):
    core, middle = inner_size(pts), middle_size(pts)
    far = pts // (core * middle)
    stepwise = [core, fns * middle, far]
    small = fns * pts <= 32
    halved = [core, fns * middle * far] if small else stepwise
    at_once = [fns * pts] if small else stepwise
    items = [pts] if small else [core * middle, far]
    return [
        Reduction(stepwise, EXPERT_ROWS),
        Reduction(stepwise, EXPERT_ROWS),
        Reduction(halved, EXPERT_ROWS),
        Reduction(halved, EXPERT_ROWS),
        Reduction(halved, MIDDLE_ROWS),
        Reduction(at_once, LAST_ROWS),
        Reduction(items, BRANCH_SENT),
    ]


def layer_norm(values):
    centred = values - jnp.mean(values, axis=0, keepdims=True)
    spread = jnp.mean(centred * centred, axis=0, keepdims=True)
    inverse = lax.rsqrt(spread + epsilon)
    return centred * inverse, inverse


def norm_back(normed, inverse, gain, upstream):
    scaled = upstream * gain
    first = jnp.mean(scaled, axis=0, keepdims=True)
    second = jnp.mean(scaled * normed, axis=0, keepdims=True)
    return (scaled - first - normed * second) * inverse


def heads_view(values):
    return values.reshape(HEADS, HEAD_DIM, values.shape[-1])


def feature_softmax(values):
    shaped = heads_view(values)
    powers = jnp.exp(shaped - jnp.max(shaped, axis=1, keepdims=True))
    return (powers * (1.0 / jnp.sum(powers, axis=1, keepdims=True))).reshape(values.shape)


def feature_softmax_back(soft, upstream):
    shaped, incoming = heads_view(soft), heads_view(upstream)
    inner = jnp.sum(shaped * incoming, axis=1, keepdims=True)
    return (shaped * (incoming - inner)).reshape(soft.shape)


def over_points(values):
    return jnp.sum(values, axis=1, keepdims=True)


def step_kernel(fns, pts, shared_rate, branch_rate, *refs):
    refs = list(refs)

    def take(n):
        got = refs[:n]
        del refs[:n]
        return got

    presence, fn_counts, item_counts = take(3)
    points_hbm, geometry_hbm, functions_hbm, cotangent_hbm, shared_hbm, branch_hbm = take(6)
    momenta_hbm = take(4)
    output, input_grad = take(2)
    shared_new, branch_new, norms_out = take(4), take(4), take(1)[0]
    shared_v, branch_v = shared_new[0], branch_new[0]
    points_v, geometry_v, functions_v, cotangent_v, branch_rows, shared_sum, branch_sum = take(7)
    fn_powers, fn_low, fn_values, fn_normed, hidden_v, pre_v, back_v, g_expert_v, up_t, down_t = take(10)
    sent, got = take(2)
    local_sem, x_send, x_recv = take(3)
    reductions = plan(fns, pts)
    bound = [take(len(reduction.scratch())) for reduction in reductions]
    assert not refs

    fn, pt = lax.axis_index("fn"), lax.axis_index("pts")
    core_size, mid_size = inner_size(pts), middle_size(pts)
    near_size = core_size * mid_size
    far, near = lax.div(pt, near_size), lax.rem(pt, near_size)
    mid, core = lax.div(near, core_size), lax.rem(near, core_size)

    def item(far_at, mid_at, core_at):
        return far_at * near_size + mid_at * core_size + core_at

    fn_axis, far_axis, mid_axis, core_axis = (fns, fn), (pts // near_size, far), (mid_size, mid), (core_size, core)
    far_level = Level([far_axis], lambda z: (fn, item(z, mid, core)))
    stepwise = [
        Level([core_axis], lambda c: (fn, item(far, mid, c))),
        Level([fn_axis, mid_axis], lambda f, m: (f, item(far, m, core))),
        far_level,
    ]
    if fns * pts <= 32:
        halved = [stepwise[0], Level([fn_axis, far_axis, mid_axis], lambda f, z, m: (f, item(z, m, core)))]
        at_once = [Level([fn_axis, far_axis, mid_axis, core_axis], lambda f, z, m, c: (f, item(z, m, c)))]
        items = [Level([far_axis, mid_axis, core_axis], lambda z, m, c: (fn, item(z, m, c)))]
        greeted = at_once
    else:
        halved = at_once = stepwise
        items = [Level([mid_axis, core_axis], lambda m, c: (fn, item(far, m, c))), far_level]
        greeted = [Level([fn_axis, mid_axis, core_axis], lambda f, m, c: (f, item(far, m, c))), far_level]
    ways = [stepwise, stepwise, halved, halved, halved, at_once, items]
    for reduction, scratch, levels in zip(reductions, bound, ways):
        reduction.bind(scratch, levels)
    experts = reductions[:EXPERTS]
    middle, last, branch = reductions[EXPERTS:]

    rows, fn_rows = points_v.shape[0], functions_v.shape[0]

    loads = []
    for at, (source, target) in enumerate(
        [
            (branch_hbm, branch_v),
            (functions_hbm, functions_v),
            (shared_hbm, shared_v),
            (points_hbm, points_v),
            (geometry_hbm, geometry_v),
            (cotangent_hbm, cotangent_v),
            *zip(momenta_hbm, [*shared_new[1:3], *branch_new[1:3]]),
        ]
    ):
        loads.append(pltpu.make_async_copy(source, target, local_sem.at[at]))
        loads[-1].start()

    barrier = pltpu.get_barrier_semaphore()
    for level in greeted:
        for _, device in level.peers[1:]:
            pl.semaphore_signal(barrier, inc=1, device_id=device, device_id_type=MESH)

    def exchange(at):
        return pltpu.make_async_remote_copy(
            src_ref=sent.at[at],
            dst_ref=got.at[at],
            send_sem=x_send.at[at],
            recv_sem=x_recv.at[at],
            device_id=(lax.rem(fn + 1, fns), pt),
            device_id_type=MESH,
        )

    row_at = lax.broadcasted_iota(jnp.int32, (D, D), 0)
    column_at = lax.broadcasted_iota(jnp.int32, (D, D), 1)
    same_head = row_at // HEAD_DIM == column_at // HEAD_DIM
    diagonal = row_at == column_at

    def diagonal_blocks(full):
        return jnp.where(same_head, full, 0.0)

    def folded(full):
        kept = diagonal_blocks(full)
        out = kept[:HEAD_DIM]
        for head in range(1, HEADS):
            out = out + kept[head * HEAD_DIM : (head + 1) * HEAD_DIM]
        return out

    def unfolded(compact):
        return diagonal_blocks(jnp.concatenate([compact] * HEADS, axis=0))

    def to_row(column):
        return jnp.sum(jnp.where(diagonal, column, 0.0), axis=0, keepdims=True)

    def to_column(row):
        return jnp.sum(jnp.where(diagonal, row, 0.0), axis=1, keepdims=True)

    loads[0].wait()
    for r in range(BRANCH_ROWS):
        branch_rows[r : r + 1, :] = branch_v[0:1, r * D : (r + 1) * D]
    kv = jnp.concatenate(
        [branch_rows[pl.ds(2, D, stride=2), :], branch_rows[pl.ds(3, D, stride=2), :]], axis=1
    ).astype(BF16)
    branch_gain = to_column(branch_rows[0:1, :])
    branch_bias = to_column(branch_rows[1:2, :])
    fn_count = fn_counts[0, 0]
    fn_weight = (presence[0, 0] * fn_count).astype(F32)
    fn_usable = lax.broadcasted_iota(jnp.int32, (1, fn_rows), 1) < fn_count
    loads[1].wait()
    normed, _ = layer_norm(functions_v[...].astype(F32).T)
    hidden = (normed * branch_gain + branch_bias).astype(BF16)
    fn_normed[...] = normed.astype(BF16)
    keyval = dot(kv.T, hidden)
    keys = jnp.where(fn_usable, keyval[:D], far_below)
    fn_values[...] = keyval[D:].astype(BF16)
    fn_max = jnp.max(keys, axis=1, keepdims=True)
    powers = jnp.where(fn_usable, jnp.exp(keys - fn_max), 0.0)
    fn_powers[...] = powers
    fn_low[...] = powers.astype(BF16)
    fn_scale = 1.0 / over_points(powers)
    fn_summary = diagonal_blocks(dot_points(fn_low[...], fn_values[...]) * fn_scale)
    weighted_summary = fn_weight * folded(fn_summary)
    sent[0, 0:HEAD_DIM, :] = weighted_summary
    sent[0, HEAD_DIM : HEAD_DIM + 8, :] = jnp.full((8, D), fn_weight, F32)
    pl.semaphore_wait(barrier, sum(level.size - 1 for level in greeted))
    exchange(0).start()

    loads[2].wait()

    def shared_rows(start, stride=1):
        return shared_v[pl.ds(start, D, stride=stride), :].astype(BF16)

    query_w = shared_rows(ROW_QUERY)
    cross_w = shared_rows(ROW_CROSS_OUT)
    self_w = shared_rows(ROW_SELF_OUT)
    qkv_w = jnp.concatenate([shared_rows(ROW_QKV + third, 3) for third in range(3)], axis=1)

    for piece_at in range(2 * EXPERTS):
        number, half = piece_at // 2, piece_at % 2
        up_t[piece_at * D : (piece_at + 1) * D, :] = shared_rows(ROW_UP + number * FF + half, 2).T
        down_t[:, piece_at * D : (piece_at + 1) * D] = shared_rows(ROW_DOWN + piece_at * D).T

    expert_at = lax.broadcasted_iota(jnp.int32, (8, D), 0)
    router_mask = lax.broadcasted_iota(jnp.int32, (8, D), 1) % EXPERTS == expert_at
    router_t = jnp.zeros((8, D), F32)
    pickers = []
    for r in range(EXPERTS):
        picker = jnp.where(column_at == r * (D // EXPERTS) + row_at // EXPERTS, 1.0, 0.0).astype(BF16)
        pickers.append(picker)
        router_row = shared_v[ROW_ROUTER + r : ROW_ROUTER + r + 1, :]
        router_t = router_t + dot(jnp.where(router_mask, router_row, 0.0).astype(BF16), picker)
    router_t = router_t.astype(BF16)

    def shared_column(row):
        return to_column(shared_v[row : row + 1, :])

    gain_one, bias_one = shared_column(ROW_GAIN_ONE), shared_column(ROW_BIAS_ONE)
    gain_two, bias_two = shared_column(ROW_GAIN_TWO), shared_column(ROW_BIAS_TWO)
    gain_three, bias_three = shared_column(ROW_GAIN_THREE), shared_column(ROW_BIAS_THREE)

    loads[3].wait()
    points = points_v[...].astype(F32).T
    normed_one, inverse_one = layer_norm(points)
    hidden_one = (normed_one * gain_one + bias_one).astype(BF16)
    cross_soft = feature_softmax(dot(query_w.T, hidden_one))
    cross_low = cross_soft.astype(BF16)

    exchange(0).wait_recv()
    weight_total = fn_weight + got[0, HEAD_DIM : HEAD_DIM + 1, :]
    fn_share = fn_weight / weight_total
    mixed = unfolded((weighted_summary + got[0, 0:HEAD_DIM, :]) / weight_total)
    mixed_low = mixed.astype(BF16)
    cross_out = dot(mixed.T.astype(BF16), cross_low).astype(BF16)
    after_cross = points + dot(cross_w.T, cross_out)
    normed_two, inverse_two = layer_norm(after_cross)
    hidden_two = (normed_two * gain_two + bias_two).astype(BF16)
    qkv = dot(qkv_w[:, D:].T, hidden_two)
    usable = lax.broadcasted_iota(jnp.int32, (1, rows), 1) + fn * rows < item_counts[0]
    keys = jnp.where(usable, qkv[:D], far_below)
    self_values = qkv[D:].astype(BF16)
    key_max = jnp.max(keys, axis=1, keepdims=True)
    key_powers = jnp.where(usable, jnp.exp(keys - key_max), 0.0)
    key_low = key_powers.astype(BF16)
    own_total = over_points(key_powers)
    key_sum = dot_points(key_low, self_values)
    sent[1, 0:HEAD_DIM, :] = folded(key_sum)
    sent[1, HEAD_DIM : HEAD_DIM + 8, :] = jnp.concatenate(
        [to_row(key_max), to_row(own_total), jnp.zeros((6, D), F32)], axis=0
    )
    exchange(1).start()

    self_soft = feature_softmax(dot(qkv_w[:, :D].T, hidden_two))
    self_weights = self_soft.astype(BF16)
    loads[4].wait()
    logits = dot_points(router_t, geometry_v[...])[:EXPERTS]
    powers = jnp.exp(logits - jnp.max(logits, axis=0, keepdims=True))
    gates = powers * (1.0 / jnp.sum(powers, axis=0, keepdims=True))
    half_gates = 0.5 * gates
    loads[5].wait()
    arriving = cotangent_v[...].astype(F32).T
    for number in range(EXPERTS):
        g_expert = (half_gates[number : number + 1] * arriving).astype(BF16)
        g_expert_v[number * D : (number + 1) * D, :] = g_expert
        down = shared_v[ROW_DOWN + number * FF : ROW_DOWN + (number + 1) * FF, :].astype(BF16)
        back_v[number * FF : (number + 1) * FF, :] = dot(down, g_expert)

    exchange(1).wait_recv()
    other_max = to_column(got[1, HEAD_DIM : HEAD_DIM + 1, :])
    other_total = to_column(got[1, HEAD_DIM + 1 : HEAD_DIM + 2, :])
    joint_max = jnp.maximum(key_max, other_max)
    own_factor, other_factor = jnp.exp(key_max - joint_max), jnp.exp(other_max - joint_max)
    joint_scale = 1.0 / (own_total * own_factor + other_total * other_factor)
    own_factor, other_factor = own_factor * joint_scale, other_factor * joint_scale
    self_summary = diagonal_blocks(key_sum) * own_factor + unfolded(got[1, 0:HEAD_DIM, :]) * other_factor
    self_low = self_summary.astype(BF16)

    self_out = dot(self_summary.T.astype(BF16), self_weights).astype(BF16)
    after_self = after_cross + dot(self_w.T, self_out)
    normed_three, inverse_three = layer_norm(after_self)
    hidden_three = (normed_three * gain_three + bias_three).astype(BF16)

    def expert_sums(number):
        part = slice(number * FF, (number + 1) * FF)
        source = experts[number].source
        up_sum = dot_points(hidden_three, pre_v[part, :])
        source[0:D, :] = up_sum[:, :D].astype(BF16)
        source[D : 2 * D, :] = up_sum[:, D:].astype(BF16)
        source[FF:, :] = dot_points(hidden_v[part, :], g_expert_v[number * D : (number + 1) * D, :]).astype(BF16)
        experts[number].begin()

    def advance(*numbers):
        for number in numbers:
            reductions[number].advance()

    upstream, gated_grads = None, []
    for number in range(EXPERTS):
        part = slice(number * FF, (number + 1) * FF)
        argument = dot(up_t[part, :], hidden_three)
        back = back_v[part, :]
        twice_cdf = 1.0 + lax.erf(argument * math.sqrt(0.5))
        bell = jnp.exp2(argument * argument * (-0.5 * math.log2(math.e)) + 0.5 * math.log2(2.0 / math.pi))
        active = argument * twice_cdf
        gated_grads.append(jnp.sum(active * back, axis=0, keepdims=True))
        hidden_v[part, :] = active.astype(BF16)
        pre_v[part, :] = (back * (twice_cdf + argument * bell)).astype(BF16)
        up = jnp.concatenate([shared_rows(ROW_UP + number * FF + half, 2) for half in range(2)], axis=1)
        more = dot(up, pre_v[part, :])
        upstream = more if upstream is None else upstream + more
        if 0 < number < 3:
            expert_sums(number - 1)
        if number == 2:
            advance(0)
        if number == 3:
            advance(1)

    gated_grads = jnp.concatenate(gated_grads, axis=0)
    g_logits = gated_grads - gates * jnp.sum(gated_grads, axis=0, keepdims=True)
    g_logits = jnp.concatenate([g_logits, jnp.zeros_like(g_logits)], axis=0).astype(BF16)
    g_after_self = arriving + norm_back(normed_three, inverse_three, gain_three, upstream)
    g_proj = g_after_self.astype(BF16)
    g_self_out = dot(self_w, g_proj).astype(BF16)
    own_grad = folded(dot_points(self_weights, g_self_out))
    sent[2, 0:HEAD_DIM, :] = own_grad
    exchange(2).start()
    expert_sums(2)
    advance(0)
    expert_sums(3)
    g_queries = feature_softmax_back(self_soft, dot(self_low, g_self_out)).astype(BF16)
    middle.source[2 * D : 3 * D, :] = dot_points(self_out, g_proj).astype(BF16)
    middle.source[3 * D :, :] = dot_points(hidden_two, g_queries).astype(BF16)
    advance(1, 2)
    upstream_three = upstream
    query_part = dot(qkv_w[:, :D], g_queries)
    advance(3)

    exchange(2).wait_recv()
    scaled_grad = unfolded(own_grad + got[2, 0:HEAD_DIM, :]) * own_factor
    correction = over_points(scaled_grad * self_summary)
    g_keys = key_powers * (dot(scaled_grad.astype(BF16), self_values) - correction)
    g_values = dot(scaled_grad.T.astype(BF16), key_low)
    g_keyval = jnp.concatenate([g_keys.astype(BF16), g_values.astype(BF16)], axis=0)
    upstream = query_part + dot(qkv_w[:, D:], g_keyval)
    keyval_sum = dot_points(hidden_two, g_keyval)
    for half in range(2):
        middle.source[half * D : (half + 1) * D, :] = keyval_sum[:, half * D : (half + 1) * D].astype(BF16)
    middle.begin()
    g_after_cross = g_after_self + norm_back(normed_two, inverse_two, gain_two, upstream)
    g_proj = g_after_cross.astype(BF16)
    g_cross_out = dot(cross_w, g_proj).astype(BF16)
    own_mixed = folded(dot_points(cross_low, g_cross_out))
    sent[3, 0:HEAD_DIM, :] = own_mixed
    exchange(3).start()
    advance(0)
    last.source[D : 2 * D, :] = dot_points(cross_out, g_proj).astype(BF16)
    router_sum = dot(g_logits, geometry_v[...])
    small = [None] * 6
    small[4] = to_row(over_points(upstream_three * normed_three))
    small[5] = to_row(over_points(upstream_three))
    small[2] = to_row(over_points(upstream * normed_two))
    small[3] = to_row(over_points(upstream))
    g_query = feature_softmax_back(cross_soft, dot(mixed_low, g_cross_out)).astype(BF16)
    advance(4)
    upstream_one = dot(query_w, g_query)
    last.source[0:D, :] = dot_points(hidden_one, g_query).astype(BF16)
    small[0] = to_row(over_points(upstream_one * normed_one))
    small[1] = to_row(over_points(upstream_one))
    last.source[2 * D :, :] = jnp.concatenate(
        [router_sum, *small, jnp.zeros((2, D), F32)], axis=0
    ).astype(BF16)
    last.begin()
    advance(1)

    exchange(3).wait_recv()
    fn_grad = unfolded((own_mixed + got[3, 0:HEAD_DIM, :]) * fn_share)
    fn_scaled = fn_grad * fn_scale
    fn_correction = over_points(fn_scaled * fn_summary)
    g_keys = fn_powers[...] * (dot(fn_scaled.astype(BF16), fn_values[...]) - fn_correction)
    g_values = dot(fn_scaled.T.astype(BF16), fn_low[...])
    g_keyval = jnp.concatenate([g_keys, g_values], axis=0).astype(BF16)
    normed_sum = dot_points(fn_normed[...], g_keyval)
    plain_sum = dot_points(jnp.ones((8, fn_rows), BF16), g_keyval)[0:1]
    kv_sum = branch_gain * normed_sum + branch_bias * plain_sum
    for half in range(2):
        branch.source[half * D : (half + 1) * D, :] = kv_sum[:, half * D : (half + 1) * D].astype(BF16)
    kv_wide = kv.astype(F32)
    branch.source[2 * D :, :] = jnp.concatenate(
        [to_row(over_points(kv_wide * normed_sum)), to_row(over_points(kv_wide * plain_sum)), jnp.zeros((30, D), F32)],
        axis=0,
    ).astype(BF16)
    branch.begin()
    total = g_after_cross + norm_back(normed_one, inverse_one, gain_one, upstream_one)
    input_grad[...] = total.T.astype(BF16)
    result = after_self
    for number in range(EXPERTS):
        part = slice(number * FF, (number + 1) * FF)
        result = result + half_gates[number : number + 1] * dot(down_t[:, part], hidden_v[part, :])
    output[...] = result.T.astype(BF16)
    advance(2, 3, 0, 1, 4)
    last.advance()
    branch.advance()
    advance(0, 1, 2, 3)

    for load in loads[6:]:
        load.wait()
    waiting = [*experts, middle, last, branch]

    def finish(reduction):
        while reduction.steps_left:
            for other in waiting:
                if other is reduction or len(other.steps_left) > 1:
                    other.advance()

    def renew(start, count):
        part = slice(start, start + count)
        new = sgd_update(*(ref[part, :] for ref in shared_new[:3]), shared_sum[part, :], shared_rate)
        for value, target in zip(new, shared_new):
            target[part, :] = value

    for number, sums in enumerate(experts):
        finish(sums)
        for half in range(2):
            shared_sum[pl.ds(ROW_UP + number * FF + half, D, stride=2), :] = sums.total[
                half * D : (half + 1) * D, :
            ].astype(F32)
        start = ROW_DOWN + number * FF
        shared_sum[start : start + FF, :] = sums.total[FF:, :].astype(F32)
    whole = -(-ROW_UP // 16) * 16
    renew(whole, SHARED_ROWS - whole)
    finish(middle)
    shared_sum[ROW_SELF_OUT : ROW_SELF_OUT + D, :] = middle.total[2 * D : 3 * D, :].astype(F32)
    for third, held in enumerate([middle.total[3 * D :, :], middle.total[:D, :], middle.total[D : 2 * D, :]]):
        shared_sum[pl.ds(ROW_QKV + third, D, stride=3), :] = held.astype(F32)
    finish(last)
    shared_sum[ROW_QUERY : ROW_QUERY + D, :] = last.total[0:D, :].astype(F32)
    shared_sum[ROW_CROSS_OUT : ROW_CROSS_OUT + D, :] = last.total[D : 2 * D, :].astype(F32)
    rest = last.total[2 * D :, :].astype(F32)
    for at, row in enumerate(
        [ROW_GAIN_ONE, ROW_BIAS_ONE, ROW_GAIN_TWO, ROW_BIAS_TWO, ROW_GAIN_THREE, ROW_BIAS_THREE]
    ):
        shared_sum[row : row + 1, :] = rest[8 + at : 9 + at]
    norms_out[...] = rest[8:14]
    router_low = rest[:8].astype(BF16)
    for r in range(EXPERTS):
        spread = dot_points(router_low, pickers[r])
        shared_sum[ROW_ROUTER + r : ROW_ROUTER + r + 1, :] = jnp.sum(
            jnp.where(router_mask, spread, 0.0), axis=0, keepdims=True
        )
    renew(0, whole)
    for at in range(4):
        exchange(at).wait_send()
    for reduction in [*experts, middle]:
        reduction.drain()
    finish(branch)
    branch_rows[0 : 2 * D, :] = branch.total[0 : 2 * D, :].astype(F32)
    branch_rows[2 * D :, :] = branch.total[2 * D :, :].astype(F32)[0:2]
    for r in range(2):
        branch_sum[0:1, r * D : (r + 1) * D] = branch_rows[2 * D + r : 2 * D + r + 1, :]
    for r in range(2 * D):
        branch_sum[0:1, (r + 2) * D : (r + 3) * D] = branch_rows[r % 2 * D + r // 2 : r % 2 * D + r // 2 + 1, :]
    new = sgd_update(*(ref[...] for ref in branch_new[:3]), branch_sum[...], branch_rate)
    for value, target in zip(new, branch_new):
        target[...] = value

    last.drain()
    branch.drain()


def sgd_update(weights, momentum, average, gradient, step_rate):
    momentum_new = momentum_decay * momentum + gradient
    weights_new = weights - step_rate * (gradient + momentum_decay * momentum_new)
    average_new = average_decay * average + (1.0 - average_decay) * weights_new
    return (weights_new, momentum_new, average_new, weights_new.astype(BF16))


def low(*shape):
    return pltpu.VMEM(shape, BF16)


def wide(*shape):
    return pltpu.VMEM(shape, F32)


def whole_step(fns, pts, rates, counts, arrays, momenta):
    points, _, functions = arrays[:3]
    rows, fn_rows = points.shape[0], functions.shape[0]
    smem = pl.BlockSpec(memory_space=pltpu.SMEM)
    vmem = pl.BlockSpec(memory_space=pltpu.VMEM)
    anywhere = pl.BlockSpec(memory_space=pl.ANY)
    branch = (1, BRANCH_ROWS * D)

    outs = [low(rows, D), low(rows, D)]
    outs += [wide(SHARED_ROWS, D)] * 3 + [low(SHARED_ROWS, D)] + [wide(*branch)] * 3 + [low(*branch)] + [wide(6, D)]
    scratch = [low(rows, D), low(rows, D), low(fn_rows, D), low(rows, D)]
    scratch += [wide(BRANCH_ROWS, D), wide(SHARED_ROWS, D), wide(*branch)]
    scratch += [wide(D, fn_rows), low(D, fn_rows), low(D, fn_rows), low(D, fn_rows), low(HIDDEN, rows), low(HIDDEN, rows)]
    scratch += [wide(HIDDEN, rows), low(EXPERTS * D, rows), low(HIDDEN, D), low(D, HIDDEN)]
    scratch += [wide(4, HEAD_DIM + 8, D), wide(4, HEAD_DIM + 8, D)]
    scratch += [pltpu.SemaphoreType.DMA((10,)), pltpu.SemaphoreType.DMA((4,)), pltpu.SemaphoreType.DMA((4,))]
    for reduction in plan(fns, pts):
        scratch += reduction.scratch()
    return pl.pallas_call(
        functools.partial(step_kernel, fns, pts, *rates),
        out_shape=outs,
        in_specs=[smem] * 3 + [anywhere] * (len(arrays) + len(momenta)),
        out_specs=[vmem] * len(outs),
        scratch_shapes=scratch,
        compiler_params=pltpu.CompilerParams(
            collective_id=0, has_side_effects=True, vmem_limit_bytes=VMEM_LIMIT << 20
        ),
    )(*counts, *(pltpu.with_memory_space_constraint(value, pltpu.HBM) for value in (*arrays, *momenta)))


def store_kernel(count, *refs):
    copies = [
        pltpu.make_async_copy(source, target, refs[-1].at[at])
        for at, (source, target) in enumerate(zip(refs[:count], refs[count:]))
    ]
    for copy in copies:
        copy.start()
    for copy in copies:
        copy.wait()


def stored(values):
    count = len(values)
    return pl.pallas_call(
        functools.partial(store_kernel, count),
        out_shape=[jax.ShapeDtypeStruct(value.shape, value.dtype) for value in values],
        in_specs=[pl.BlockSpec(memory_space=pltpu.VMEM)] * count,
        out_specs=[pl.BlockSpec(memory_space=pl.ANY)] * count,
        scratch_shapes=[pltpu.SemaphoreType.DMA((count,))],
        compiler_params=pltpu.CompilerParams(vmem_limit_bytes=4 << 20),
    )(*values)


def local(
    fns,
    pts,
    points_in,
    geometry,
    functions,
    presence,
    fn_counts,
    item_counts,
    cotangent,
    shared_weights,
    shared_momentum,
    shared_average,
    branch_weights,
    branch_momentum,
    branch_average,
):
    rows, fn_rows = points_in.shape[1], functions.shape[2]
    rates = (0.1 / math.sqrt(pts * rows * fns), 0.1 / math.sqrt(pts * fn_rows))
    arrays = [
        points_in.reshape(rows, D),
        geometry.reshape(rows, D),
        functions.reshape(fn_rows, D),
        cotangent.reshape(rows, D),
        shared_weights.reshape(SHARED_ROWS, D),
        branch_weights,
    ]
    momenta = [value.reshape(SHARED_ROWS, D) for value in (shared_momentum, shared_average)]
    momenta += [branch_momentum, branch_average]
    new = stored(whole_step(fns, pts, rates, (presence, fn_counts, item_counts), arrays, momenta))
    return (
        new[0].reshape(1, rows, D),
        new[1].reshape(1, rows, D),
        *(value.reshape(-1) for value in new[2:6]),
        *new[6:],
    )


def solution(mesh):
    split = P("pts", "fn", None)
    return jax.shard_map(
        functools.partial(local, mesh.shape["fn"], mesh.shape["pts"]),
        mesh=mesh,
        in_specs=(
            split,
            split,
            P("fn", "pts", None, None),
            P("fn", "pts"),
            P("fn", "pts"),
            P("pts"),
            split,
            P(),
            P(),
            P(),
            P("fn", None),
            P("fn", None),
            P("fn", None),
        ),
        out_specs=(
            split,
            split,
            P(),
            P(),
            P(),
            P(),
            P("fn", None),
            P("fn", None),
            P("fn", None),
            P("fn", None),
            P(),
        ),
        check_vma=False,
    )
```
